256 devices in a mesh: row: 16 (over x, z_hi), col: 16 (over y, z_lo, core).
Axes of the slice: x: 4, y: 4, z: 8 (z_hi: 4, z_lo: 2; z = z_hi * 2 + z_lo), core: 2. Of those that a mesh axis runs over, the one named last changes fastest.
Arguments:
- object_field: float32 [2, 4096, 4096], P(None, 'row', 'col'), may hold values from -6 to 6
- probe: float32 [2, 4, 128, 128], replicated, may hold values from -3 to 3
- amplitudes: float32 [16, 16, 3, 4, 128, 128], P('row', 'col'), may hold values from 0.3 to 3
- offsets: int32 [16, 16, 3, 4, 2], P('row', 'col'), may hold values from -64 to 192, as said below
Outputs:
- object_new: float32 [2, 4096, 4096], P(None, 'row', 'col')
- probe_step: float32 [2, 4, 128, 128], replicated
The draws below stay inside these ranges and needn't reach their ends.
Inputs may be any that keep to these rules, and one draw needn't show every extreme that they name: `offsets`: in every batch of every device the first position is at (-64, -64) and the second at (192, 192).
All inputs are finite; a program needn't handle non-finite values.
Results may differ from the reference program's by a relative error of at most 0.0001.
Values sent between devices are 32-bit elements; how exact they have to be, the bound alone decides.
A program may use at most 64 MiB of HBM per device.

```python
import math
import jax
import jax.numpy as jnp
from jax import lax

PATCH = 128
MODES = 4
TILE = 256
POS_DEV = 4
BATCHES = 3
GRID_ROWS = 16
GRID_COLS = 16
ROWS_ALL = 4096
COLS_ALL = 4096


def draw_offsets(key, part):
    half_patch = PATCH // 2
    values = jax.random.randint(key, (GRID_ROWS, GRID_COLS, BATCHES, POS_DEV, 2), -half_patch, TILE - half_patch + 1, dtype=jnp.int32)
    values = values.at[:, :, :, 0, :].set(-half_patch)
    values = values.at[:, :, :, 1, :].set(TILE - half_patch)
    return values


def level_of(rng, dims, split, least, high):
    def one(axis_at, parts):
        heights = jax.random.uniform(jax.random.fold_in(jax.random.fold_in(rng, 6), axis_at), (parts,), jnp.float32, least / len(split), high / len(split))
        return jnp.repeat(jnp.exp(heights), dims[axis_at] // parts).reshape((-1,) + (1,) * (len(dims) - axis_at - 1))

    level = one(*split[0])
    for cut in split[1:]:
        level = level * one(*cut)
    return level


def gaussian(key, extent, scale, most, cuts=(), kind=jnp.bfloat16):
    entries = jax.random.normal(key, extent, jnp.float32) * scale
    if len(cuts) > 0:
        entries = level_of(key, extent, cuts, -0.22, 0.18) * entries
    return jnp.clip(entries, min=-most, max=most).astype(kind)


def setup_inputs(seed: int = 0) -> dict:
    key_of = jax.random.split(jax.random.key(seed), 5)
    return {
        "object_field": gaussian(key_of[0], (2, ROWS_ALL, COLS_ALL), 1.0, 6.0, ((1, 16), (2, 16)), jnp.float32),
        "probe": gaussian(key_of[1], (2, MODES, PATCH, PATCH), 0.5, 3.0, (), jnp.float32),
        "amplitudes": jnp.clip(jnp.exp(math.log(3.0) - 2.3025851 * jax.random.uniform(key_of[2], (GRID_ROWS, GRID_COLS, BATCHES, POS_DEV, PATCH, PATCH), jnp.float32) ** level_of(key_of[2], (GRID_ROWS, GRID_COLS, BATCHES, POS_DEV, PATCH, PATCH), ((0, 16), (1, 16)), -0.2, 0.2)), 0.3, 3.0),
        "offsets": draw_offsets(jax.random.fold_in(key_of[4], 71), 0),
    }


AMP_FLOOR = 0.25
OBJECT_REG = 0.5
PROBE_REG = 1.0
PRECISE_DOT = lax.Precision.HIGHEST

def dft_tables(length):
    indices = jnp.arange(length, dtype=jnp.int32)
    product = indices[:, None] * indices[None, :] % length
    angles = product.astype(jnp.float32) * (2.0 * math.pi / length)
    factor_norm = 1.0 / math.sqrt(length)
    return (jnp.cos(angles) * factor_norm, -jnp.sin(angles) * factor_norm)

def transform(field_real, field_imag, table_real, table_imag, direction):
    signed = direction * table_imag
    left_real = jnp.einsum('jk,...kl->...jl', table_real, field_real, precision=PRECISE_DOT) - jnp.einsum('jk,...kl->...jl', signed, field_imag, precision=PRECISE_DOT)
    left_imag = jnp.einsum('jk,...kl->...jl', table_real, field_imag, precision=PRECISE_DOT) + jnp.einsum('jk,...kl->...jl', signed, field_real, precision=PRECISE_DOT)
    out_real = jnp.einsum('...jk,kl->...jl', left_real, table_real, precision=PRECISE_DOT) - jnp.einsum('...jk,kl->...jl', left_imag, signed, precision=PRECISE_DOT)
    out_imag = jnp.einsum('...jk,kl->...jl', left_imag, table_real, precision=PRECISE_DOT) + jnp.einsum('...jk,kl->...jl', left_real, signed, precision=PRECISE_DOT)
    return (out_real, out_imag)

def patch_terms(patch_real, patch_imag, probe_real, probe_imag, measured, table_real, table_imag):
    wave_real = probe_real[None] * patch_real[:, None] - probe_imag[None] * patch_imag[:, None]
    wave_imag = probe_real[None] * patch_imag[:, None] + probe_imag[None] * patch_real[:, None]
    far_real, far_imag = transform(wave_real, wave_imag, table_real, table_imag, 1.0)
    intensity = lax.optimization_barrier(jnp.sum(far_real * far_real + far_imag * far_imag, axis=1))
    factor = measured / jnp.maximum(jnp.sqrt(intensity), AMP_FLOOR) - 1.0
    change_real, change_imag = transform(factor[:, None] * far_real, factor[:, None] * far_imag, table_real, table_imag, -1.0)
    object_real = lax.optimization_barrier(jnp.sum(probe_real[None] * change_real + probe_imag[None] * change_imag, axis=1))
    object_imag = lax.optimization_barrier(jnp.sum(probe_real[None] * change_imag - probe_imag[None] * change_real, axis=1))
    gradient_real = lax.optimization_barrier(jnp.sum(patch_real[:, None] * change_real + patch_imag[:, None] * change_imag, axis=0))
    gradient_imag = lax.optimization_barrier(jnp.sum(patch_real[:, None] * change_imag - patch_imag[:, None] * change_real, axis=0))
    object_power = lax.optimization_barrier(jnp.sum(patch_real * patch_real + patch_imag * patch_imag, axis=0))
    return (object_real, object_imag, gradient_real, gradient_imag, object_power)

def reference(object_field, probe, amplitudes, offsets):
    half_patch = PATCH // 2
    table_real, table_imag = dft_tables(PATCH)
    probe_real, probe_imag = (probe[0], probe[1])
    lighting = lax.optimization_barrier(jnp.sum(probe_real * probe_real + probe_imag * probe_imag, axis=0))
    grad_real = jnp.zeros((MODES, PATCH, PATCH), jnp.float32)
    grad_imag = jnp.zeros((MODES, PATCH, PATCH), jnp.float32)
    power_total = jnp.zeros((PATCH, PATCH), jnp.float32)
    device_rows = jnp.arange(GRID_ROWS, dtype=jnp.int32)[:, None, None] * TILE
    device_cols = jnp.arange(GRID_COLS, dtype=jnp.int32)[None, :, None] * TILE
    blocks = GRID_ROWS * GRID_COLS
    zero_start = jnp.zeros((), jnp.int32)
    current_object = object_field
    for batch_index in range(BATCHES):
        padded = jnp.pad(current_object, ((0, 0), (half_patch, half_patch), (half_patch, half_patch)))
        row_starts = (device_rows + offsets[:, :, batch_index, :, 0] + half_patch).reshape(-1).astype(jnp.int32)
        col_starts = (device_cols + offsets[:, :, batch_index, :, 1] + half_patch).reshape(-1).astype(jnp.int32)

        def one_patch(row_start, col_start):
            return lax.dynamic_slice(padded, (zero_start, row_start, col_start), (2, PATCH, PATCH))
        patches = jax.vmap(one_patch)(row_starts, col_starts)
        measured = amplitudes[:, :, batch_index].reshape(blocks, POS_DEV, PATCH, PATCH)

        def per_block(pieces):
            block_patches, block_measured = pieces
            return patch_terms(block_patches[:, 0], block_patches[:, 1], probe_real, probe_imag, block_measured, table_real, table_imag)
        object_real, object_imag, block_real, block_imag, block_power = lax.map(per_block, (patches.reshape(blocks, POS_DEV, 2, PATCH, PATCH), measured))
        grad_real = grad_real + lax.optimization_barrier(jnp.sum(block_real, axis=0))
        grad_imag = grad_imag + lax.optimization_barrier(jnp.sum(block_imag, axis=0))
        power_total = power_total + lax.optimization_barrier(jnp.sum(block_power, axis=0))
        object_real = object_real.reshape(-1, PATCH, PATCH)
        object_imag = object_imag.reshape(-1, PATCH, PATCH)
        stacked = jnp.stack([object_real, object_imag, jnp.broadcast_to(lighting, object_real.shape)], axis=1)
        buffer = jnp.zeros((3, ROWS_ALL + PATCH, COLS_ALL + PATCH), jnp.float32)

        def add_patch(position, current):
            corner = (zero_start, row_starts[position].astype(jnp.int32), col_starts[position].astype(jnp.int32))
            region = lax.dynamic_slice(current, corner, (3, PATCH, PATCH))
            return lax.dynamic_update_slice(current, region + stacked[position], corner)
        buffer = lax.fori_loop(0, stacked.shape[0], add_patch, buffer)
        center = buffer[:, half_patch:half_patch + ROWS_ALL, half_patch:half_patch + COLS_ALL]
        current_object = current_object + center[0:2] / (center[2] + OBJECT_REG)
    root_power = jnp.sqrt(power_total + PROBE_REG)
    probe_step = jnp.stack([grad_real / root_power, grad_imag / root_power])
    return (current_object, probe_step)
```

```python
import functools
import math

import jax
import jax.numpy as jnp
import ml_dtypes
import numpy as np
from jax import lax
from jax.experimental import pallas as pl
from jax.experimental.pallas import tpu as pltpu
from jax.sharding import PartitionSpec as P

N = 128
MODES = 4
TILE = 256
POS = 4
BATCHES = 3
HALF = 64
PADROWS = 384
FAR = 100000

AMP_FLOOR = 0.25
OBJECT_REG = 0.5
PROBE_REG = 1.0

MESH = pl.DeviceIdType.MESH
VM = pl.BlockSpec(memory_space=pltpu.VMEM)
SM = pl.BlockSpec(memory_space=pltpu.SMEM)


def tables():
    k = np.arange(N)
    ang = (k[:, None] * k[None, :] % N) * (2.0 * math.pi / N)
    fr, fi = np.cos(ang) / math.sqrt(N), -np.sin(ang) / math.sqrt(N)
    a = np.block([[fr, fi], [-fi, fr]])
    b = np.block([[fr, -fi], [fi, fr]])

    def split(m):
        hi = m.astype(np.float32).astype(ml_dtypes.bfloat16)
        lo = (m - hi.astype(np.float64)).astype(np.float32).astype(ml_dtypes.bfloat16)
        return hi, lo

    ah, al = split(a)
    bh, bl = split(b)
    right = lambda h, l: np.concatenate([h, h, l], axis=0)
    left = lambda h, l: np.concatenate([h, h, l], axis=1)
    return right(ah, al), left(bh, bl), left(ah, al), right(bh, bl)


def lanes(shape):
    return lax.broadcasted_iota(jnp.int32, shape, 1)


def split_hi_lo(x):
    hi = x.astype(jnp.bfloat16)
    lo = (x - hi.astype(jnp.float32)).astype(jnp.bfloat16)
    return hi, lo


def dot(a, b):
    return jnp.dot(a, b, preferred_element_type=jnp.float32)


def right_mul(x, table):
    hi, lo = split_hi_lo(x)
    return dot(jnp.concatenate([hi, lo, hi], axis=1), table)


def left_mul(table, x):
    hi, lo = split_hi_lo(x)
    return dot(table, jnp.concatenate([hi, lo, hi], axis=0))


def compute_kernel(batch, offs, info, obj, hl, hr, probe, amp, gin, a3r, b3l, a3l, b3r,
                   center, left, right, linv, gout, pad, buf, light, ltg):
    lane = lanes((N, N))
    for ch in range(2):
        pad[ch, 1] = obj[ch, :, 0:128]
        pad[ch, 2] = obj[ch, :, 128:256]
    pad[0, 0] = pltpu.roll(hl[...], HALF, 1)
    pad[1, 0] = hl[...]
    pad[0, 3] = hr[...]
    pad[1, 3] = pltpu.roll(hr[...], HALF, 1)
    buf[...] = jnp.zeros(buf.shape, jnp.float32)
    light[...] = jnp.zeros(light.shape, jnp.float32)
    gout[...] = gin[...]
    total = jnp.zeros((N, N), jnp.float32)
    for m in range(MODES):
        total += probe[0, m] * probe[0, m] + probe[1, m] * probe[1, m]
    ltg[...] = total

    def place(ref, rows, c0, value):
        t = lax.shift_right_logical(c0, 7)
        s = lax.bitwise_and(c0, 127)
        turned = pltpu.roll(value, s, 1)
        ref[t, rows] += jnp.where(lane >= s, turned, 0.0)
        ref[t + 1, rows] += jnp.where(lane < s, turned, 0.0)

    def light_step(i, carry):
        block = i // POS
        p = i % POS
        cr = block // 3
        rr = block % 3
        r = offs[cr, rr, 0, batch * 8 + p * 2] + (rr - 1) * TILE
        c = offs[cr, rr, 0, batch * 8 + p * 2 + 1] + (cr - 1) * TILE

        @pl.when((r > -192) & (r < 320) & (c > -128) & (c < 256))
        def _():
            place(light, pl.ds(r + 192, N), c + 128, ltg[...])

        return carry

    lax.fori_loop(0, 9 * POS, light_step, 0)

    def step(p, carry):
        r0 = offs[1, 1, 0, batch * 8 + p * 2] + HALF
        c0 = offs[1, 1, 0, batch * 8 + p * 2 + 1] + 128
        t = lax.shift_right_logical(c0, 7)
        s = lax.bitwise_and(c0, 127)
        rows = pl.ds(r0, N)
        back = lax.bitwise_and(128 - s, 127)

        def cut(ch):
            one = pltpu.roll(pad[ch, t, rows], back, 1)
            two = pltpu.roll(pad[ch, t + 1, rows], back, 1)
            return jnp.where(lane < 128 - s, one, two)

        pr, pi = cut(0), cut(1)
        waves = []
        for m in range(MODES):
            qr, qi = probe[0, m], probe[1, m]
            waves.append(jnp.concatenate([qr * pr - qi * pi, qr * pi + qi * pr], axis=1))
        half = right_mul(jnp.concatenate(waves, axis=0), a3r[...])
        rows_of = [half[m * N:(m + 1) * N] for m in range(MODES)]
        stacked = jnp.concatenate(
            [jnp.concatenate([h[:, :N] for h in rows_of], axis=1),
             jnp.concatenate([h[:, N:] for h in rows_of], axis=1)], axis=0)
        far = left_mul(b3l[...], stacked)
        inten = jnp.zeros((N, N), jnp.float32)
        for m in range(MODES):
            fr, fi = far[:N, m * N:(m + 1) * N], far[N:, m * N:(m + 1) * N]
            inten += fr * fr + fi * fi
        factor = amp[p] * lax.rsqrt(jnp.maximum(inten, AMP_FLOOR * AMP_FLOOR)) - 1.0
        factor = jnp.concatenate([factor] * MODES, axis=1)
        factor = jnp.concatenate([factor] * 2, axis=0)
        back_half = left_mul(a3l[...], far * factor)
        lhs = jnp.concatenate(
            [jnp.concatenate([back_half[:N, m * N:(m + 1) * N], back_half[N:, m * N:(m + 1) * N]], axis=1)
             for m in range(MODES)], axis=0)
        change = right_mul(lhs, b3r[...])
        tr = jnp.zeros((N, N), jnp.float32)
        ti = jnp.zeros((N, N), jnp.float32)
        for m in range(MODES):
            qr, qi = probe[0, m], probe[1, m]
            cr, ci = change[m * N:(m + 1) * N, :N], change[m * N:(m + 1) * N, N:]
            tr += qr * cr + qi * ci
            ti += qr * ci - qi * cr
            gout[m] += pr * cr + pi * ci
            gout[MODES + m] += pr * ci - pi * cr
        gout[2 * MODES] += pr * pr + pi * pi
        place(buf.at[0], rows, c0, tr)
        place(buf.at[1], rows, c0, ti)
        return carry

    lax.fori_loop(0, POS, step, 0)

    for ch in range(2):
        center[ch, :, 0:128] = buf[ch, 1]
        center[ch, :, 128:256] = buf[ch, 2]
    wide = lanes((PADROWS, N))
    left[...] = jnp.where(wide < HALF, pltpu.roll(buf[0, 0], HALF, 1), buf[1, 0])
    right[...] = jnp.where(wide < HALF, buf[0, 3], pltpu.roll(buf[1, 3], HALF, 1))
    row = lax.broadcasted_iota(jnp.int32, (PADROWS, N), 0)
    low = jnp.where(info[0] == 0, HALF, 0)
    high = jnp.where(info[0] == info[1] - 1, HALF + TILE, PADROWS)
    inside = (row >= low) & (row < high)
    for t in range(2):
        linv[:, t * 128:t * 128 + 128] = jnp.where(inside, 1.0 / (light[t + 1, 128:512] + OBJECT_REG), 0.0)


def run_compute(batch, offs, info, obj, hl, hr, probe, amp, gin, tabs):
    f = jnp.float32
    return pl.pallas_call(
        functools.partial(compute_kernel, batch),
        out_shape=(
            jax.ShapeDtypeStruct((2, PADROWS, TILE), f),
            jax.ShapeDtypeStruct((PADROWS, N), f),
            jax.ShapeDtypeStruct((PADROWS, N), f),
            jax.ShapeDtypeStruct((PADROWS, TILE), f),
            jax.ShapeDtypeStruct((2 * MODES + 1, N, N), f),
        ),
        in_specs=[SM, SM] + [VM] * 10,
        out_specs=(VM,) * 5,
        scratch_shapes=[
            pltpu.VMEM((2, 4, PADROWS, N), f),
            pltpu.VMEM((2, 4, PADROWS, N), f),
            pltpu.VMEM((4, 640, N), f),
            pltpu.VMEM((N, N), f),
        ],
        compiler_params=pltpu.CompilerParams(vmem_limit_bytes=28 * 2**20),
        name="compute",
    )(offs, info, obj, hl, hr, probe, amp, gin, *tabs)


def position():
    row, col = lax.axis_index("row"), lax.axis_index("col")
    rows, cols = lax.axis_size("row"), lax.axis_size("col")
    up = (row > 0, {"row": jnp.maximum(row - 1, 0), "col": col})
    down = (row < rows - 1, {"row": jnp.minimum(row + 1, rows - 1), "col": col})
    left = (col > 0, {"row": row, "col": jnp.maximum(col - 1, 0)})
    right = (col < cols - 1, {"row": row, "col": jnp.minimum(col + 1, cols - 1)})
    return up, down, left, right


def greet(sides):
    barrier = pltpu.get_barrier_semaphore()
    for there, device in sides:
        @pl.when(there)
        def _(device=device):
            pl.semaphore_signal(barrier, inc=1, device_id=device, device_id_type=MESH)
    pl.semaphore_wait(barrier, sum(there.astype(jnp.int32) for there, _ in sides))


class Link:
    def __init__(self, src, dst, send, recv, to, source):
        self.there, device = to
        self.source = source[0]
        self.copy = pltpu.make_async_remote_copy(
            src_ref=src, dst_ref=dst, send_sem=send, recv_sem=recv,
            device_id=device, device_id_type=MESH)

    def start(self):
        @pl.when(self.there)
        def _():
            self.copy.start()

    def arrived(self):
        @pl.when(self.source)
        def _():
            self.copy.wait_recv()

    def sent(self):
        @pl.when(self.there)
        def _():
            self.copy.wait_send()


def strips(re0, im0, re1, im1):
    lane = lanes(re0.shape)
    left = jnp.where(lane < HALF, re0, pltpu.roll(im0, HALF, 1))
    right = jnp.where(lane < HALF, pltpu.roll(re1, HALF, 1), im1)
    return left, right


def first_kernel(obj, offs, out, hl_out, hr_out, offs_out,
                 from_up, from_down, sl, sr, hl, hr, table, send, recv):
    up, down, left, right = position()
    for ref in (from_up, from_down, hl, hr):
        ref[...] = jnp.zeros(ref.shape, ref.dtype)
    table[...] = jnp.full(table.shape, FAR, jnp.int32)
    table[1, 1] = offs[...]
    greet((up, down, left, right))

    count = iter(range(100))

    def link(src, dst, to, source):
        i = next(count)
        return Link(src, dst, send.at[i], recv.at[i], to, source)

    rows = [
        link(obj.at[:, pl.ds(0, HALF), :], from_down, up, down),
        link(obj.at[:, pl.ds(TILE - HALF, HALF), :], from_up, down, up),
        link(table.at[1, 1], table.at[1, 2], up, down),
        link(table.at[1, 1], table.at[1, 0], down, up),
    ]
    for c in rows:
        c.start()

    def cols(at, size):
        a = link(sl.at[pl.ds(at, size)], hr.at[pl.ds(at, size)], left, right)
        b = link(sr.at[pl.ds(at, size)], hl.at[pl.ds(at, size)], right, left)
        return [a, b]

    every = list(rows)
    a, b = strips(obj[0, :, 0:128], obj[1, :, 0:128], obj[0, :, 128:256], obj[1, :, 128:256])
    sl[HALF:HALF + TILE] = a
    sr[HALF:HALF + TILE] = b
    mid = cols(HALF, TILE)
    for c in mid:
        c.start()
    every += mid
    out[:, HALF:HALF + TILE, :] = obj[...]
    for c in rows:
        c.arrived()
    more = [
        link(table.at[1], table.at[2], left, right),
        link(table.at[1], table.at[0], right, left),
    ]
    for c in more:
        c.start()
    for ref, at in ((from_up, 0), (from_down, HALF + TILE)):
        a, b = strips(ref[0, :, 0:128], ref[1, :, 0:128], ref[0, :, 128:256], ref[1, :, 128:256])
        sl[at:at + HALF] = a
        sr[at:at + HALF] = b
        both = cols(at, HALF)
        for c in both:
            c.start()
        more += both
        out[:, at:at + HALF, :] = ref[...]
    every += more
    for c in mid + more:
        c.arrived()
    hl_out[...] = hl[...]
    hr_out[...] = hr[...]
    offs_out[...] = table[...]
    for c in every:
        c.sent()


def run_first(obj, offs):
    f = jnp.float32
    return pl.pallas_call(
        first_kernel,
        out_shape=(
            jax.ShapeDtypeStruct((2, PADROWS, TILE), f),
            jax.ShapeDtypeStruct((PADROWS, N), f),
            jax.ShapeDtypeStruct((PADROWS, N), f),
            jax.ShapeDtypeStruct((3, 3, 8, N), jnp.int32),
        ),
        in_specs=[VM, VM],
        out_specs=(VM,) * 4,
        scratch_shapes=[
            pltpu.VMEM((2, HALF, TILE), f),
            pltpu.VMEM((2, HALF, TILE), f),
            pltpu.VMEM((PADROWS, N), f),
            pltpu.VMEM((PADROWS, N), f),
            pltpu.VMEM((PADROWS, N), f),
            pltpu.VMEM((PADROWS, N), f),
            pltpu.VMEM((3, 3, 8, N), jnp.int32),
            pltpu.SemaphoreType.DMA((12,)),
            pltpu.SemaphoreType.DMA((12,)),
        ],
        compiler_params=pltpu.CompilerParams(collective_id=0, has_side_effects=True, vmem_limit_bytes=14 * 2**20),
        name="first",
    )(obj, offs)


def fold_kernel(last, center, ls, rs, obj, linv, out, *rest):
    if last:
        from_left, from_right, total, from_up, from_down, send, recv = rest
        reach = HALF
    else:
        hl_out, hr_out, from_left, from_right, total, from_up, from_down, sl, sr, hl, hr, send, recv = rest
        reach = N
    up, down, left, right = position()
    for ref in (from_left, from_right, from_up, from_down) + (() if last else (hl, hr)):
        ref[...] = jnp.zeros(ref.shape, ref.dtype)
    greet((up, down, left, right))
    count = iter(range(100))

    def link(src, dst, to, source):
        i = next(count)
        return Link(src, dst, send.at[i], recv.at[i], to, source)

    every = []
    cols = {}
    for at in (0, 256, 128):
        w = pl.ds(at, N)
        cols[at] = [link(ls.at[w], from_right.at[w], left, right),
                    link(rs.at[w], from_left.at[w], right, left)]
        for c in cols[at]:
            c.start()
        every += cols[at]

    def add_cols(at):
        for c in cols[at]:
            c.arrived()
        w = slice(at, at + N)
        lane = lanes((N, N))
        a, b = from_left[w], from_right[w]
        total[0, w, 0:128] = center[0, w, 0:128] + jnp.where(lane < HALF, a, 0.0)
        total[1, w, 0:128] = center[1, w, 0:128] + jnp.where(lane < HALF, pltpu.roll(a, HALF, 1), 0.0)
        total[0, w, 128:256] = center[0, w, 128:256] + jnp.where(lane >= HALF, pltpu.roll(b, HALF, 1), 0.0)
        total[1, w, 128:256] = center[1, w, 128:256] + jnp.where(lane >= HALF, b, 0.0)

    add_cols(0)
    to_up = link(total.at[:, pl.ds(0, reach), :], from_down, up, down)
    to_up.start()
    add_cols(256)
    to_down = link(total.at[:, pl.ds(PADROWS - reach, reach), :], from_up, down, up)
    to_down.start()
    add_cols(128)
    every += [to_up, to_down]

    halos = []

    def update(at, size, extra):
        w = slice(at, at + size)
        lv = linv[w]
        new = []
        for ch in range(2):
            t = total[ch, w]
            if extra is not None:
                t = t + extra[ch]
            new.append(obj[ch, w] + t * lv)
            if last:
                out[ch, at - HALF:at - HALF + size] = new[ch]
            else:
                out[ch, w] = new[ch]
        if not last:
            a, b = strips(new[0][:, 0:128], new[1][:, 0:128], new[0][:, 128:256], new[1][:, 128:256])
            sl[w] = a
            sr[w] = b
            d = pl.ds(at, size)
            both = [link(sl.at[d], hr.at[d], left, right), link(sr.at[d], hl.at[d], right, left)]
            for c in both:
                c.start()
            halos.extend(both)

    update(N, N, None)
    start = HALF if last else 0
    to_down.arrived()
    update(start, reach, from_up)
    to_up.arrived()
    update(256, reach, from_down)
    every += halos
    if not last:
        for c in halos:
            c.arrived()
        hl_out[...] = hl[...]
        hr_out[...] = hr[...]
    for c in every:
        c.sent()


def run_fold(last, ident, center, ls, rs, obj, linv):
    f = jnp.float32
    reach = HALF if last else N
    strip = pltpu.VMEM((PADROWS, N), f)
    strip_out = jax.ShapeDtypeStruct((PADROWS, N), f)
    if last:
        shapes = (jax.ShapeDtypeStruct((2, TILE, TILE), f),)
    else:
        shapes = (jax.ShapeDtypeStruct((2, PADROWS, TILE), f), strip_out, strip_out)
    return pl.pallas_call(
        functools.partial(fold_kernel, last),
        out_shape=shapes,
        in_specs=[VM] * 5,
        out_specs=(VM,) * len(shapes),
        scratch_shapes=[
            strip, strip,
            pltpu.VMEM((2, PADROWS, TILE), f),
            pltpu.VMEM((2, reach, TILE), f),
            pltpu.VMEM((2, reach, TILE), f),
        ] + ([] if last else [strip] * 4) + [
            pltpu.SemaphoreType.DMA((14,)),
            pltpu.SemaphoreType.DMA((14,)),
        ],
        compiler_params=pltpu.CompilerParams(collective_id=ident, has_side_effects=True, vmem_limit_bytes=14 * 2**20),
        name="fold_last" if last else f"fold{ident}",
    )(center, ls, rs, obj, linv)


TILES = 144
HALFT = 72
PIECE = 9
SUB = 3


def reduce_kernel(g, out, r1, s1, r2, s2, r3, z, fin, ag1, ag2, ag3, send, recv):
    row, col = lax.axis_index("row"), lax.axis_index("col")
    x, zh = row // 4, row % 4
    core, group = col % 2, col // 2
    partner = {"row": row, "col": col + 1 - 2 * core}

    def in_group(d):
        return lax.rem(group + d, 8)

    def group_dev(k):
        return {"row": row, "col": k * 2 + core}

    def x_dev(k):
        return {"row": k * 4 + zh, "col": col}

    def z_dev(k):
        return {"row": x * 4 + k, "col": col}

    peers = [partner] + [group_dev(in_group(d)) for d in range(1, 8)]
    peers += [x_dev(lax.rem(x + d, 4)) for d in range(1, 4)]
    peers += [z_dev(lax.rem(zh + d, 4)) for d in range(1, 4)]

    s2[pl.ds(PIECE, 12 - PIECE)] = jnp.zeros((12 - PIECE, 8, N), jnp.float32)
    barrier = pltpu.get_barrier_semaphore()
    for device in peers:
        pl.semaphore_signal(barrier, inc=1, device_id=device, device_id_type=MESH)
    pl.semaphore_wait(barrier, len(peers))

    count = iter(range(100))
    every = []

    def go(src, dst, device):
        i = next(count)
        c = pltpu.make_async_remote_copy(
            src_ref=src, dst_ref=dst, send_sem=send.at[i], recv_sem=recv.at[i],
            device_id=device, device_id_type=MESH)
        c.start()
        every.append(c)
        return c

    c = go(g.at[pl.ds((1 - core) * HALFT, HALFT)], r1, partner)
    c.wait_recv()
    s1[...] = g[pl.ds(core * HALFT, HALFT)] + r1[...]

    cs = [go(s1.at[pl.ds(in_group(d) * PIECE, PIECE)], r2.at[d - 1], group_dev(in_group(d))) for d in range(1, 8)]
    acc = s1[pl.ds(group * PIECE, PIECE)]
    for d, c in enumerate(cs):
        c.wait_recv()
        acc = acc + r2[d]
    s2[pl.ds(0, PIECE)] = acc

    cs = [go(s2.at[pl.ds(lax.rem(x + d, 4) * SUB, SUB)], r3.at[d - 1], x_dev(lax.rem(x + d, 4))) for d in range(1, 4)]
    acc = s2[pl.ds(x * SUB, SUB)]
    for d, c in enumerate(cs):
        c.wait_recv()
        acc = acc + r3[d]
    z[0] = acc

    cs = [go(z.at[0], z.at[d], z_dev(lax.rem(zh + d, 4))) for d in range(1, 4)]
    for c in cs:
        c.wait_recv()
    acc = z[lax.rem(zh, 4)]
    for k in range(1, 4):
        acc = acc + z[lax.rem(zh - k + 4, 4)]
    fin[...] = acc

    cs = [go(fin, ag1.at[pl.ds(x * SUB, SUB)], x_dev(lax.rem(x + d, 4))) for d in range(1, 4)]
    ag1[pl.ds(x * SUB, SUB)] = fin[...]
    for c in cs:
        c.wait_recv()

    cs = [go(ag1.at[pl.ds(0, PIECE)], ag2.at[pl.ds(group * PIECE, PIECE)], group_dev(in_group(d))) for d in range(1, 8)]
    ag2[pl.ds(group * PIECE, PIECE)] = ag1[pl.ds(0, PIECE)]
    for c in cs:
        c.wait_recv()

    c = go(ag2, ag3.at[pl.ds(core * HALFT, HALFT)], partner)
    ag3[pl.ds(core * HALFT, HALFT)] = ag2[...]
    c.wait_recv()

    inv = lax.rsqrt(ag3[pl.ds(128, 16)] + PROBE_REG)
    for k in range(8):
        out[pl.ds(16 * k, 16)] = ag3[pl.ds(16 * k, 16)] * inv
    for c in every:
        c.wait_send()


def run_reduce(g):
    f = jnp.float32
    shape = lambda *n: pltpu.VMEM(n + (8, N), f)
    return pl.pallas_call(
        reduce_kernel,
        out_shape=jax.ShapeDtypeStruct((128, 8, N), f),
        in_specs=[VM],
        out_specs=VM,
        scratch_shapes=[
            shape(HALFT), shape(HALFT), shape(7, PIECE), shape(12), shape(3, SUB),
            shape(4, SUB), shape(SUB), shape(12), shape(HALFT), shape(TILES),
            pltpu.SemaphoreType.DMA((25,)),
            pltpu.SemaphoreType.DMA((25,)),
        ],
        compiler_params=pltpu.CompilerParams(collective_id=9, has_side_effects=True, vmem_limit_bytes=14 * 2**20),
        name="reduce",
    )(g)


def on_device(object_field, probe, amplitudes, offsets):
    info = jnp.stack([lax.axis_index("row"), jnp.int32(lax.axis_size("row"))]).astype(jnp.int32)
    mine = jnp.pad(offsets.reshape(1, 24), ((0, 7), (0, N - 24)))
    tabs = [jnp.asarray(t) for t in tables()]
    obj, hl, hr, offs = run_first(object_field, mine)
    grads = jnp.zeros((2 * MODES + 1, N, N), jnp.float32)
    amps = amplitudes.reshape(BATCHES, POS, N, N)
    for b in range(BATCHES):
        center, ls, rs, linv, grads = run_compute(b, offs, info, obj, hl, hr, probe, amps[b], grads, tabs)
        if b < BATCHES - 1:
            obj, hl, hr = run_fold(False, b + 1, center, ls, rs, obj, linv)
        else:
            (obj,) = run_fold(True, b + 1, center, ls, rs, obj, linv)
    step = run_reduce(grads.reshape(TILES, 8, N))
    return obj, step.reshape(2, MODES, N, N)


def solution(mesh):
    placed = (
        P(None, "row", "col"),
        P(),
        P("row", "col", None, None, None, None),
        P("row", "col", None, None, None),
    )
    return jax.shard_map(
        on_device,
        mesh=mesh,
        in_specs=placed,
        out_specs=(P(None, "row", "col"), P()),
        check_vma=False,
    )
```

```python
import functools
import math

import jax
import jax.numpy as jnp
import ml_dtypes
import numpy as np
from jax import lax
from jax.experimental import pallas as pl
from jax.experimental.pallas import tpu as pltpu
from jax.sharding import PartitionSpec as P

N = 128
MODES = 4
TILE = 256
POS = 4
BATCHES = 3
HALF = 64
PADROWS = 384
FAR = 100000

AMP_FLOOR = 0.25
OBJECT_REG = 0.5
PROBE_REG = 1.0

MESH = pl.DeviceIdType.MESH
VM = pl.BlockSpec(memory_space=pltpu.VMEM)
SM = pl.BlockSpec(memory_space=pltpu.SMEM)


def tables():
    k = np.arange(N)
    ang = (k[:, None] * k[None, :] % N) * (2.0 * math.pi / N)
    fr, fi = np.cos(ang) / math.sqrt(N), -np.sin(ang) / math.sqrt(N)
    a = np.block([[fr, fi], [-fi, fr]])
    b = np.block([[fr, -fi], [fi, fr]])

    def split(m):
        hi = m.astype(np.float32).astype(ml_dtypes.bfloat16)
        lo = (m - hi.astype(np.float64)).astype(np.float32).astype(ml_dtypes.bfloat16)
        return hi, lo

    ah, al = split(a)
    bh, bl = split(b)
    right = lambda h, l: np.concatenate([h, h, l], axis=0)
    left = lambda h, l: np.concatenate([h, h, l], axis=1)
    return right(ah, al), left(bh, bl), left(ah, al), right(bh, bl)


def lanes(shape):
    return lax.broadcasted_iota(jnp.int32, shape, 1)


def split_hi_lo(x):
    hi = x.astype(jnp.bfloat16)
    lo = (x - hi.astype(jnp.float32)).astype(jnp.bfloat16)
    return hi, lo


def dot(a, b):
    return jnp.dot(a, b, preferred_element_type=jnp.float32)


def right_mul(x, table):
    hi, lo = split_hi_lo(x)
    return dot(jnp.concatenate([hi, lo, hi], axis=1), table)


def left_mul(table, x):
    hi, lo = split_hi_lo(x)
    return dot(table, jnp.concatenate([hi, lo, hi], axis=0))


def position():
    row, col = lax.axis_index("row"), lax.axis_index("col")
    rows, cols = lax.axis_size("row"), lax.axis_size("col")
    up = (row > 0, {"row": jnp.maximum(row - 1, 0), "col": col})
    down = (row < rows - 1, {"row": jnp.minimum(row + 1, rows - 1), "col": col})
    left = (col > 0, {"row": row, "col": jnp.maximum(col - 1, 0)})
    right = (col < cols - 1, {"row": row, "col": jnp.minimum(col + 1, cols - 1)})
    return up, down, left, right


def greet(sides, others=()):
    barrier = pltpu.get_barrier_semaphore()
    for there, device in sides:
        @pl.when(there)
        def _(device=device):
            pl.semaphore_signal(barrier, inc=1, device_id=device, device_id_type=MESH)
    for device in others:
        pl.semaphore_signal(barrier, inc=1, device_id=device, device_id_type=MESH)


def greeted(sides, others=()):
    barrier = pltpu.get_barrier_semaphore()
    pl.semaphore_wait(barrier, sum(there.astype(jnp.int32) for there, _ in sides) + len(others))


class Link:
    def __init__(self, src, dst, send, recv, to, source):
        self.there, device = to
        self.source = source[0]
        self.copy = pltpu.make_async_remote_copy(
            src_ref=src, dst_ref=dst, send_sem=send, recv_sem=recv,
            device_id=device, device_id_type=MESH)

    def start(self):
        @pl.when(self.there)
        def _():
            self.copy.start()

    def arrived(self):
        @pl.when(self.source)
        def _():
            self.copy.wait_recv()

    def sent(self):
        @pl.when(self.there)
        def _():
            self.copy.wait_send()


def clear_missing(pairs):
    for there, ref in pairs:
        @pl.when(jnp.logical_not(there))
        def _(ref=ref):
            ref[...] = jnp.zeros(ref.shape, ref.dtype)


def turn(x):
    return pltpu.roll(x, HALF, 1)


def halo_strips(re, im):
    lane = lanes(re.shape)
    ti = turn(im)
    return jnp.where(lane < HALF, ti, re), jnp.where(lane < HALF, re, ti)


def first_kernel(obj, offs, out, offs_out, me, sl, sr, hl, hr, table, send, recv):
    up, down, left, right = position()
    lane = lanes((TILE, N))
    table[...] = jnp.full(table.shape, FAR, jnp.int32)
    table[1, 1] = offs[...]
    clear_missing([(left[0], hl), (right[0], hr),
                   (up[0], me.at[:, :, pl.ds(0, HALF), :]),
                   (down[0], me.at[:, :, pl.ds(PADROWS - HALF, HALF), :])])
    greet((up, down, left, right))
    own = slice(HALF, HALF + TILE)
    for ch in range(2):
        a, b = turn(obj[ch, :, 0:128]), turn(obj[ch, :, 128:256])
        me[1, ch, own] = jnp.where(lane < HALF, b, a)
        me[0, ch, own] = jnp.where(lane < HALF, a, b)
    greeted((up, down, left, right))

    count = iter(range(100))

    def link(src, dst, to, source):
        i = next(count)
        return Link(src, dst, send.at[i], recv.at[i], to, source)

    def rows(which):
        top, bottom = pl.ds(HALF, HALF), pl.ds(TILE, HALF)
        above, below = pl.ds(0, HALF), pl.ds(PADROWS - HALF, HALF)
        return [link(me.at[which, :, top, :], me.at[which, :, below, :], up, down),
                link(me.at[which, :, bottom, :], me.at[which, :, above, :], down, up)]

    def cols(at, size):
        w = slice(at, at + size)
        a, b = halo_strips(me[1, 0, w], me[1, 1, w])
        sl[w] = a
        sr[w] = b
        d = pl.ds(at, size)
        both = [link(sl.at[d], hr.at[d], left, right), link(sr.at[d], hl.at[d], right, left)]
        for c in both:
            c.start()
        return both

    tell = [link(table.at[1, 1], table.at[1, 2], up, down),
            link(table.at[1, 1], table.at[1, 0], down, up)]
    edge = rows(1)
    middle = rows(0)
    for c in tell + edge:
        c.start()
    late = cols(HALF, TILE)
    for c in middle:
        c.start()
    for c in tell:
        c.arrived()
    more = [link(table.at[1], table.at[2], left, right),
            link(table.at[1], table.at[0], right, left)]
    for c in more:
        c.start()
    late += more
    edge[1].arrived()
    late += cols(0, HALF)
    edge[0].arrived()
    late += cols(PADROWS - HALF, HALF)
    for c in middle:
        c.arrived()
    for ch in range(2):
        out[ch, 1] = me[0, ch]
    for c in late:
        c.arrived()
    finish_tiles(out, me, hl, hr)
    offs_out[...] = table[...]
    for c in tell + edge + middle + late:
        c.sent()


def finish_tiles(out, me, hl, hr):
    wide = lanes((PADROWS, N))
    out[0, 0] = jnp.where(wide < HALF, hl[...], me[1, 0])
    out[1, 0] = jnp.where(wide < HALF, turn(hl[...]), me[1, 1])
    out[0, 2] = jnp.where(wide < HALF, me[1, 0], hr[...])
    out[1, 2] = jnp.where(wide < HALF, me[1, 1], turn(hr[...]))


def run_first(obj, offs):
    f = jnp.float32
    strip = pltpu.VMEM((PADROWS, N), f)
    return pl.pallas_call(
        first_kernel,
        out_shape=(
            jax.ShapeDtypeStruct((2, 3, PADROWS, N), f),
            jax.ShapeDtypeStruct((3, 3, 8, N), jnp.int32),
        ),
        in_specs=[VM, VM],
        out_specs=(VM,) * 2,
        scratch_shapes=[
            pltpu.VMEM((2, 2, PADROWS, N), f),
            strip, strip, strip, strip,
            pltpu.VMEM((3, 3, 8, N), jnp.int32),
            pltpu.SemaphoreType.DMA((14,)),
            pltpu.SemaphoreType.DMA((14,)),
        ],
        compiler_params=pltpu.CompilerParams(collective_id=0, has_side_effects=True, vmem_limit_bytes=14 * 2**20),
        name="first",
    )(obj, offs)


def spread(dest, value, s):
    lane = lanes((N, N))
    turned = pltpu.roll(value, s, 1)
    dest[0, N:2 * N] = jnp.where(lane >= s, turned, 0.0)
    dest[1, N:2 * N] = jnp.where(lane < s, turned, 0.0)


def window(src, r0, t, i, k):
    j = k - t
    hit = (j == 0) | (j == 1)
    start = jnp.where(hit, jnp.clip(N + N * i - r0, 0, 2 * N), 0)
    return src[jnp.where(hit, j, 0), pl.ds(start, N)]


def transforms(batch, offs, tiles, probe, amp, gout, z, a3r, b3l, a3l, b3r):
    lane = lanes((N, N))

    def step(p, carry):
        r0 = offs[1, 1, 0, batch * 8 + p * 2] + HALF
        c0 = offs[1, 1, 0, batch * 8 + p * 2 + 1] + HALF
        t = lax.shift_right_arithmetic(c0, 7)
        s = lax.bitwise_and(c0, 127)
        rows = pl.ds(r0, N)
        back = lax.bitwise_and(128 - s, 127)
        after = jnp.minimum(t + 1, 2)

        def cut(ch):
            one = pltpu.roll(tiles[ch, t, rows], back, 1)
            two = pltpu.roll(tiles[ch, after, rows], back, 1)
            return jnp.where(lane < 128 - s, one, two)

        pr, pi = cut(0), cut(1)
        waves = []
        for m in range(MODES):
            qr, qi = probe[0, m], probe[1, m]
            waves.append(jnp.concatenate([qr * pr - qi * pi, qr * pi + qi * pr], axis=1))
        half = right_mul(jnp.concatenate(waves, axis=0), a3r[...])
        rows_of = [half[m * N:(m + 1) * N] for m in range(MODES)]
        stacked = jnp.concatenate(
            [jnp.concatenate([h[:, :N] for h in rows_of], axis=1),
             jnp.concatenate([h[:, N:] for h in rows_of], axis=1)], axis=0)
        far = left_mul(b3l[...], stacked)
        inten = jnp.zeros((N, N), jnp.float32)
        for m in range(MODES):
            fr, fi = far[:N, m * N:(m + 1) * N], far[N:, m * N:(m + 1) * N]
            inten += fr * fr + fi * fi
        factor = amp[batch, p] * lax.rsqrt(jnp.maximum(inten, AMP_FLOOR * AMP_FLOOR)) - 1.0
        factor = jnp.concatenate([factor] * MODES, axis=1)
        factor = jnp.concatenate([factor] * 2, axis=0)
        back_half = left_mul(a3l[...], far * factor)
        lhs = jnp.concatenate(
            [jnp.concatenate([back_half[:N, m * N:(m + 1) * N], back_half[N:, m * N:(m + 1) * N]], axis=1)
             for m in range(MODES)], axis=0)
        change = right_mul(lhs, b3r[...])
        tr = jnp.zeros((N, N), jnp.float32)
        ti = jnp.zeros((N, N), jnp.float32)
        for m in range(MODES):
            qr, qi = probe[0, m], probe[1, m]
            cr, ci = change[m * N:(m + 1) * N, :N], change[m * N:(m + 1) * N, N:]
            tr += qr * cr + qi * ci
            ti += qr * ci - qi * cr
            gout[m] += pr * cr + pi * ci
            gout[MODES + m] += pr * ci - pi * cr
        gout[2 * MODES] += pr * pr + pi * pi
        spread(z.at[p, 0], tr, s)
        spread(z.at[p, 1], ti, s)
        return carry

    lax.fori_loop(0, POS, step, 0)


def light_maps(batch, offs, probe, zl, light):
    lane = lanes((N, N))
    total = jnp.zeros((N, N), jnp.float32)
    for m in range(MODES):
        total += probe[0, m] * probe[0, m] + probe[1, m] * probe[1, m]
    for j in range(2):
        zl[j, 0:N] = jnp.zeros((N, N), jnp.float32)
        zl[j, 2 * N:] = jnp.zeros((N, N), jnp.float32)
    zl[2, 0:N] = total
    light[...] = jnp.zeros(light.shape, jnp.float32)

    def step(i, carry):
        block, p = i // POS, i % POS
        cr, rr = block // 3, block % 3
        r0 = offs[cr, rr, 0, batch * 8 + p * 2] + (rr - 1) * TILE + HALF
        c0 = offs[cr, rr, 0, batch * 8 + p * 2 + 1] + (cr - 1) * TILE + HALF
        t = lax.shift_right_arithmetic(c0, 7)
        spread(zl, zl[2, 0:N], lax.bitwise_and(c0, 127))
        for b in range(3):
            w = slice(b * N, b * N + N)
            light[0, w] += window(zl, r0, t, b, 1)
            light[1, w] += jnp.where(lane < HALF, window(zl, r0, t, b, 2), window(zl, r0, t, b, 0))
        return carry

    lax.fori_loop(0, 9 * POS, step, 0)
    row, rows = lax.axis_index("row"), lax.axis_size("row")
    place = lax.broadcasted_iota(jnp.int32, (PADROWS, N), 0)
    low = jnp.where(row == 0, HALF, 0)
    high = jnp.where(row == rows - 1, HALF + TILE, PADROWS)
    inside = (place >= low) & (place < high)
    for j in range(2):
        light[j] = jnp.where(inside, 1.0 / (light[j] + OBJECT_REG), 0.0)


TILES = 144
HALFT = 72
PIECE = 9
SUB = 3


class Reduction:
    def __init__(self, g, out, r1, s1, r2, s2, r3, z, fin, ag1, ag2, ag3, send, recv):
        self.refs = (g, out, r1, s1, r2, s2, r3, z, fin, ag1, ag2, ag3)
        self.send, self.recv = send, recv
        self.count = iter(range(100))
        self.every = []
        row, col = lax.axis_index("row"), lax.axis_index("col")
        self.x, self.zh = row // 4, row % 4
        self.core, self.group = col % 2, col // 2
        self.row, self.col = row, col
        self.partner = {"row": row, "col": col + 1 - 2 * self.core}
        self.peers = [self.partner]
        self.peers += [self.group_dev(self.in_group(d)) for d in range(1, 8)]
        self.peers += [self.x_dev(d) for d in range(1, 4)]
        self.peers += [self.z_dev(d) for d in range(1, 4)]

    def in_group(self, d):
        return lax.rem(self.group + d, 8)

    def group_dev(self, k):
        return {"row": self.row, "col": k * 2 + self.core}

    def x_dev(self, d):
        return {"row": lax.rem(self.x + d, 4) * 4 + self.zh, "col": self.col}

    def z_dev(self, d):
        return {"row": self.x * 4 + lax.rem(self.zh + d, 4), "col": self.col}

    def go(self, src, dst, device):
        i = next(self.count)
        c = pltpu.make_async_remote_copy(
            src_ref=src, dst_ref=dst, send_sem=self.send.at[i], recv_sem=self.recv.at[i],
            device_id=device, device_id_type=MESH)
        c.start()
        self.every.append(c)
        return c

    def stages(self):
        g, out, r1, s1, r2, s2, r3, z, fin, ag1, ag2, ag3 = self.refs
        x, zh, core, group, go, in_group = self.x, self.zh, self.core, self.group, self.go, self.in_group
        s2[pl.ds(PIECE, 12 - PIECE)] = jnp.zeros((12 - PIECE, 8, N), jnp.float32)
        c = go(g.at[pl.ds((1 - core) * HALFT, HALFT)], r1, self.partner)
        yield
        c.wait_recv()
        s1[...] = g[pl.ds(core * HALFT, HALFT)] + r1[...]
        cs = [go(s1.at[pl.ds(in_group(d) * PIECE, PIECE)], r2.at[d - 1], self.group_dev(in_group(d))) for d in range(1, 8)]
        yield
        acc = s1[pl.ds(group * PIECE, PIECE)]
        for d, c in enumerate(cs):
            c.wait_recv()
            acc = acc + r2[d]
        s2[pl.ds(0, PIECE)] = acc
        cs = [go(s2.at[pl.ds(lax.rem(x + d, 4) * SUB, SUB)], r3.at[d - 1], self.x_dev(d)) for d in range(1, 4)]
        yield
        acc = s2[pl.ds(x * SUB, SUB)]
        for d, c in enumerate(cs):
            c.wait_recv()
            acc = acc + r3[d]
        z[0] = acc
        cs = [go(z.at[0], z.at[d], self.z_dev(d)) for d in range(1, 4)]
        yield
        for c in cs:
            c.wait_recv()
        acc = z[lax.rem(zh, 4)]
        for k in range(1, 4):
            acc = acc + z[lax.rem(zh - k + 4, 4)]
        fin[...] = acc
        cs = [go(fin, ag1.at[pl.ds(x * SUB, SUB)], self.x_dev(d)) for d in range(1, 4)]
        ag1[pl.ds(x * SUB, SUB)] = fin[...]
        yield
        for c in cs:
            c.wait_recv()
        cs = [go(ag1.at[pl.ds(0, PIECE)], ag2.at[pl.ds(group * PIECE, PIECE)], self.group_dev(in_group(d))) for d in range(1, 8)]
        ag2[pl.ds(group * PIECE, PIECE)] = ag1[pl.ds(0, PIECE)]
        yield
        for c in cs:
            c.wait_recv()
        c = go(ag2, ag3.at[pl.ds(core * HALFT, HALFT)], self.partner)
        ag3[pl.ds(core * HALFT, HALFT)] = ag2[...]
        yield
        c.wait_recv()
        inv = lax.rsqrt(ag3[pl.ds(128, 16)] + PROBE_REG)
        for k in range(8):
            out[pl.ds(16 * k, 16)] = ag3[pl.ds(16 * k, 16)] * inv
        for c in self.every:
            c.wait_send()
        yield


def reduction_scratch():
    f = jnp.float32
    shape = lambda *n: pltpu.VMEM(n + (8, N), f)
    return [shape(HALFT), shape(HALFT), shape(7, PIECE), shape(12), shape(3, SUB),
            shape(4, SUB), shape(SUB), shape(12), shape(HALFT), shape(TILES),
            pltpu.SemaphoreType.DMA((25,)), pltpu.SemaphoreType.DMA((25,))]


def batch_kernel(batch, last, offs, tiles, probe, amp, gin, a3r, b3l, a3l, b3r, *rest):
    if last:
        out, step_out, gout, flat, z, zl, light, ls, rs, ls_in, rs_in, me, fresh, from_up, from_down, send, recv, *more = rest
        reach = HALF
        red = Reduction(flat, step_out, *more)
        others = red.peers
    else:
        out, gout, z, zl, light, ls, rs, ls_in, rs_in, me, fresh, from_up, from_down, sl, sr, hl, hr, send, recv = rest
        reach = N
        others = ()
    up, down, left, right = sides = position()
    clear_missing([(left[0], rs_in), (right[0], ls_in), (up[0], from_up), (down[0], from_down)])
    if not last:
        clear_missing([(left[0], hl), (right[0], hr)])
    greet(sides, others)

    blank = jnp.zeros((N, N), jnp.float32)
    for p in range(POS):
        for ch in range(2):
            for j in range(2):
                z[p, ch, j, 0:N] = blank
                z[p, ch, j, 2 * N:] = blank
    gout[...] = gin[...]
    transforms(batch, offs, tiles, probe, amp, gout, z, a3r, b3l, a3l, b3r)
    if last:
        flat[...] = gout[...].reshape(TILES, 8, N)
    spots = []
    for p in range(POS):
        r0 = offs[1, 1, 0, batch * 8 + p * 2] + HALF
        c0 = offs[1, 1, 0, batch * 8 + p * 2 + 1] + HALF
        spots.append((p, r0, lax.shift_right_arithmetic(c0, 7)))
    greeted(sides, others)

    count = iter(range(100))

    def link(src, dst, to, source):
        i = next(count)
        return Link(src, dst, send.at[i], recv.at[i], to, source)

    def gathered(ch, i, k):
        acc = None
        for p, r0, t in spots:
            w = window(z.at[p, ch], r0, t, i, k)
            acc = w if acc is None else acc + w
        return acc

    lane = lanes((N, N))
    every = []
    cols = {}

    def send_cols(i):
        w = slice(i * N, i * N + N)
        t0 = [gathered(ch, i, 0) for ch in range(2)]
        t2 = [gathered(ch, i, 2) for ch in range(2)]
        ls[w] = jnp.where(lane < HALF, t0[0], turn(t0[1]))
        rs[w] = jnp.where(lane < HALF, turn(t2[0]), t2[1])
        for ch in range(2):
            me[1, ch, w] = jnp.where(lane < HALF, t2[ch], t0[ch])
        d = pl.ds(i * N, N)
        cols[i] = [link(ls.at[d], ls_in.at[d], left, right), link(rs.at[d], rs_in.at[d], right, left)]
        for c in cols[i]:
            c.start()
        every.extend(cols[i])

    def middle(i):
        for ch in range(2):
            me[0, ch, i * N:i * N + N] = gathered(ch, i, 1)

    def fold_cols(i):
        for c in cols[i]:
            c.arrived()
        w = slice(i * N, i * N + N)
        a, b = ls_in[w], rs_in[w]
        me[1, 0, w] += jnp.where(lane < HALF, a, turn(b))
        me[1, 1, w] += jnp.where(lane < HALF, turn(a), b)

    stage = iter(red.stages()) if last else iter([None] * 20)
    next(stage)
    send_cols(0)
    send_cols(2)
    middle(0)
    row_links = {}

    def rows_pair(which, top):
        if last:
            at = 0 if top else PADROWS - HALF
        else:
            at = 0 if top else PADROWS - N
        d = pl.ds(at, reach)
        if top:
            c = link(me.at[which, :, d, :], from_down.at[which], up, down)
        else:
            c = link(me.at[which, :, d, :], from_up.at[which], down, up)
        c.start()
        every.append(c)
        row_links[which, top] = c

    rows_pair(0, True)
    middle(2)
    rows_pair(0, False)
    send_cols(1)
    middle(1)
    if last:
        next(stage)
    light_maps(batch, offs, probe, zl, light)
    fold_cols(0)
    rows_pair(1, True)
    fold_cols(2)
    rows_pair(1, False)
    fold_cols(1)
    if last:
        next(stage)

    halos = []

    def update(which, at, size, extra):
        w = slice(at, at + size)
        lv = light[which, w]
        mine = lanes((size, N))
        for ch in range(2):
            t = me[which, ch, w]
            if extra is not None:
                t = t + extra[which, ch]
            old = tiles[ch, 1, w] if which == 0 else jnp.where(mine < HALF, tiles[ch, 2, w], tiles[ch, 0, w])
            fresh[which, ch, w] = old + t * lv

    def halo(at, size):
        w = slice(at, at + size)
        a, b = halo_strips(fresh[1, 0, w], fresh[1, 1, w])
        sl[w] = a
        sr[w] = b
        d = pl.ds(at, size)
        both = [link(sl.at[d], hr.at[d], left, right), link(sr.at[d], hl.at[d], right, left)]
        for c in both:
            c.start()
        halos.extend(both)

    update(1, N, N, None)
    if not last:
        halo(N, N)
    update(0, N, N, None)
    if last:
        next(stage)
    start = HALF if last else 0
    row_links[1, False].arrived()
    update(1, start, reach, from_up)
    if not last:
        halo(0, N)
    row_links[1, True].arrived()
    update(1, 2 * N, reach, from_down)
    if not last:
        halo(2 * N, N)
    row_links[0, False].arrived()
    update(0, start, reach, from_up)
    row_links[0, True].arrived()
    update(0, 2 * N, reach, from_down)
    every.extend(halos)
    if last:
        wide = lanes((TILE, N))
        w = slice(HALF, HALF + TILE)
        for ch in range(2):
            m, e = fresh[0, ch, w], fresh[1, ch, w]
            out[ch, :, 0:128] = turn(jnp.where(wide < HALF, m, e))
            out[ch, :, 128:256] = turn(jnp.where(wide < HALF, e, m))
        for _ in stage:
            pass
    else:
        for ch in range(2):
            out[ch, 1] = fresh[0, ch]
        for c in halos:
            c.arrived()
        finish_tiles(out, fresh, hl, hr)
    for c in every:
        c.sent()


def run_batch(batch, last, offs, tiles, probe, amp, gin, tabs):
    f = jnp.float32
    strip = pltpu.VMEM((PADROWS, N), f)
    sums = jax.ShapeDtypeStruct((2 * MODES + 1, N, N), f)
    reach = HALF if last else N
    if last:
        shapes = (jax.ShapeDtypeStruct((2, TILE, TILE), f), jax.ShapeDtypeStruct((128, 8, N), f))
        extra = [pltpu.VMEM((2 * MODES + 1, N, N), f), pltpu.VMEM((TILES, 8, N), f)]
    else:
        shapes = (jax.ShapeDtypeStruct((2, 3, PADROWS, N), f), sums)
        extra = []
    return pl.pallas_call(
        functools.partial(batch_kernel, batch, last),
        out_shape=shapes,
        in_specs=[SM] + [VM] * 8,
        out_specs=(VM,) * len(shapes),
        scratch_shapes=extra + [
            pltpu.VMEM((POS, 2, 2, PADROWS, N), f),
            pltpu.VMEM((3, PADROWS, N), f),
            pltpu.VMEM((2, PADROWS, N), f),
            strip, strip, strip, strip,
            pltpu.VMEM((2, 2, PADROWS, N), f),
            pltpu.VMEM((2, 2, PADROWS, N), f),
            pltpu.VMEM((2, 2, reach, N), f),
            pltpu.VMEM((2, 2, reach, N), f),
        ] + ([] if last else [strip] * 4) + [
            pltpu.SemaphoreType.DMA((16,)),
            pltpu.SemaphoreType.DMA((16,)),
        ] + (reduction_scratch() if last else []),
        compiler_params=pltpu.CompilerParams(
            collective_id=1 + batch, has_side_effects=True, vmem_limit_bytes=36 * 2**20),
        name=f"batch{batch}",
    )(offs, tiles, probe, amp, gin, *tabs)


def on_device(object_field, probe, amplitudes, offsets):
    mine = jnp.pad(offsets.reshape(1, 24), ((0, 7), (0, N - 24)))
    tabs = [jnp.asarray(t) for t in tables()]
    tiles, offs = run_first(object_field, mine)
    grads = jnp.zeros((2 * MODES + 1, N, N), jnp.float32)
    amps = amplitudes.reshape(BATCHES, POS, N, N)
    for b in range(BATCHES - 1):
        tiles, grads = run_batch(b, False, offs, tiles, probe, amps, grads, tabs)
    obj, step = run_batch(BATCHES - 1, True, offs, tiles, probe, amps, grads, tabs)
    return obj, step.reshape(2, MODES, N, N)


def solution(mesh):
    placed = (
        P(None, "row", "col"),
        P(),
        P("row", "col", None, None, None, None),
        P("row", "col", None, None, None),
    )
    return jax.shard_map(
        on_device,
        mesh=mesh,
        in_specs=placed,
        out_specs=(P(None, "row", "col"), P()),
        check_vma=False,
    )
```

```python
import functools
import math

import jax
import jax.numpy as jnp
import ml_dtypes
import numpy as np
from jax import lax
from jax.experimental import pallas as pl
from jax.experimental.pallas import tpu as pltpu
from jax.sharding import PartitionSpec as P

N = 128
MODES = 4
TILE = 256
POS = 4
BATCHES = 3
HALF = 64
PADROWS = 384
FAR = 100000

AMP_FLOOR = 0.25
OBJECT_REG = 0.5
PROBE_REG = 1.0

MESH = pl.DeviceIdType.MESH
VM = pl.BlockSpec(memory_space=pltpu.VMEM)
SM = pl.BlockSpec(memory_space=pltpu.SMEM)


def tables():
    k = np.arange(N)
    ang = (k[:, None] * k[None, :] % N) * (2.0 * math.pi / N)
    fr, fi = np.cos(ang) / math.sqrt(N), -np.sin(ang) / math.sqrt(N)
    a = np.block([[fr, fi], [-fi, fr]])
    b = np.block([[fr, -fi], [fi, fr]])

    def split(m):
        hi = m.astype(np.float32).astype(ml_dtypes.bfloat16)
        lo = (m - hi.astype(np.float64)).astype(np.float32).astype(ml_dtypes.bfloat16)
        return hi, lo

    ah, al = split(a)
    bh, bl = split(b)
    return ah, al, bh, bl


def lanes(shape):
    return lax.broadcasted_iota(jnp.int32, shape, 1)


def split_hi_lo(x):
    hi = x.astype(jnp.bfloat16)
    lo = (x - hi.astype(jnp.float32)).astype(jnp.bfloat16)
    return hi, lo


def dot(a, b):
    return jnp.dot(a, b, preferred_element_type=jnp.float32)


def right_mul(x, th, tl):
    hi, lo = split_hi_lo(x)
    return dot(jnp.concatenate([hi, lo, hi], axis=1), jnp.concatenate([th, th, tl], axis=0))


def left_mul(th, tl, x):
    hi, lo = split_hi_lo(x)
    return dot(jnp.concatenate([th, th, tl], axis=1), jnp.concatenate([hi, lo, hi], axis=0))


def position():
    row, col = lax.axis_index("row"), lax.axis_index("col")
    rows, cols = lax.axis_size("row"), lax.axis_size("col")
    up = (row > 0, {"row": jnp.maximum(row - 1, 0), "col": col})
    down = (row < rows - 1, {"row": jnp.minimum(row + 1, rows - 1), "col": col})
    left = (col > 0, {"row": row, "col": jnp.maximum(col - 1, 0)})
    right = (col < cols - 1, {"row": row, "col": jnp.minimum(col + 1, cols - 1)})
    return up, down, left, right


def greet(sides, others=()):
    barrier = pltpu.get_barrier_semaphore()
    for there, device in sides:
        @pl.when(there)
        def _(device=device):
            pl.semaphore_signal(barrier, inc=1, device_id=device, device_id_type=MESH)
    for device in others:
        pl.semaphore_signal(barrier, inc=1, device_id=device, device_id_type=MESH)


def greeted(sides, others=()):
    barrier = pltpu.get_barrier_semaphore()
    pl.semaphore_wait(barrier, sum(there.astype(jnp.int32) for there, _ in sides) + len(others))


class Link:
    def __init__(self, src, dst, send, recv, to, source):
        self.there, device = to
        self.source = source[0]
        self.copy = pltpu.make_async_remote_copy(
            src_ref=src, dst_ref=dst, send_sem=send, recv_sem=recv,
            device_id=device, device_id_type=MESH)

    def start(self):
        @pl.when(self.there)
        def _():
            self.copy.start()

    def arrived(self):
        @pl.when(self.source)
        def _():
            self.copy.wait_recv()

    def sent(self):
        @pl.when(self.there)
        def _():
            self.copy.wait_send()


def clear_missing(pairs):
    for there, ref in pairs:
        @pl.when(jnp.logical_not(there))
        def _(ref=ref):
            ref[...] = jnp.zeros(ref.shape, ref.dtype)


def turn(x):
    return pltpu.roll(x, HALF, 1)


def halo_strips(re, im):
    lane = lanes(re.shape)
    ti = turn(im)
    return jnp.where(lane < HALF, ti, re), jnp.where(lane < HALF, re, ti)


def first_kernel(obj_hbm, offs, *rest):
    far_refs, rest = rest[:6], rest[6:]
    out, offs_out, *near_refs = rest[:8]
    obj, me, sl, sr, hl, hr, table, send, recv, local = rest[8:]
    up, down, left, right = position()
    load = pltpu.make_async_copy(obj_hbm, obj, local.at[0])
    load.start()
    loads = [pltpu.make_async_copy(a, b, local.at[i + 1]) for i, (a, b) in enumerate(zip(far_refs, near_refs))]
    for c in loads:
        c.start()
    lane = lanes((TILE, N))
    table[...] = jnp.full(table.shape, FAR, jnp.int32)
    table[1, 1] = offs[...]
    clear_missing([(left[0], hl), (right[0], hr),
                   (up[0], me.at[:, :, pl.ds(0, HALF), :]),
                   (down[0], me.at[:, :, pl.ds(PADROWS - HALF, HALF), :])])
    greet((up, down, left, right))
    own = slice(HALF, HALF + TILE)
    load.wait()
    for ch in range(2):
        a, b = turn(obj[ch, :, 0:128]), turn(obj[ch, :, 128:256])
        me[1, ch, own] = jnp.where(lane < HALF, b, a)
        me[0, ch, own] = jnp.where(lane < HALF, a, b)
    greeted((up, down, left, right))

    count = iter(range(100))

    def link(src, dst, to, source):
        i = next(count)
        return Link(src, dst, send.at[i], recv.at[i], to, source)

    def rows(which):
        top, bottom = pl.ds(HALF, HALF), pl.ds(TILE, HALF)
        above, below = pl.ds(0, HALF), pl.ds(PADROWS - HALF, HALF)
        return [link(me.at[which, :, top, :], me.at[which, :, below, :], up, down),
                link(me.at[which, :, bottom, :], me.at[which, :, above, :], down, up)]

    def cols(at, size):
        w = slice(at, at + size)
        a, b = halo_strips(me[1, 0, w], me[1, 1, w])
        sl[w] = a
        sr[w] = b
        d = pl.ds(at, size)
        both = [link(sl.at[d], hr.at[d], left, right), link(sr.at[d], hl.at[d], right, left)]
        for c in both:
            c.start()
        return both

    tell = [link(table.at[1, 1], table.at[1, 2], up, down),
            link(table.at[1, 1], table.at[1, 0], down, up)]
    edge = rows(1)
    middle = rows(0)
    for c in tell + edge:
        c.start()
    late = cols(HALF, TILE)
    for c in middle:
        c.start()
    for c in tell:
        c.arrived()
    more = [link(table.at[1], table.at[2], left, right),
            link(table.at[1], table.at[0], right, left)]
    for c in more:
        c.start()
    late += more
    edge[1].arrived()
    late += cols(0, HALF)
    edge[0].arrived()
    late += cols(PADROWS - HALF, HALF)
    for c in middle:
        c.arrived()
    for ch in range(2):
        out[ch, 1] = me[0, ch]
    for c in late:
        c.arrived()
    finish_tiles(out, me, hl, hr)
    offs_out[...] = table[...]
    for c in loads:
        c.wait()
    for c in tell + edge + middle + late:
        c.sent()


def finish_tiles(out, me, hl, hr):
    wide = lanes((PADROWS, N))
    out[0, 0] = jnp.where(wide < HALF, hl[...], me[1, 0])
    out[1, 0] = jnp.where(wide < HALF, turn(hl[...]), me[1, 1])
    out[0, 2] = jnp.where(wide < HALF, me[1, 0], hr[...])
    out[1, 2] = jnp.where(wide < HALF, me[1, 1], turn(hr[...]))


def run_first(obj, offs, others):
    f = jnp.float32
    strip = pltpu.VMEM((PADROWS, N), f)
    hbm = pl.BlockSpec(memory_space=pltpu.HBM)
    return pl.pallas_call(
        first_kernel,
        out_shape=(
            jax.ShapeDtypeStruct((2, 3, PADROWS, N), f),
            jax.ShapeDtypeStruct((3, 3, 8, N), jnp.int32),
        ) + tuple(jax.ShapeDtypeStruct(a.shape, a.dtype) for a in others),
        in_specs=[hbm, VM] + [hbm] * 6,
        out_specs=(VM,) * 8,
        scratch_shapes=[
            pltpu.VMEM((2, TILE, TILE), f),
            pltpu.VMEM((2, 2, PADROWS, N), f),
            strip, strip, strip, strip,
            pltpu.VMEM((3, 3, 8, N), jnp.int32),
            pltpu.SemaphoreType.DMA((14,)),
            pltpu.SemaphoreType.DMA((14,)),
            pltpu.SemaphoreType.DMA((7,)),
        ],
        compiler_params=pltpu.CompilerParams(collective_id=0, has_side_effects=True, vmem_limit_bytes=14 * 2**20),
        name="first",
    )(obj, offs, *others)


def spread(dest, value, s):
    lane = lanes((N, N))
    turned = pltpu.roll(value, s, 1)
    dest[0, N:2 * N] = jnp.where(lane >= s, turned, 0.0)
    dest[1, N:2 * N] = jnp.where(lane < s, turned, 0.0)


def window(src, r0, t, i, k):
    j = k - t
    hit = (j == 0) | (j == 1)
    start = jnp.where(hit, jnp.clip(N + N * i - r0, 0, 2 * N), 0)
    return src[jnp.where(hit, j, 0), pl.ds(start, N)]


STATIC = ((0, 0, 0), (1, 2 * N, 2))
MOVING = (2, 3)


def spot(offs, block, batch, p):
    cr, rr = block
    r0 = offs[cr, rr, 0, batch * 8 + p * 2] + (rr - 1) * TILE + HALF
    c0 = offs[cr, rr, 0, batch * 8 + p * 2 + 1] + (cr - 1) * TILE + HALF
    return r0, lax.shift_right_arithmetic(c0, 7), lax.bitwise_and(c0, 127)


def terms(pr, pi, probe, measured, gout, gin, first, ah, al, bh, bl):
    waves = []
    for m in range(MODES):
        qr, qi = probe[0, m], probe[1, m]
        waves.append(jnp.concatenate([qr * pr - qi * pi, qr * pi + qi * pr], axis=1))
    half = right_mul(jnp.concatenate(waves, axis=0), ah[...], al[...])
    rows_of = [half[m * N:(m + 1) * N] for m in range(MODES)]
    stacked = jnp.concatenate(
        [jnp.concatenate([h[:, :N] for h in rows_of], axis=1),
         jnp.concatenate([h[:, N:] for h in rows_of], axis=1)], axis=0)
    far = left_mul(bh[...], bl[...], stacked)
    inten = jnp.zeros((N, N), jnp.float32)
    for m in range(MODES):
        fr, fi = far[:N, m * N:(m + 1) * N], far[N:, m * N:(m + 1) * N]
        inten += fr * fr + fi * fi
    factor = measured * lax.rsqrt(jnp.maximum(inten, AMP_FLOOR * AMP_FLOOR)) - 1.0
    factor = jnp.concatenate([factor] * MODES, axis=1)
    factor = jnp.concatenate([factor] * 2, axis=0)
    back_half = left_mul(ah[...], al[...], far * factor)
    lhs = jnp.concatenate(
        [jnp.concatenate([back_half[:N, m * N:(m + 1) * N], back_half[N:, m * N:(m + 1) * N]], axis=1)
         for m in range(MODES)], axis=0)
    change = right_mul(lhs, bh[...], bl[...])
    tr = jnp.zeros((N, N), jnp.float32)
    ti = jnp.zeros((N, N), jnp.float32)

    def accumulate(k, value):
        if not first:
            gout[k] += value
        elif gin is None:
            gout[k] = value
        else:
            gout[k] = gin[k] + value

    for m in range(MODES):
        qr, qi = probe[0, m], probe[1, m]
        cr, ci = change[m * N:(m + 1) * N, :N], change[m * N:(m + 1) * N, N:]
        tr += qr * cr + qi * ci
        ti += qr * ci - qi * cr
        accumulate(m, pr * cr + pi * ci)
        accumulate(MODES + m, pr * ci - pi * cr)
    accumulate(2 * MODES, pr * pr + pi * pi)
    return tr, ti


def transforms(batch, offs, tiles, probe, amp, gout, gin, z, fixed, tabs):
    lane = lanes((N, N))
    for p, at, t in STATIC:
        pr, pi = tiles[0, t, at:at + N], tiles[1, t, at:at + N]
        tr, ti = terms(pr, pi, probe, amp[batch, p], gout, gin, p == 0, *tabs)
        fixed[p, 0] = tr
        fixed[p, 1] = ti
    for n, p in enumerate(MOVING):
        r0, t, s = spot(offs, (1, 1), batch, p)
        rows = pl.ds(r0, N)
        back = lax.bitwise_and(128 - s, 127)
        after = jnp.minimum(t + 1, 2)

        def cut(ch):
            one = pltpu.roll(tiles[ch, t, rows], back, 1)
            two = pltpu.roll(tiles[ch, after, rows], back, 1)
            return jnp.where(lane < 128 - s, one, two)

        tr, ti = terms(cut(0), cut(1), probe, amp[batch, p], gout, gin, False, *tabs)
        spread(z.at[n, 0], tr, s)
        spread(z.at[n, 1], ti, s)


def light_maps(batch, offs, probe, zl, light):
    row, rows = lax.axis_index("row"), lax.axis_size("row")
    col, cols = lax.axis_index("col"), lax.axis_size("col")
    lane = lanes((N, N))
    total = jnp.zeros((N, N), jnp.float32)
    for m in range(MODES):
        total += probe[0, m] * probe[0, m] + probe[1, m] * probe[1, m]
    blank = jnp.zeros((N, N), jnp.float32)
    slots = zl.shape[0]
    for n in range(slots):
        for j in range(2):
            zl[n, j, 0:N] = blank
            zl[n, j, 2 * N:] = blank

    def there(yes):
        return yes.astype(jnp.float32)

    up, down, left, right = there(row > 0), there(row < rows - 1), there(col > 0), there(col < cols - 1)
    corner = {(0, 0): 1.0 + up * left, (0, 2): right + up, (2, 0): down + left, (2, 2): 1.0 + down * right}
    sums = {}
    for i in (0, 2):
        sums[i] = total * jnp.where(lane < HALF, corner[i, 2], corner[i, 0])
    light[1, 0:N] = sums[0]
    light[1, N:2 * N] = blank
    light[1, 2 * N:] = sums[2]
    for i in range(3):
        light[0, i * N:i * N + N] = blank

    n = 0
    for cr in range(3):
        for rr in range(3):
            for p in MOVING:
                r0, t, s = spot(offs, (cr, rr), batch, p)
                buf = zl.at[n % slots]
                n += 1
                spread(buf, total, s)
                for i in {0: (0,), 1: (0, 1, 2), 2: (2,)}[rr]:
                    w = slice(i * N, i * N + N)
                    if cr == 0:
                        light[1, w] += jnp.where(lane < HALF, 0.0, window(buf, r0, t, i, 0))
                    elif cr == 2:
                        light[1, w] += jnp.where(lane < HALF, window(buf, r0, t, i, 2), 0.0)
                    else:
                        light[0, w] += window(buf, r0, t, i, 1)
                        light[1, w] += jnp.where(lane < HALF, window(buf, r0, t, i, 2), window(buf, r0, t, i, 0))
    place = lax.broadcasted_iota(jnp.int32, (PADROWS, N), 0)
    low = jnp.where(row == 0, HALF, 0)
    high = jnp.where(row == rows - 1, HALF + TILE, PADROWS)
    inside = (place >= low) & (place < high)
    for j in range(2):
        light[j] = jnp.where(inside, 1.0 / (light[j] + OBJECT_REG), 0.0)


TILES = 144
HALFT = 72
PIECE = 9
SUB = 3


class Reduction:
    def __init__(self, g, out, r1, s1, r2, s2, r3, z, fin, ag1, ag2, ag3, send, recv):
        self.refs = (g, out, r1, s1, r2, s2, r3, z, fin, ag1, ag2, ag3)
        self.send, self.recv = send, recv
        self.count = iter(range(100))
        self.every = []
        row, col = lax.axis_index("row"), lax.axis_index("col")
        self.x, self.zh = row // 4, row % 4
        self.core, self.group = col % 2, col // 2
        self.row, self.col = row, col
        self.partner = {"row": row, "col": col + 1 - 2 * self.core}
        self.peers = [self.partner]
        self.peers += [self.group_dev(self.in_group(d)) for d in range(1, 8)]
        self.peers += [self.x_dev(d) for d in range(1, 4)]
        self.peers += [self.z_dev(d) for d in range(1, 4)]

    def in_group(self, d):
        return lax.rem(self.group + d, 8)

    def group_dev(self, k):
        return {"row": self.row, "col": k * 2 + self.core}

    def x_dev(self, d):
        return {"row": lax.rem(self.x + d, 4) * 4 + self.zh, "col": self.col}

    def z_dev(self, d):
        return {"row": self.x * 4 + lax.rem(self.zh + d, 4), "col": self.col}

    def go(self, src, dst, device):
        i = next(self.count)
        c = pltpu.make_async_remote_copy(
            src_ref=src, dst_ref=dst, send_sem=self.send.at[i], recv_sem=self.recv.at[i],
            device_id=device, device_id_type=MESH)
        c.start()
        self.every.append(c)
        return c

    def stages(self):
        g, out, r1, s1, r2, s2, r3, z, fin, ag1, ag2, ag3 = self.refs
        x, zh, core, group, go, in_group = self.x, self.zh, self.core, self.group, self.go, self.in_group
        s2[pl.ds(PIECE, 12 - PIECE)] = jnp.zeros((12 - PIECE, 8, N), jnp.float32)
        c = go(g.at[pl.ds((1 - core) * HALFT, HALFT)], r1, self.partner)
        yield
        c.wait_recv()
        s1[...] = g[pl.ds(core * HALFT, HALFT)] + r1[...]
        cs = [go(s1.at[pl.ds(in_group(d) * PIECE, PIECE)], r2.at[d - 1], self.group_dev(in_group(d))) for d in range(1, 8)]
        yield
        acc = s1[pl.ds(group * PIECE, PIECE)]
        for d, c in enumerate(cs):
            c.wait_recv()
            acc = acc + r2[d]
        s2[pl.ds(0, PIECE)] = acc
        cs = [go(s2.at[pl.ds(lax.rem(x + d, 4) * SUB, SUB)], r3.at[d - 1], self.x_dev(d)) for d in range(1, 4)]
        yield
        acc = s2[pl.ds(x * SUB, SUB)]
        for d, c in enumerate(cs):
            c.wait_recv()
            acc = acc + r3[d]
        z[0] = acc
        cs = [go(z.at[0], z.at[d], self.z_dev(d)) for d in range(1, 4)]
        yield
        for c in cs:
            c.wait_recv()
        acc = z[lax.rem(zh, 4)]
        for k in range(1, 4):
            acc = acc + z[lax.rem(zh - k + 4, 4)]
        fin[...] = acc
        cs = [go(fin, ag1.at[pl.ds(x * SUB, SUB)], self.x_dev(d)) for d in range(1, 4)]
        ag1[pl.ds(x * SUB, SUB)] = fin[...]
        yield
        for c in cs:
            c.wait_recv()
        cs = [go(ag1.at[pl.ds(0, PIECE)], ag2.at[pl.ds(group * PIECE, PIECE)], self.group_dev(in_group(d))) for d in range(1, 8)]
        ag2[pl.ds(group * PIECE, PIECE)] = ag1[pl.ds(0, PIECE)]
        yield
        for c in cs:
            c.wait_recv()
        c = go(ag2, ag3.at[pl.ds(core * HALFT, HALFT)], self.partner)
        ag3[pl.ds(core * HALFT, HALFT)] = ag2[...]
        yield
        c.wait_recv()
        inv = lax.rsqrt(ag3[pl.ds(128, 16)] + PROBE_REG)
        for k in range(8):
            out[pl.ds(16 * k, 16)] = ag3[pl.ds(16 * k, 16)] * inv
        for c in self.every:
            c.wait_send()
        yield


def reduction_scratch():
    f = jnp.float32
    shape = lambda *n: pltpu.VMEM(n + (8, N), f)
    return [shape(HALFT), shape(HALFT), shape(7, PIECE), shape(12), shape(3, SUB),
            shape(4, SUB), shape(SUB), shape(12), shape(HALFT), shape(TILES),
            pltpu.SemaphoreType.DMA((25,)), pltpu.SemaphoreType.DMA((25,))]


def batch_kernel(batch, last, offs, tiles, *rest):
    tabs, (amp, probe), rest = rest[:4], rest[4:6], rest[6:]
    gin = None
    if batch:
        gin, *rest = rest
    if last:
        out, step_out, gout, flat, z, fixed, zl, light, ls, rs, ls_in, rs_in, me, fresh, from_up, from_down, send, recv, *more = rest
        reach = HALF
        red = Reduction(flat, step_out, *more)
        others = red.peers
    else:
        out, gout, z, fixed, zl, light, ls, rs, ls_in, rs_in, me, fresh, from_up, from_down, sl, sr, hl, hr, send, recv = rest
        reach = N
        others = ()
    up, down, left, right = sides = position()
    clear_missing([(left[0], rs_in), (right[0], ls_in), (up[0], from_up), (down[0], from_down)])
    if not last:
        clear_missing([(left[0], hl), (right[0], hr)])
    greet(sides, others)

    blank = jnp.zeros((N, N), jnp.float32)
    for n in range(len(MOVING)):
        for ch in range(2):
            for j in range(2):
                z[n, ch, j, 0:N] = blank
                z[n, ch, j, 2 * N:] = blank
    transforms(batch, offs, tiles, probe, amp, gout, gin, z, fixed, tabs)
    if last:
        flat[...] = gout[...].reshape(TILES, 8, N)
    greeted(sides, others)

    count = iter(range(100))

    def link(src, dst, to, source):
        i = next(count)
        return Link(src, dst, send.at[i], recv.at[i], to, source)

    def gathered(ch, i, k):
        acc = None
        for n, p in enumerate(MOVING):
            r0, t, _ = spot(offs, (1, 1), batch, p)
            w = window(z.at[n, ch], r0, t, i, k)
            acc = w if acc is None else acc + w
        for p, at, tile in STATIC:
            if (at, tile) == (i * N, k):
                acc = acc + fixed[p, ch]
        return acc

    lane = lanes((N, N))
    every = []
    cols = {}

    def send_cols(i):
        w = slice(i * N, i * N + N)
        t0 = [gathered(ch, i, 0) for ch in range(2)]
        t2 = [gathered(ch, i, 2) for ch in range(2)]
        ls[w] = jnp.where(lane < HALF, t0[0], turn(t0[1]))
        rs[w] = jnp.where(lane < HALF, turn(t2[0]), t2[1])
        for ch in range(2):
            me[1, ch, w] = jnp.where(lane < HALF, t2[ch], t0[ch])
        d = pl.ds(i * N, N)
        cols[i] = [link(ls.at[d], ls_in.at[d], left, right), link(rs.at[d], rs_in.at[d], right, left)]
        for c in cols[i]:
            c.start()
        every.extend(cols[i])

    def middle(i):
        for ch in range(2):
            me[0, ch, i * N:i * N + N] = gathered(ch, i, 1)

    def fold_cols(i):
        for c in cols[i]:
            c.arrived()
        w = slice(i * N, i * N + N)
        a, b = ls_in[w], rs_in[w]
        me[1, 0, w] += jnp.where(lane < HALF, a, turn(b))
        me[1, 1, w] += jnp.where(lane < HALF, turn(a), b)

    stage = iter(red.stages()) if last else iter([None] * 20)
    next(stage)
    send_cols(0)
    send_cols(2)
    middle(0)
    row_links = {}

    def rows_pair(which, top):
        if last:
            at = 0 if top else PADROWS - HALF
        else:
            at = 0 if top else PADROWS - N
        d = pl.ds(at, reach)
        if top:
            c = link(me.at[which, :, d, :], from_down.at[which], up, down)
        else:
            c = link(me.at[which, :, d, :], from_up.at[which], down, up)
        c.start()
        every.append(c)
        row_links[which, top] = c

    rows_pair(0, True)
    middle(2)
    rows_pair(0, False)
    send_cols(1)
    middle(1)
    if last:
        next(stage)
    light_maps(batch, offs, probe, zl, light)
    fold_cols(0)
    rows_pair(1, True)
    fold_cols(2)
    rows_pair(1, False)
    fold_cols(1)
    if last:
        next(stage)

    halos = []

    def update(which, at, size, extra):
        w = slice(at, at + size)
        lv = light[which, w]
        mine = lanes((size, N))
        for ch in range(2):
            t = me[which, ch, w]
            if extra is not None:
                t = t + extra[which, ch]
            old = tiles[ch, 1, w] if which == 0 else jnp.where(mine < HALF, tiles[ch, 2, w], tiles[ch, 0, w])
            fresh[which, ch, w] = old + t * lv

    def halo(at, size):
        w = slice(at, at + size)
        a, b = halo_strips(fresh[1, 0, w], fresh[1, 1, w])
        sl[w] = a
        sr[w] = b
        d = pl.ds(at, size)
        both = [link(sl.at[d], hr.at[d], left, right), link(sr.at[d], hl.at[d], right, left)]
        for c in both:
            c.start()
        halos.extend(both)

    update(1, N, N, None)
    if not last:
        halo(N, N)
    update(0, N, N, None)
    if last:
        next(stage)
    start = HALF if last else 0
    row_links[1, False].arrived()
    update(1, start, reach, from_up)
    if not last:
        halo(0, N)
    row_links[1, True].arrived()
    update(1, 2 * N, reach, from_down)
    if not last:
        halo(2 * N, N)
    row_links[0, False].arrived()
    update(0, start, reach, from_up)
    row_links[0, True].arrived()
    update(0, 2 * N, reach, from_down)
    every.extend(halos)
    if last:
        wide = lanes((TILE, N))
        w = slice(HALF, HALF + TILE)
        for ch in range(2):
            m, e = fresh[0, ch, w], fresh[1, ch, w]
            out[ch, :, 0:128] = turn(jnp.where(wide < HALF, m, e))
            out[ch, :, 128:256] = turn(jnp.where(wide < HALF, e, m))
        for _ in stage:
            pass
    else:
        for ch in range(2):
            out[ch, 1] = fresh[0, ch]
        for c in halos:
            c.arrived()
        finish_tiles(out, fresh, hl, hr)
    for c in every:
        c.sent()


def run_batch(batch, last, offs, tiles, others, gin):
    f = jnp.float32
    strip = pltpu.VMEM((PADROWS, N), f)
    sums = jax.ShapeDtypeStruct((2 * MODES + 1, N, N), f)
    reach = HALF if last else N
    if last:
        shapes = (jax.ShapeDtypeStruct((2, TILE, TILE), f), jax.ShapeDtypeStruct((128, 8, N), f))
        extra = [pltpu.VMEM((2 * MODES + 1, N, N), f), pltpu.VMEM((TILES, 8, N), f)]
    else:
        shapes = (jax.ShapeDtypeStruct((2, 3, PADROWS, N), f), sums)
        extra = []
    return pl.pallas_call(
        functools.partial(batch_kernel, batch, last),
        out_shape=shapes,
        in_specs=[SM] + [VM] * (1 + len(others) + len(gin)),
        out_specs=(VM,) * len(shapes),
        scratch_shapes=extra + [
            pltpu.VMEM((len(MOVING), 2, 2, PADROWS, N), f),
            pltpu.VMEM((len(STATIC), 2, N, N), f),
            pltpu.VMEM((3, 2, PADROWS, N), f),
            pltpu.VMEM((2, PADROWS, N), f),
            strip, strip, strip, strip,
            pltpu.VMEM((2, 2, PADROWS, N), f),
            pltpu.VMEM((2, 2, PADROWS, N), f),
            pltpu.VMEM((2, 2, reach, N), f),
            pltpu.VMEM((2, 2, reach, N), f),
        ] + ([] if last else [strip] * 4) + [
            pltpu.SemaphoreType.DMA((16,)),
            pltpu.SemaphoreType.DMA((16,)),
        ] + (reduction_scratch() if last else []),
        compiler_params=pltpu.CompilerParams(
            collective_id=1 + batch, has_side_effects=True, vmem_limit_bytes=36 * 2**20),
        name=f"batch{batch}",
    )(offs, tiles, *others, *gin)


def on_device(object_field, probe, amplitudes, offsets):
    mine = jnp.pad(offsets.reshape(1, 24), ((0, 7), (0, N - 24)))
    amps = amplitudes.reshape(BATCHES, POS, N, N)
    tabs = [jnp.asarray(t) for t in tables()]
    keep = lambda a: pltpu.with_memory_space_constraint(a, pltpu.HBM)
    tiles, offs, *others = run_first(keep(object_field), mine, [keep(a) for a in (*tabs, amps, probe)])
    grads = ()
    for b in range(BATCHES - 1):
        tiles, sums = run_batch(b, False, offs, tiles, others, grads)
        grads = (sums,)
    obj, step = run_batch(BATCHES - 1, True, offs, tiles, others, grads)
    return obj, step.reshape(2, MODES, N, N)


def solution(mesh):
    placed = (
        P(None, "row", "col"),
        P(),
        P("row", "col", None, None, None, None),
        P("row", "col", None, None, None),
    )
    return jax.shard_map(
        on_device,
        mesh=mesh,
        in_specs=placed,
        out_specs=(P(None, "row", "col"), P()),
        check_vma=False,
    )
```

```python
import functools
import math

import jax
import jax.numpy as jnp
import ml_dtypes
import numpy as np
from jax import lax
from jax.experimental import pallas as pl
from jax.experimental.pallas import tpu as pltpu
from jax.sharding import PartitionSpec as P

N = 128
MODES = 4
TILE = 256
POS = 4
BATCHES = 3
HALF = 64
PADROWS = 384
FAR = 100000

AMP_FLOOR = 0.25
OBJECT_REG = 0.5
PROBE_REG = 1.0

MESH = pl.DeviceIdType.MESH
VM = pl.BlockSpec(memory_space=pltpu.VMEM)
SM = pl.BlockSpec(memory_space=pltpu.SMEM)


def tables():
    k = np.arange(N)
    ang = (k[:, None] * k[None, :] % N) * (2.0 * math.pi / N)
    fr, fi = np.cos(ang) / math.sqrt(N), -np.sin(ang) / math.sqrt(N)
    a = np.block([[fr, fi], [-fi, fr]])
    b = np.block([[fr, -fi], [fi, fr]])

    def split(m):
        hi = m.astype(np.float32).astype(ml_dtypes.bfloat16)
        lo = (m - hi.astype(np.float64)).astype(np.float32).astype(ml_dtypes.bfloat16)
        return hi, lo

    ah, al = split(a)
    bh, bl = split(b)
    return ah, al, bh, bl


def lanes(shape):
    return lax.broadcasted_iota(jnp.int32, shape, 1)


def split_hi_lo(x):
    hi = x.astype(jnp.bfloat16)
    lo = (x - hi.astype(jnp.float32)).astype(jnp.bfloat16)
    return hi, lo


def dot(a, b):
    return jnp.dot(a, b, preferred_element_type=jnp.float32)


def right_mul(x, th, tl):
    hi, lo = split_hi_lo(x)
    return dot(jnp.concatenate([hi, lo, hi], axis=1), jnp.concatenate([th, th, tl], axis=0))


def left_mul(th, tl, x):
    hi, lo = split_hi_lo(x)
    return dot(jnp.concatenate([th, th, tl], axis=1), jnp.concatenate([hi, lo, hi], axis=0))


def position():
    row, col = lax.axis_index("row"), lax.axis_index("col")
    rows, cols = lax.axis_size("row"), lax.axis_size("col")
    up = (row > 0, {"row": jnp.maximum(row - 1, 0), "col": col})
    down = (row < rows - 1, {"row": jnp.minimum(row + 1, rows - 1), "col": col})
    left = (col > 0, {"row": row, "col": jnp.maximum(col - 1, 0)})
    right = (col < cols - 1, {"row": row, "col": jnp.minimum(col + 1, cols - 1)})
    return up, down, left, right


def greet(sides, others=()):
    barrier = pltpu.get_barrier_semaphore()
    for there, device in sides:
        @pl.when(there)
        def _(device=device):
            pl.semaphore_signal(barrier, inc=1, device_id=device, device_id_type=MESH)
    for device in others:
        pl.semaphore_signal(barrier, inc=1, device_id=device, device_id_type=MESH)


def greeted(sides, others=()):
    barrier = pltpu.get_barrier_semaphore()
    pl.semaphore_wait(barrier, sum(there.astype(jnp.int32) for there, _ in sides) + len(others))


class Link:
    def __init__(self, src, dst, send, recv, to, source):
        self.there, device = to
        self.source = source[0]
        self.copy = pltpu.make_async_remote_copy(
            src_ref=src, dst_ref=dst, send_sem=send, recv_sem=recv,
            device_id=device, device_id_type=MESH)

    def start(self):
        @pl.when(self.there)
        def _():
            self.copy.start()

    def arrived(self):
        @pl.when(self.source)
        def _():
            self.copy.wait_recv()

    def sent(self):
        @pl.when(self.there)
        def _():
            self.copy.wait_send()


def clear_missing(pairs):
    for there, ref in pairs:
        @pl.when(jnp.logical_not(there))
        def _(ref=ref):
            ref[...] = jnp.zeros(ref.shape, ref.dtype)


def turn(x):
    return pltpu.roll(x, HALF, 1)


def halo_strips(re, im):
    lane = lanes(re.shape)
    ti = turn(im)
    return jnp.where(lane < HALF, ti, re), jnp.where(lane < HALF, re, ti)


def first_kernel(obj_hbm, offs, *rest):
    far_refs, rest = rest[:6], rest[6:]
    out, offs_out, *near_refs = rest[:8]
    obj, me, sl, sr, hl, hr, table, send, recv, local = rest[8:]
    up, down, left, right = position()
    load = pltpu.make_async_copy(obj_hbm, obj, local.at[0])
    load.start()
    loads = [pltpu.make_async_copy(a, b, local.at[i + 1]) for i, (a, b) in enumerate(zip(far_refs, near_refs))]
    for c in loads:
        c.start()
    lane = lanes((TILE, N))
    table[...] = jnp.full(table.shape, FAR, jnp.int32)
    table[1, 1] = offs[...]
    clear_missing([(left[0], hl), (right[0], hr),
                   (up[0], me.at[:, :, pl.ds(0, HALF), :]),
                   (down[0], me.at[:, :, pl.ds(PADROWS - HALF, HALF), :])])
    greet((up, down, left, right))
    own = slice(HALF, HALF + TILE)
    load.wait()
    for ch in range(2):
        a, b = turn(obj[ch, :, 0:128]), turn(obj[ch, :, 128:256])
        me[1, ch, own] = jnp.where(lane < HALF, b, a)
        me[0, ch, own] = jnp.where(lane < HALF, a, b)
    greeted((up, down, left, right))

    count = iter(range(100))

    def link(src, dst, to, source):
        i = next(count)
        return Link(src, dst, send.at[i], recv.at[i], to, source)

    def rows(which):
        top, bottom = pl.ds(HALF, HALF), pl.ds(TILE, HALF)
        above, below = pl.ds(0, HALF), pl.ds(PADROWS - HALF, HALF)
        return [link(me.at[which, :, top, :], me.at[which, :, below, :], up, down),
                link(me.at[which, :, bottom, :], me.at[which, :, above, :], down, up)]

    def cols(at, size):
        w = slice(at, at + size)
        a, b = halo_strips(me[1, 0, w], me[1, 1, w])
        sl[w] = a
        sr[w] = b
        d = pl.ds(at, size)
        both = [link(sl.at[d], hr.at[d], left, right), link(sr.at[d], hl.at[d], right, left)]
        for c in both:
            c.start()
        return both

    tell = [link(table.at[1, 1], table.at[1, 2], up, down),
            link(table.at[1, 1], table.at[1, 0], down, up)]
    edge = rows(1)
    middle = rows(0)
    for c in tell + edge:
        c.start()
    late = cols(HALF, TILE)
    for c in middle:
        c.start()
    for c in tell:
        c.arrived()
    more = [link(table.at[1], table.at[2], left, right),
            link(table.at[1], table.at[0], right, left)]
    for c in more:
        c.start()
    late += more
    edge[1].arrived()
    late += cols(0, HALF)
    edge[0].arrived()
    late += cols(PADROWS - HALF, HALF)
    for c in middle:
        c.arrived()
    for ch in range(2):
        out[ch, 1] = me[0, ch]
    for c in late:
        c.arrived()
    finish_tiles(out, me, hl, hr)
    offs_out[...] = table[...]
    for c in loads:
        c.wait()
    for c in tell + edge + middle + late:
        c.sent()


def finish_tiles(out, me, hl, hr):
    wide = lanes((PADROWS, N))
    out[0, 0] = jnp.where(wide < HALF, hl[...], me[1, 0])
    out[1, 0] = jnp.where(wide < HALF, turn(hl[...]), me[1, 1])
    out[0, 2] = jnp.where(wide < HALF, me[1, 0], hr[...])
    out[1, 2] = jnp.where(wide < HALF, me[1, 1], turn(hr[...]))


def run_first(obj, offs, others):
    f = jnp.float32
    strip = pltpu.VMEM((PADROWS, N), f)
    hbm = pl.BlockSpec(memory_space=pltpu.HBM)
    return pl.pallas_call(
        first_kernel,
        out_shape=(
            jax.ShapeDtypeStruct((2, 3, PADROWS, N), f),
            jax.ShapeDtypeStruct((3, 3, 8, N), jnp.int32),
        ) + tuple(jax.ShapeDtypeStruct(a.shape, a.dtype) for a in others),
        in_specs=[hbm, VM] + [hbm] * 6,
        out_specs=(VM,) * 8,
        scratch_shapes=[
            pltpu.VMEM((2, TILE, TILE), f),
            pltpu.VMEM((2, 2, PADROWS, N), f),
            strip, strip, strip, strip,
            pltpu.VMEM((3, 3, 8, N), jnp.int32),
            pltpu.SemaphoreType.DMA((14,)),
            pltpu.SemaphoreType.DMA((14,)),
            pltpu.SemaphoreType.DMA((7,)),
        ],
        compiler_params=pltpu.CompilerParams(collective_id=0, has_side_effects=True, vmem_limit_bytes=14 * 2**20),
        name="first",
    )(obj, offs, *others)


def spread(dest, value, s):
    lane = lanes((N, N))
    turned = pltpu.roll(value, s, 1)
    dest[0, N:2 * N] = jnp.where(lane >= s, turned, 0.0)
    dest[1, N:2 * N] = jnp.where(lane < s, turned, 0.0)


def window(src, r0, t, i, k):
    j = k - t
    hit = (j == 0) | (j == 1)
    start = jnp.where(hit, jnp.clip(N + N * i - r0, 0, 2 * N), 0)
    return src[jnp.where(hit, j, 0), pl.ds(start, N)]


STATIC = ((0, 0, 0), (1, 2 * N, 2))
MOVING = (2, 3)


def spot(offs, block, batch, p):
    cr, rr = block
    r0 = offs[cr, rr, 0, batch * 8 + p * 2] + (rr - 1) * TILE + HALF
    c0 = offs[cr, rr, 0, batch * 8 + p * 2 + 1] + (cr - 1) * TILE + HALF
    return r0, lax.shift_right_arithmetic(c0, 7), lax.bitwise_and(c0, 127)


def terms(pr, pi, probe, measured, gout, gin, first, ah, al, bh, bl):
    waves = []
    for m in range(MODES):
        qr, qi = probe[0, m], probe[1, m]
        waves.append(jnp.concatenate([qr * pr - qi * pi, qr * pi + qi * pr], axis=1))
    half = right_mul(jnp.concatenate(waves, axis=0), ah[...], al[...])
    rows_of = [half[m * N:(m + 1) * N] for m in range(MODES)]
    stacked = jnp.concatenate(
        [jnp.concatenate([h[:, :N] for h in rows_of], axis=1),
         jnp.concatenate([h[:, N:] for h in rows_of], axis=1)], axis=0)
    far = left_mul(bh[...], bl[...], stacked)
    inten = jnp.zeros((N, N), jnp.float32)
    for m in range(MODES):
        fr, fi = far[:N, m * N:(m + 1) * N], far[N:, m * N:(m + 1) * N]
        inten += fr * fr + fi * fi
    factor = measured * lax.rsqrt(jnp.maximum(inten, AMP_FLOOR * AMP_FLOOR)) - 1.0
    factor = jnp.concatenate([factor] * MODES, axis=1)
    factor = jnp.concatenate([factor] * 2, axis=0)
    back_half = left_mul(ah[...], al[...], far * factor)
    lhs = jnp.concatenate(
        [jnp.concatenate([back_half[:N, m * N:(m + 1) * N], back_half[N:, m * N:(m + 1) * N]], axis=1)
         for m in range(MODES)], axis=0)
    change = right_mul(lhs, bh[...], bl[...])
    tr = jnp.zeros((N, N), jnp.float32)
    ti = jnp.zeros((N, N), jnp.float32)

    def accumulate(k, value):
        if not first:
            gout[k] += value
        elif gin is None:
            gout[k] = value
        else:
            gout[k] = gin[k] + value

    for m in range(MODES):
        qr, qi = probe[0, m], probe[1, m]
        cr, ci = change[m * N:(m + 1) * N, :N], change[m * N:(m + 1) * N, N:]
        tr += qr * cr + qi * ci
        ti += qr * ci - qi * cr
        accumulate(m, pr * cr + pi * ci)
        accumulate(MODES + m, pr * ci - pi * cr)
    accumulate(2 * MODES, pr * pr + pi * pi)
    return tr, ti


def moving_terms(batch, offs, tiles, probe, amp, gout, gin, z, tabs):
    lane = lanes((N, N))
    for n, p in enumerate(MOVING):
        r0, t, s = spot(offs, (1, 1), batch, p)
        rows = pl.ds(r0, N)
        back = lax.bitwise_and(128 - s, 127)
        after = jnp.minimum(t + 1, 2)

        def cut(ch):
            one = pltpu.roll(tiles[ch, t, rows], back, 1)
            two = pltpu.roll(tiles[ch, after, rows], back, 1)
            return jnp.where(lane < 128 - s, one, two)

        tr, ti = terms(cut(0), cut(1), probe, amp[batch, p], gout, gin, n == 0, *tabs)
        spread(z.at[n, 0], tr, s)
        spread(z.at[n, 1], ti, s)


def static_terms(batch, tiles, probe, amp, gout, fixed, tabs):
    for p, at, t in STATIC:
        pr, pi = tiles[0, t, at:at + N], tiles[1, t, at:at + N]
        tr, ti = terms(pr, pi, probe, amp[batch, p], gout, None, False, *tabs)
        fixed[p, 0] = tr
        fixed[p, 1] = ti


def light_maps(batch, offs, probe, zl, light):
    row, rows = lax.axis_index("row"), lax.axis_size("row")
    col, cols = lax.axis_index("col"), lax.axis_size("col")
    lane = lanes((N, N))
    total = jnp.zeros((N, N), jnp.float32)
    for m in range(MODES):
        total += probe[0, m] * probe[0, m] + probe[1, m] * probe[1, m]
    blank = jnp.zeros((N, N), jnp.float32)
    slots = zl.shape[0]
    for n in range(slots):
        for j in range(2):
            zl[n, j, 0:N] = blank
            zl[n, j, 2 * N:] = blank

    def there(yes):
        return yes.astype(jnp.float32)

    up, down, left, right = there(row > 0), there(row < rows - 1), there(col > 0), there(col < cols - 1)
    corner = {(0, 0): 1.0 + up * left, (0, 2): right + up, (2, 0): down + left, (2, 2): 1.0 + down * right}
    sums = {}
    for i in (0, 2):
        sums[i] = total * jnp.where(lane < HALF, corner[i, 2], corner[i, 0])
    light[1, 0:N] = sums[0]
    light[1, N:2 * N] = blank
    light[1, 2 * N:] = sums[2]
    for i in range(3):
        light[0, i * N:i * N + N] = blank

    n = 0
    for cr in range(3):
        for rr in range(3):
            for p in MOVING:
                r0, t, s = spot(offs, (cr, rr), batch, p)
                buf = zl.at[n % slots]
                n += 1
                spread(buf, total, s)
                for i in {0: (0,), 1: (0, 1, 2), 2: (2,)}[rr]:
                    w = slice(i * N, i * N + N)
                    if cr == 0:
                        light[1, w] += jnp.where(lane < HALF, 0.0, window(buf, r0, t, i, 0))
                    elif cr == 2:
                        light[1, w] += jnp.where(lane < HALF, window(buf, r0, t, i, 2), 0.0)
                    else:
                        light[0, w] += window(buf, r0, t, i, 1)
                        light[1, w] += jnp.where(lane < HALF, window(buf, r0, t, i, 2), window(buf, r0, t, i, 0))
    place = lax.broadcasted_iota(jnp.int32, (PADROWS, N), 0)
    low = jnp.where(row == 0, HALF, 0)
    high = jnp.where(row == rows - 1, HALF + TILE, PADROWS)
    inside = (place >= low) & (place < high)
    for j in range(2):
        light[j] = jnp.where(inside, 1.0 / (light[j] + OBJECT_REG), 0.0)


TILES = 144
HALFT = 72
PART = 36
SPLITS = (("group", 8, 5, "x", 4, 2), ("x", 4, 9, "group", 8, 2))


class Mates:
    def __init__(self):
        self.row, self.col = lax.axis_index("row"), lax.axis_index("col")
        self.x, self.zh = self.row // 4, self.row % 4
        self.core, self.group = self.col % 2, self.col // 2
        self.partner = {"row": self.row, "col": self.col + 1 - 2 * self.core}

    def at(self, axis, d):
        if axis == "group":
            k = lax.rem(self.group + d, 8)
            return k, {"row": self.row, "col": k * 2 + self.core}
        if axis == "x":
            k = lax.rem(self.x + d, 4)
            return k, {"row": k * 4 + self.zh, "col": self.col}
        k = lax.rem(self.zh + d, 4)
        return k, {"row": self.x * 4 + k, "col": self.col}

    def everyone(self):
        return ([self.partner] + [self.at("group", d)[1] for d in range(1, 8)]
                + [self.at("x", d)[1] for d in range(1, 4)] + [self.at("z", d)[1] for d in range(1, 4)])


def reduce_part(part, mates, g, whole, bufs):
    axis1, n1, p1, axis2, n2, p2 = SPLITS[part]
    r1, s1, r2, s2, r3, z, fin, ag1, ag2, send, recv = bufs
    count = iter(range(100))
    every = []

    def go(src, dst, device):
        i = next(count)
        c = pltpu.make_async_remote_copy(
            src_ref=src, dst_ref=dst, send_sem=send.at[i], recv_sem=recv.at[i],
            device_id=device, device_id_type=MESH)
        c.start()
        every.append(c)
        return c

    def scatter(src, slots, axis, n, p):
        cs = []
        for d in range(1, n):
            k, device = mates.at(axis, d)
            cs.append(go(src.at[pl.ds(k * p, p)], slots.at[d - 1], device))
        return cs

    def collect(src, slots, axis, p, cs):
        acc = src[pl.ds(mates.at(axis, 0)[0] * p, p)]
        for d, c in enumerate(cs):
            c.wait_recv()
            acc = acc + slots[d]
        return acc

    def gather(src, dst, axis, n, p):
        me = pl.ds(mates.at(axis, 0)[0] * p, p)
        cs = [go(src, dst.at[me], mates.at(axis, d)[1]) for d in range(1, n)]
        dst[me] = src[...]
        return cs

    core = mates.core
    if s1.shape[0] > PART:
        s1[pl.ds(PART, s1.shape[0] - PART)] = jnp.zeros((s1.shape[0] - PART, 8, N), jnp.float32)
    s2[pl.ds(p1, s2.shape[0] - p1)] = jnp.zeros((s2.shape[0] - p1, 8, N), jnp.float32)
    c = go(g.at[pl.ds((1 - core) * HALFT + part * PART, PART)], r1, mates.partner)
    yield
    c.wait_recv()
    s1[pl.ds(0, PART)] = g[pl.ds(core * HALFT + part * PART, PART)] + r1[...]
    cs = scatter(s1, r2, axis1, n1, p1)
    yield
    s2[pl.ds(0, p1)] = collect(s1, r2, axis1, p1, cs)
    cs = scatter(s2, r3, axis2, n2, p2)
    yield
    z[0] = collect(s2, r3, axis2, p2, cs)
    cs = [go(z.at[0], z.at[d], mates.at("z", d)[1]) for d in range(1, 4)]
    yield
    for c in cs:
        c.wait_recv()
    acc = z[lax.rem(mates.zh, 4)]
    for k in range(1, 4):
        acc = acc + z[lax.rem(mates.zh - k + 4, 4)]
    fin[...] = acc
    cs = gather(fin, ag1, axis2, n2, p2)
    yield
    for c in cs:
        c.wait_recv()
    cs = gather(ag1.at[pl.ds(0, p1)], ag2, axis1, n1, p1)
    yield
    for c in cs:
        c.wait_recv()
    mine = pl.ds(core * HALFT + part * PART, PART)
    c = go(ag2.at[pl.ds(0, PART)], whole.at[mine], mates.partner)
    whole[mine] = ag2[pl.ds(0, PART)]
    yield
    c.wait_recv()
    for c in every:
        c.wait_send()
    yield


PART_REFS = 11


def reduction_scratch():
    f = jnp.float32
    shape = lambda *n: pltpu.VMEM(n + (8, N), f)
    refs = [shape(TILES)]
    for _, n1, p1, _, n2, p2 in SPLITS:
        refs += [shape(PART), shape(n1 * p1), shape(n1 - 1, p1), shape(n2 * p2), shape(n2 - 1, p2),
                 shape(4, p2), shape(p2), shape(n2 * p2), shape(n1 * p1),
                 pltpu.SemaphoreType.DMA((25,)), pltpu.SemaphoreType.DMA((25,))]
    return refs


def batch_kernel(batch, last, offs, tiles, *rest):
    tabs, (amp, probe), rest = rest[:4], rest[4:6], rest[6:]
    gin = None
    if batch:
        gin, *rest = rest
    others, parts = (), ()
    if last:
        out, step_out, gout, flat, z, fixed, zl, light, ls, rs, ls_in, rs_in, me, fresh, from_up, from_down, send, recv, whole, *more = rest
        mates = Mates()
        others = mates.everyone()
        parts = [reduce_part(k, mates, flat, whole, more[k * PART_REFS:(k + 1) * PART_REFS]) for k in range(2)]
        reach = HALF
    else:
        out, gout, z, fixed, zl, light, ls, rs, ls_in, rs_in, me, fresh, from_up, from_down, sl, sr, hl, hr, send, recv = rest
        reach = N
    up, down, left, right = sides = position()
    clear_missing([(left[0], rs_in), (right[0], ls_in), (up[0], from_up), (down[0], from_down)])
    if not last:
        clear_missing([(left[0], hl), (right[0], hr)])
    greet(sides, others)

    def advance():
        for part in parts:
            next(part)

    blank = jnp.zeros((N, N), jnp.float32)
    for n in range(len(MOVING)):
        for ch in range(2):
            for j in range(2):
                z[n, ch, j, 0:N] = blank
                z[n, ch, j, 2 * N:] = blank
    moving_terms(batch, offs, tiles, probe, amp, gout, gin, z, tabs)
    greeted(sides, others)

    count = iter(range(100))
    every = []

    def link(src, dst, to, source):
        i = next(count)
        c = Link(src, dst, send.at[i], recv.at[i], to, source)
        c.start()
        every.append(c)
        return c

    def gathered(ch, i, k):
        acc = None
        for n, p in enumerate(MOVING):
            r0, t, _ = spot(offs, (1, 1), batch, p)
            w = window(z.at[n, ch], r0, t, i, k)
            acc = w if acc is None else acc + w
        for p, at, tile in STATIC:
            if (at, tile) == (i * N, k):
                acc = acc + fixed[p, ch]
        return acc

    lane = lanes((N, N))
    cols = {}
    row_links = {}

    def side_strips(i):
        w = slice(i * N, i * N + N)
        t0 = [gathered(ch, i, 0) for ch in range(2)]
        t2 = [gathered(ch, i, 2) for ch in range(2)]
        ls[w] = jnp.where(lane < HALF, t0[0], turn(t0[1]))
        rs[w] = jnp.where(lane < HALF, turn(t2[0]), t2[1])
        for ch in range(2):
            me[1, ch, w] = jnp.where(lane < HALF, t2[ch], t0[ch])

    def send_cols(at, size):
        d = pl.ds(at, size)
        cols[at] = [link(ls.at[d], ls_in.at[d], left, right), link(rs.at[d], rs_in.at[d], right, left)]

    def middle(i):
        for ch in range(2):
            me[0, ch, i * N:i * N + N] = gathered(ch, i, 1)

    def send_rows(which, top, at, size):
        base = 0 if top else PADROWS - reach
        src, dst = pl.ds(at, size), pl.ds(at - base, size)
        if top:
            c = link(me.at[which, :, src, :], from_down.at[which, :, dst, :], up, down)
        else:
            c = link(me.at[which, :, src, :], from_up.at[which, :, dst, :], down, up)
        row_links[which, top, at - base] = c

    def fold_cols(at, size):
        for c in cols[at]:
            c.arrived()
        w = slice(at, at + size)
        side = lanes((size, N))
        a, b = ls_in[w], rs_in[w]
        me[1, 0, w] += jnp.where(side < HALF, a, turn(b))
        me[1, 1, w] += jnp.where(side < HALF, turn(a), b)

    middle(0)
    send_rows(0, True, 0, reach)
    middle(2)
    send_rows(0, False, PADROWS - reach, reach)
    side_strips(1)
    send_cols(N, N)
    static_terms(batch, tiles, probe, amp, gout, fixed, tabs)
    if last:
        flat[...] = gout[...].reshape(TILES, 8, N)
    advance()
    order = ((0, True), (320, False), (64, True), (256, False))
    for i in (0, 2):
        side_strips(i)
        if i == 0:
            send_cols(0, HALF)
    send_cols(320, HALF)
    send_cols(64, HALF)
    send_cols(256, HALF)
    advance()
    middle(1)
    light_maps(batch, offs, probe, zl, light)
    for at, top in order:
        fold_cols(at, HALF)
        if not last or at in (0, 320):
            send_rows(1, top, at, HALF)
    advance()
    fold_cols(N, N)
    halos = []

    def update(which, at, size, extra):
        w = slice(at, at + size)
        lv = light[which, w]
        mine = lanes((size, N))
        for ch in range(2):
            t = me[which, ch, w]
            if extra is not None:
                t = t + extra[ch]
            old = tiles[ch, 1, w] if which == 0 else jnp.where(mine < HALF, tiles[ch, 2, w], tiles[ch, 0, w])
            fresh[which, ch, w] = old + t * lv

    def halo(at, size):
        if last:
            return
        w = slice(at, at + size)
        a, b = halo_strips(fresh[1, 0, w], fresh[1, 1, w])
        sl[w] = a
        sr[w] = b
        d = pl.ds(at, size)
        halos.extend([link(sl.at[d], hr.at[d], left, right), link(sr.at[d], hl.at[d], right, left)])

    update(1, N, N, None)
    halo(N, N)
    update(0, N, N, None)
    advance()
    if last:
        row_links[1, False, 0].arrived()
        update(1, HALF, HALF, from_up.at[1])
        row_links[1, True, 0].arrived()
        update(1, 256, HALF, from_down.at[1])
        row_links[0, False, 0].arrived()
        update(0, HALF, HALF, from_up.at[0])
        row_links[0, True, 0].arrived()
        update(0, 256, HALF, from_down.at[0])
        wide = lanes((TILE, N))
        w = slice(HALF, HALF + TILE)
        for ch in range(2):
            m, e = fresh[0, ch, w], fresh[1, ch, w]
            out[ch, :, 0:128] = turn(jnp.where(wide < HALF, m, e))
            out[ch, :, 128:256] = turn(jnp.where(wide < HALF, e, m))
        for _ in range(4):
            advance()
        inv = lax.rsqrt(whole[pl.ds(128, 16)] + PROBE_REG)
        for k in range(8):
            step_out[pl.ds(16 * k, 16)] = whole[pl.ds(16 * k, 16)] * inv
    else:
        for top, at in ((True, 0), (False, 64), (True, 64), (False, 0)):
            row_links[1, top, at].arrived()
            source, base = (from_down, 2 * N) if top else (from_up, 0)
            update(1, base + at, HALF, source.at[1, :, pl.ds(at, HALF), :])
            halo(base + at, HALF)
        row_links[0, False, 0].arrived()
        update(0, 0, N, from_up.at[0])
        row_links[0, True, 0].arrived()
        update(0, 2 * N, N, from_down.at[0])
        for ch in range(2):
            out[ch, 1] = fresh[0, ch]
        for c in halos:
            c.arrived()
        finish_tiles(out, fresh, hl, hr)
    for c in every:
        c.sent()


def run_batch(batch, last, offs, tiles, others, gin):
    f = jnp.float32
    strip = pltpu.VMEM((PADROWS, N), f)
    sums = jax.ShapeDtypeStruct((2 * MODES + 1, N, N), f)
    reach = HALF if last else N
    if last:
        shapes = (jax.ShapeDtypeStruct((2, TILE, TILE), f), jax.ShapeDtypeStruct((128, 8, N), f))
        extra = [pltpu.VMEM((2 * MODES + 1, N, N), f), pltpu.VMEM((TILES, 8, N), f)]
    else:
        shapes = (jax.ShapeDtypeStruct((2, 3, PADROWS, N), f), sums)
        extra = []
    return pl.pallas_call(
        functools.partial(batch_kernel, batch, last),
        out_shape=shapes,
        in_specs=[SM] + [VM] * (1 + len(others) + len(gin)),
        out_specs=(VM,) * len(shapes),
        scratch_shapes=extra + [
            pltpu.VMEM((len(MOVING), 2, 2, PADROWS, N), f),
            pltpu.VMEM((len(STATIC), 2, N, N), f),
            pltpu.VMEM((3, 2, PADROWS, N), f),
            pltpu.VMEM((2, PADROWS, N), f),
            strip, strip, strip, strip,
            pltpu.VMEM((2, 2, PADROWS, N), f),
            pltpu.VMEM((2, 2, PADROWS, N), f),
            pltpu.VMEM((2, 2, reach, N), f),
            pltpu.VMEM((2, 2, reach, N), f),
        ] + ([] if last else [strip] * 4) + [
            pltpu.SemaphoreType.DMA((26,)),
            pltpu.SemaphoreType.DMA((26,)),
        ] + (reduction_scratch() if last else []),
        compiler_params=pltpu.CompilerParams(
            collective_id=1 + batch, has_side_effects=True, vmem_limit_bytes=36 * 2**20),
        name=f"batch{batch}",
    )(offs, tiles, *others, *gin)


def on_device(object_field, probe, amplitudes, offsets):
    mine = jnp.pad(offsets.reshape(1, 24), ((0, 7), (0, N - 24)))
    amps = amplitudes.reshape(BATCHES, POS, N, N)
    tabs = [jnp.asarray(t) for t in tables()]
    keep = lambda a: pltpu.with_memory_space_constraint(a, pltpu.HBM)
    tiles, offs, *others = run_first(keep(object_field), mine, [keep(a) for a in (*tabs, amps, probe)])
    grads = ()
    for b in range(BATCHES - 1):
        tiles, sums = run_batch(b, False, offs, tiles, others, grads)
        grads = (sums,)
    obj, step = run_batch(BATCHES - 1, True, offs, tiles, others, grads)
    return obj, step.reshape(2, MODES, N, N)


def solution(mesh):
    placed = (
        P(None, "row", "col"),
        P(),
        P("row", "col", None, None, None, None),
        P("row", "col", None, None, None),
    )
    return jax.shard_map(
        on_device,
        mesh=mesh,
        in_specs=placed,
        out_specs=(P(None, "row", "col"), P()),
        check_vma=False,
    )
```

```python
import functools
import math

import jax
import jax.numpy as jnp
import ml_dtypes
import numpy as np
from jax import lax
from jax.experimental import pallas as pl
from jax.experimental.pallas import tpu as pltpu
from jax.sharding import PartitionSpec as P

N = 128
MODES = 4
TILE = 256
POS = 4
BATCHES = 3
HALF = 64
PADROWS = 384
FAR = 100000

AMP_FLOOR = 0.25
OBJECT_REG = 0.5
PROBE_REG = 1.0

MESH = pl.DeviceIdType.MESH
VM = pl.BlockSpec(memory_space=pltpu.VMEM)
SM = pl.BlockSpec(memory_space=pltpu.SMEM)


def tables():
    k = np.arange(N)
    ang = (k[:, None] * k[None, :] % N) * (2.0 * math.pi / N)
    fr, fi = np.cos(ang) / math.sqrt(N), -np.sin(ang) / math.sqrt(N)
    a = np.block([[fr, fi], [-fi, fr]])
    b = np.block([[fr, -fi], [fi, fr]])

    def split(m):
        hi = m.astype(np.float32).astype(ml_dtypes.bfloat16)
        lo = (m - hi.astype(np.float64)).astype(np.float32).astype(ml_dtypes.bfloat16)
        return hi, lo

    ah, al = split(a)
    bh, bl = split(b)
    return ah, al, bh, bl


def lanes(shape):
    return lax.broadcasted_iota(jnp.int32, shape, 1)


def split_hi_lo(x):
    hi = x.astype(jnp.bfloat16)
    lo = (x - hi.astype(jnp.float32)).astype(jnp.bfloat16)
    return hi, lo


def dot(a, b):
    return jnp.dot(a, b, preferred_element_type=jnp.float32)


def right_mul(x, th, tl):
    hi, lo = split_hi_lo(x)
    return dot(jnp.concatenate([hi, lo, hi], axis=1), jnp.concatenate([th, th, tl], axis=0))


def left_mul(th, tl, x):
    hi, lo = split_hi_lo(x)
    return dot(jnp.concatenate([th, th, tl], axis=1), jnp.concatenate([hi, lo, hi], axis=0))


def position():
    row, col = lax.axis_index("row"), lax.axis_index("col")
    rows, cols = lax.axis_size("row"), lax.axis_size("col")
    up = (row > 0, {"row": jnp.maximum(row - 1, 0), "col": col})
    down = (row < rows - 1, {"row": jnp.minimum(row + 1, rows - 1), "col": col})
    left = (col > 0, {"row": row, "col": jnp.maximum(col - 1, 0)})
    right = (col < cols - 1, {"row": row, "col": jnp.minimum(col + 1, cols - 1)})
    return up, down, left, right


def greet(sides, others=()):
    barrier = pltpu.get_barrier_semaphore()
    for there, device in sides:
        @pl.when(there)
        def _(device=device):
            pl.semaphore_signal(barrier, inc=1, device_id=device, device_id_type=MESH)
    for device in others:
        pl.semaphore_signal(barrier, inc=1, device_id=device, device_id_type=MESH)


def greeted(sides, others=()):
    barrier = pltpu.get_barrier_semaphore()
    pl.semaphore_wait(barrier, sum(there.astype(jnp.int32) for there, _ in sides) + len(others))


class Link:
    def __init__(self, src, dst, send, recv, to, source):
        self.there, device = to
        self.source = source[0]
        self.copy = pltpu.make_async_remote_copy(
            src_ref=src, dst_ref=dst, send_sem=send, recv_sem=recv,
            device_id=device, device_id_type=MESH)

    def start(self):
        @pl.when(self.there)
        def _():
            self.copy.start()

    def arrived(self):
        @pl.when(self.source)
        def _():
            self.copy.wait_recv()

    def sent(self):
        @pl.when(self.there)
        def _():
            self.copy.wait_send()


def clear_missing(pairs):
    for there, ref in pairs:
        @pl.when(jnp.logical_not(there))
        def _(ref=ref):
            ref[...] = jnp.zeros(ref.shape, ref.dtype)


def turn(x):
    return pltpu.roll(x, HALF, 1)


def halo_strips(re, im):
    lane = lanes(re.shape)
    ti = turn(im)
    return jnp.where(lane < HALF, ti, re), jnp.where(lane < HALF, re, ti)


def first_kernel(obj_hbm, offs, *rest):
    far_refs, rest = rest[:6], rest[6:]
    out, offs_out, *near_refs = rest[:8]
    obj, me, sl, sr, hl, hr, table, send, recv, local = rest[8:]
    up, down, left, right = position()
    load = pltpu.make_async_copy(obj_hbm, obj, local.at[0])
    load.start()
    loads = [pltpu.make_async_copy(a, b, local.at[i + 1]) for i, (a, b) in enumerate(zip(far_refs, near_refs))]
    for c in loads:
        c.start()
    lane = lanes((TILE, N))
    table[...] = jnp.full(table.shape, FAR, jnp.int32)
    table[1, 1] = offs[...]
    clear_missing([(left[0], hl), (right[0], hr),
                   (up[0], me.at[:, :, pl.ds(0, HALF), :]),
                   (down[0], me.at[:, :, pl.ds(PADROWS - HALF, HALF), :])])
    greet((up, down, left, right))
    own = slice(HALF, HALF + TILE)
    load.wait()
    for ch in range(2):
        a, b = turn(obj[ch, :, 0:128]), turn(obj[ch, :, 128:256])
        me[1, ch, own] = jnp.where(lane < HALF, b, a)
        me[0, ch, own] = jnp.where(lane < HALF, a, b)
    greeted((up, down, left, right))

    count = iter(range(100))

    def link(src, dst, to, source):
        i = next(count)
        return Link(src, dst, send.at[i], recv.at[i], to, source)

    def rows(which):
        top, bottom = pl.ds(HALF, HALF), pl.ds(TILE, HALF)
        above, below = pl.ds(0, HALF), pl.ds(PADROWS - HALF, HALF)
        return [link(me.at[which, :, top, :], me.at[which, :, below, :], up, down),
                link(me.at[which, :, bottom, :], me.at[which, :, above, :], down, up)]

    def cols(at, size):
        w = slice(at, at + size)
        a, b = halo_strips(me[1, 0, w], me[1, 1, w])
        sl[w] = a
        sr[w] = b
        d = pl.ds(at, size)
        both = [link(sl.at[d], hr.at[d], left, right), link(sr.at[d], hl.at[d], right, left)]
        for c in both:
            c.start()
        return both

    tell = [link(table.at[1, 1], table.at[1, 2], up, down),
            link(table.at[1, 1], table.at[1, 0], down, up)]
    edge = rows(1)
    middle = rows(0)
    for c in tell + edge:
        c.start()
    late = cols(HALF, TILE)
    for c in middle:
        c.start()
    for c in tell:
        c.arrived()
    more = [link(table.at[1], table.at[2], left, right),
            link(table.at[1], table.at[0], right, left)]
    for c in more:
        c.start()
    late += more
    edge[1].arrived()
    late += cols(0, HALF)
    edge[0].arrived()
    late += cols(PADROWS - HALF, HALF)
    for c in middle:
        c.arrived()
    for ch in range(2):
        out[ch, 1] = me[0, ch]
    for c in late:
        c.arrived()
    finish_tiles(out, me, hl, hr)
    offs_out[...] = table[...]
    for c in loads:
        c.wait()
    for c in tell + edge + middle + late:
        c.sent()


def finish_tiles(out, me, hl, hr):
    wide = lanes((PADROWS, N))
    out[0, 0] = jnp.where(wide < HALF, hl[...], me[1, 0])
    out[1, 0] = jnp.where(wide < HALF, turn(hl[...]), me[1, 1])
    out[0, 2] = jnp.where(wide < HALF, me[1, 0], hr[...])
    out[1, 2] = jnp.where(wide < HALF, me[1, 1], turn(hr[...]))


def run_first(obj, offs, others):
    f = jnp.float32
    strip = pltpu.VMEM((PADROWS, N), f)
    hbm = pl.BlockSpec(memory_space=pltpu.HBM)
    return pl.pallas_call(
        first_kernel,
        out_shape=(
            jax.ShapeDtypeStruct((2, 3, PADROWS, N), f),
            jax.ShapeDtypeStruct((3, 3, 8, N), jnp.int32),
        ) + tuple(jax.ShapeDtypeStruct(a.shape, a.dtype) for a in others),
        in_specs=[hbm, VM] + [hbm] * 6,
        out_specs=(VM,) * 8,
        scratch_shapes=[
            pltpu.VMEM((2, TILE, TILE), f),
            pltpu.VMEM((2, 2, PADROWS, N), f),
            strip, strip, strip, strip,
            pltpu.VMEM((3, 3, 8, N), jnp.int32),
            pltpu.SemaphoreType.DMA((14,)),
            pltpu.SemaphoreType.DMA((14,)),
            pltpu.SemaphoreType.DMA((7,)),
        ],
        compiler_params=pltpu.CompilerParams(collective_id=0, has_side_effects=True, vmem_limit_bytes=14 * 2**20),
        name="first",
    )(obj, offs, *others)


def spread(dest, value, s):
    lane = lanes((N, N))
    turned = pltpu.roll(value, s, 1)
    dest[0, N:2 * N] = jnp.where(lane >= s, turned, 0.0)
    dest[1, N:2 * N] = jnp.where(lane < s, turned, 0.0)


def window(src, r0, t, i, k):
    j = k - t
    hit = (j == 0) | (j == 1)
    start = jnp.where(hit, jnp.clip(N + N * i - r0, 0, 2 * N), 0)
    return src[jnp.where(hit, j, 0), pl.ds(start, N)]


STATIC = ((0, 0, 0), (1, 2 * N, 2))
MOVING = (2, 3)


def spot(offs, block, batch, p):
    cr, rr = block
    r0 = offs[cr, rr, 0, batch * 8 + p * 2] + (rr - 1) * TILE + HALF
    c0 = offs[cr, rr, 0, batch * 8 + p * 2 + 1] + (cr - 1) * TILE + HALF
    return r0, lax.shift_right_arithmetic(c0, 7), lax.bitwise_and(c0, 127)


def terms(pr, pi, probe, measured, gout, gin, first, ah, al, bh, bl):
    waves = []
    for m in range(MODES):
        qr, qi = probe[0, m], probe[1, m]
        waves.append(jnp.concatenate([qr * pr - qi * pi, qr * pi + qi * pr], axis=1))
    half = right_mul(jnp.concatenate(waves, axis=0), ah[...], al[...])
    rows_of = [half[m * N:(m + 1) * N] for m in range(MODES)]
    stacked = jnp.concatenate(
        [jnp.concatenate([h[:, :N] for h in rows_of], axis=1),
         jnp.concatenate([h[:, N:] for h in rows_of], axis=1)], axis=0)
    far = left_mul(bh[...], bl[...], stacked)
    inten = jnp.zeros((N, N), jnp.float32)
    for m in range(MODES):
        fr, fi = far[:N, m * N:(m + 1) * N], far[N:, m * N:(m + 1) * N]
        inten += fr * fr + fi * fi
    factor = measured * lax.rsqrt(jnp.maximum(inten, AMP_FLOOR * AMP_FLOOR)) - 1.0
    factor = jnp.concatenate([factor] * MODES, axis=1)
    factor = jnp.concatenate([factor] * 2, axis=0)
    back_half = left_mul(ah[...], al[...], far * factor)
    lhs = jnp.concatenate(
        [jnp.concatenate([back_half[:N, m * N:(m + 1) * N], back_half[N:, m * N:(m + 1) * N]], axis=1)
         for m in range(MODES)], axis=0)
    change = right_mul(lhs, bh[...], bl[...])
    tr = jnp.zeros((N, N), jnp.float32)
    ti = jnp.zeros((N, N), jnp.float32)

    def accumulate(k, value):
        if not first:
            gout[k] += value
        elif gin is None:
            gout[k] = value
        else:
            gout[k] = gin[k] + value

    for m in range(MODES):
        qr, qi = probe[0, m], probe[1, m]
        cr, ci = change[m * N:(m + 1) * N, :N], change[m * N:(m + 1) * N, N:]
        tr += qr * cr + qi * ci
        ti += qr * ci - qi * cr
        accumulate(m, pr * cr + pi * ci)
        accumulate(MODES + m, pr * ci - pi * cr)
    accumulate(2 * MODES, pr * pr + pi * pi)
    return tr, ti


def moving_terms(batch, offs, tiles, probe, amp, gout, gin, z, tabs):
    lane = lanes((N, N))
    for n, p in enumerate(MOVING):
        r0, t, s = spot(offs, (1, 1), batch, p)
        rows = pl.ds(r0, N)
        back = lax.bitwise_and(128 - s, 127)
        after = jnp.minimum(t + 1, 2)

        def cut(ch):
            one = pltpu.roll(tiles[ch, t, rows], back, 1)
            two = pltpu.roll(tiles[ch, after, rows], back, 1)
            return jnp.where(lane < 128 - s, one, two)

        tr, ti = terms(cut(0), cut(1), probe, amp[batch, p], gout, gin, n == 0, *tabs)
        spread(z.at[n, 0], tr, s)
        spread(z.at[n, 1], ti, s)


def static_terms(batch, tiles, probe, amp, gout, fixed, tabs):
    for p, at, t in STATIC:
        pr, pi = tiles[0, t, at:at + N], tiles[1, t, at:at + N]
        tr, ti = terms(pr, pi, probe, amp[batch, p], gout, None, False, *tabs)
        fixed[p, 0] = tr
        fixed[p, 1] = ti


def light_maps(batch, offs, probe, zl, light):
    row, rows = lax.axis_index("row"), lax.axis_size("row")
    col, cols = lax.axis_index("col"), lax.axis_size("col")
    lane = lanes((N, N))
    total = jnp.zeros((N, N), jnp.float32)
    for m in range(MODES):
        total += probe[0, m] * probe[0, m] + probe[1, m] * probe[1, m]
    blank = jnp.zeros((N, N), jnp.float32)
    slots = zl.shape[0]
    for n in range(slots):
        for j in range(2):
            zl[n, j, 0:N] = blank
            zl[n, j, 2 * N:] = blank

    def there(yes):
        return yes.astype(jnp.float32)

    up, down, left, right = there(row > 0), there(row < rows - 1), there(col > 0), there(col < cols - 1)
    corner = {(0, 0): 1.0 + up * left, (0, 2): right + up, (2, 0): down + left, (2, 2): 1.0 + down * right}
    sums = {}
    for i in (0, 2):
        sums[i] = total * jnp.where(lane < HALF, corner[i, 2], corner[i, 0])
    light[1, 0:N] = sums[0]
    light[1, N:2 * N] = blank
    light[1, 2 * N:] = sums[2]
    for i in range(3):
        light[0, i * N:i * N + N] = blank

    n = 0
    for cr in range(3):
        for rr in range(3):
            for p in MOVING:
                r0, t, s = spot(offs, (cr, rr), batch, p)
                buf = zl.at[n % slots]
                n += 1
                spread(buf, total, s)
                for i in {0: (0,), 1: (0, 1, 2), 2: (2,)}[rr]:
                    w = slice(i * N, i * N + N)
                    if cr == 0:
                        light[1, w] += jnp.where(lane < HALF, 0.0, window(buf, r0, t, i, 0))
                    elif cr == 2:
                        light[1, w] += jnp.where(lane < HALF, window(buf, r0, t, i, 2), 0.0)
                    else:
                        light[0, w] += window(buf, r0, t, i, 1)
                        light[1, w] += jnp.where(lane < HALF, window(buf, r0, t, i, 2), window(buf, r0, t, i, 0))
    place = lax.broadcasted_iota(jnp.int32, (PADROWS, N), 0)
    low = jnp.where(row == 0, HALF, 0)
    high = jnp.where(row == rows - 1, HALF + TILE, PADROWS)
    inside = (place >= low) & (place < high)
    for j in range(2):
        light[j] = jnp.where(inside, 1.0 / (light[j] + OBJECT_REG), 0.0)


TILES = 144
HALFT = 72
PART = 36
SPLITS = (("group", 8, 5, "x", 4, 2), ("x", 4, 9, "group", 8, 2))


class Mates:
    def __init__(self):
        self.row, self.col = lax.axis_index("row"), lax.axis_index("col")
        self.x, self.zh = self.row // 4, self.row % 4
        self.core, self.group = self.col % 2, self.col // 2
        self.partner = {"row": self.row, "col": self.col + 1 - 2 * self.core}

    def at(self, axis, d):
        if axis == "group":
            k = lax.rem(self.group + d, 8)
            return k, {"row": self.row, "col": k * 2 + self.core}
        if axis == "x":
            k = lax.rem(self.x + d, 4)
            return k, {"row": k * 4 + self.zh, "col": self.col}
        k = lax.rem(self.zh + d, 4)
        return k, {"row": self.x * 4 + k, "col": self.col}

    def everyone(self):
        return ([self.partner] + [self.at("group", d)[1] for d in range(1, 8)]
                + [self.at("x", d)[1] for d in range(1, 4)] + [self.at("z", d)[1] for d in range(1, 4)])


def reduce_part(part, mates, g, whole, bufs):
    axis1, n1, p1, axis2, n2, p2 = SPLITS[part]
    r1, s1, r2, s2, r3, z, fin, ag1, ag2, send, recv = bufs
    count = iter(range(100))
    every = []

    def go(src, dst, device):
        i = next(count)
        c = pltpu.make_async_remote_copy(
            src_ref=src, dst_ref=dst, send_sem=send.at[i], recv_sem=recv.at[i],
            device_id=device, device_id_type=MESH)
        c.start()
        every.append(c)
        return c

    def scatter(src, slots, axis, n, p):
        cs = []
        for d in range(1, n):
            k, device = mates.at(axis, d)
            cs.append(go(src.at[pl.ds(k * p, p)], slots.at[d - 1], device))
        return cs

    def collect(src, slots, axis, p, cs):
        acc = src[pl.ds(mates.at(axis, 0)[0] * p, p)]
        for d, c in enumerate(cs):
            c.wait_recv()
            acc = acc + slots[d]
        return acc

    def gather(src, dst, axis, n, p):
        me = pl.ds(mates.at(axis, 0)[0] * p, p)
        cs = [go(src, dst.at[me], mates.at(axis, d)[1]) for d in range(1, n)]
        dst[me] = src[...]
        return cs

    core = mates.core
    if s1.shape[0] > PART:
        s1[pl.ds(PART, s1.shape[0] - PART)] = jnp.zeros((s1.shape[0] - PART, 8, N), jnp.float32)
    s2[pl.ds(p1, s2.shape[0] - p1)] = jnp.zeros((s2.shape[0] - p1, 8, N), jnp.float32)
    c = go(g.at[pl.ds((1 - core) * HALFT + part * PART, PART)], r1, mates.partner)
    yield
    c.wait_recv()
    s1[pl.ds(0, PART)] = g[pl.ds(core * HALFT + part * PART, PART)] + r1[...]
    cs = scatter(s1, r2, axis1, n1, p1)
    yield
    s2[pl.ds(0, p1)] = collect(s1, r2, axis1, p1, cs)
    cs = scatter(s2, r3, axis2, n2, p2)
    yield
    z[0] = collect(s2, r3, axis2, p2, cs)
    cs = [go(z.at[0], z.at[d], mates.at("z", d)[1]) for d in range(1, 4)]
    yield
    for c in cs:
        c.wait_recv()
    acc = z[lax.rem(mates.zh, 4)]
    for k in range(1, 4):
        acc = acc + z[lax.rem(mates.zh - k + 4, 4)]
    fin[...] = acc
    cs = gather(fin, ag1, axis2, n2, p2)
    yield
    for c in cs:
        c.wait_recv()
    cs = gather(ag1.at[pl.ds(0, p1)], ag2, axis1, n1, p1)
    yield
    for c in cs:
        c.wait_recv()
    mine = pl.ds(core * HALFT + part * PART, PART)
    c = go(ag2.at[pl.ds(0, PART)], whole.at[mine], mates.partner)
    whole[mine] = ag2[pl.ds(0, PART)]
    yield
    c.wait_recv()
    for c in every:
        c.wait_send()
    yield


PART_REFS = 11


def reduction_scratch():
    f = jnp.float32
    shape = lambda *n: pltpu.VMEM(n + (8, N), f)
    refs = [shape(TILES)]
    for _, n1, p1, _, n2, p2 in SPLITS:
        refs += [shape(PART), shape(n1 * p1), shape(n1 - 1, p1), shape(n2 * p2), shape(n2 - 1, p2),
                 shape(4, p2), shape(p2), shape(n2 * p2), shape(n1 * p1),
                 pltpu.SemaphoreType.DMA((25,)), pltpu.SemaphoreType.DMA((25,))]
    return refs


def batch_kernel(batch, last, offs, tiles, *rest):
    tabs, (amp, probe), rest = rest[:4], rest[4:6], rest[6:]
    gin = None
    if batch:
        gin, *rest = rest
    others, parts = (), ()
    if last:
        out, step_out, gout, flat, z, fixed, zl, light, ls, rs, ls_in, rs_in, me, fresh, from_up, from_down, send, recv, whole, *more = rest
        mates = Mates()
        others = mates.everyone()
        parts = [reduce_part(k, mates, flat, whole, more[k * PART_REFS:(k + 1) * PART_REFS]) for k in range(2)]
        reach = HALF
    else:
        out, gout, z, fixed, zl, light, ls, rs, ls_in, rs_in, me, fresh, from_up, from_down, sl, sr, hl, hr, send, recv = rest
        reach = N
    up, down, left, right = sides = position()
    clear_missing([(left[0], rs_in), (right[0], ls_in), (up[0], from_up), (down[0], from_down)])
    if not last:
        clear_missing([(left[0], hl), (right[0], hr)])
    greet(sides, others)

    def advance():
        for part in parts:
            next(part)

    blank = jnp.zeros((N, N), jnp.float32)
    for n in range(len(MOVING)):
        for ch in range(2):
            for j in range(2):
                z[n, ch, j, 0:N] = blank
                z[n, ch, j, 2 * N:] = blank
    moving_terms(batch, offs, tiles, probe, amp, gout, gin, z, tabs)
    greeted(sides, others)

    count = iter(range(100))
    every = []

    def link(src, dst, to, source):
        i = next(count)
        c = Link(src, dst, send.at[i], recv.at[i], to, source)
        c.start()
        every.append(c)
        return c

    def gathered(ch, i, k):
        acc = None
        for n, p in enumerate(MOVING):
            r0, t, _ = spot(offs, (1, 1), batch, p)
            w = window(z.at[n, ch], r0, t, i, k)
            acc = w if acc is None else acc + w
        for p, at, tile in STATIC:
            if (at, tile) == (i * N, k):
                acc = acc + fixed[p, ch]
        return acc

    lane = lanes((N, N))
    cols = {}
    row_links = {}

    def side_strips(i):
        w = slice(i * N, i * N + N)
        t0 = [gathered(ch, i, 0) for ch in range(2)]
        t2 = [gathered(ch, i, 2) for ch in range(2)]
        ls[w] = jnp.where(lane < HALF, t0[0], turn(t0[1]))
        rs[w] = jnp.where(lane < HALF, turn(t2[0]), t2[1])
        for ch in range(2):
            me[1, ch, w] = jnp.where(lane < HALF, t2[ch], t0[ch])

    def send_cols(at, size):
        d = pl.ds(at, size)
        cols[at] = [link(ls.at[d], ls_in.at[d], left, right), link(rs.at[d], rs_in.at[d], right, left)]

    def middle(i):
        for ch in range(2):
            me[0, ch, i * N:i * N + N] = gathered(ch, i, 1)

    def send_rows(which, top, at, size):
        base = 0 if top else PADROWS - reach
        src, dst = pl.ds(at, size), pl.ds(at - base, size)
        if top:
            c = link(me.at[which, :, src, :], from_down.at[which, :, dst, :], up, down)
        else:
            c = link(me.at[which, :, src, :], from_up.at[which, :, dst, :], down, up)
        row_links[which, top, at - base] = c

    def fold_cols(at, size):
        for c in cols[at]:
            c.arrived()
        w = slice(at, at + size)
        side = lanes((size, N))
        a, b = ls_in[w], rs_in[w]
        me[1, 0, w] += jnp.where(side < HALF, a, turn(b))
        me[1, 1, w] += jnp.where(side < HALF, turn(a), b)

    order = ((0, True), (320, False), (64, True), (256, False))

    def send_edges():
        for at, top in order:
            fold_cols(at, HALF)
            if not last or at in (0, 320):
                send_rows(1, top, at, HALF)

    if last:
        static_terms(batch, tiles, probe, amp, gout, fixed, tabs)
        flat[...] = gout[...].reshape(TILES, 8, N)
        advance()
        middle(0)
        send_rows(0, True, 0, reach)
        middle(2)
        send_rows(0, False, PADROWS - reach, reach)
        advance()
        for i in (0, 2, 1):
            side_strips(i)
        middle(1)
        light_maps(batch, offs, probe, zl, light)
        advance()
        for at, _ in order:
            send_cols(at, HALF)
        send_cols(N, N)
        advance()
        send_edges()
    else:
        middle(0)
        send_rows(0, True, 0, reach)
        middle(2)
        send_rows(0, False, PADROWS - reach, reach)
        side_strips(1)
        send_cols(N, N)
        static_terms(batch, tiles, probe, amp, gout, fixed, tabs)
        side_strips(0)
        send_cols(0, HALF)
        side_strips(2)
        for at in (320, 64, 256):
            send_cols(at, HALF)
        middle(1)
        light_maps(batch, offs, probe, zl, light)
        send_edges()
    fold_cols(N, N)
    halos = []

    def update(which, at, size, extra):
        w = slice(at, at + size)
        lv = light[which, w]
        mine = lanes((size, N))
        for ch in range(2):
            t = me[which, ch, w]
            if extra is not None:
                t = t + extra[ch]
            old = tiles[ch, 1, w] if which == 0 else jnp.where(mine < HALF, tiles[ch, 2, w], tiles[ch, 0, w])
            fresh[which, ch, w] = old + t * lv

    def halo(at, size):
        if last:
            return
        w = slice(at, at + size)
        a, b = halo_strips(fresh[1, 0, w], fresh[1, 1, w])
        sl[w] = a
        sr[w] = b
        d = pl.ds(at, size)
        halos.extend([link(sl.at[d], hr.at[d], left, right), link(sr.at[d], hl.at[d], right, left)])

    update(1, N, N, None)
    halo(N, N)
    update(0, N, N, None)
    if last:
        row_links[1, False, 0].arrived()
        update(1, HALF, HALF, from_up.at[1])
        row_links[1, True, 0].arrived()
        update(1, 256, HALF, from_down.at[1])
        row_links[0, False, 0].arrived()
        update(0, HALF, HALF, from_up.at[0])
        row_links[0, True, 0].arrived()
        update(0, 256, HALF, from_down.at[0])
        wide = lanes((TILE, N))
        w = slice(HALF, HALF + TILE)
        for ch in range(2):
            m, e = fresh[0, ch, w], fresh[1, ch, w]
            out[ch, :, 0:128] = turn(jnp.where(wide < HALF, m, e))
            out[ch, :, 128:256] = turn(jnp.where(wide < HALF, e, m))
        for _ in range(4):
            advance()
        inv = lax.rsqrt(whole[pl.ds(128, 16)] + PROBE_REG)
        for k in range(8):
            step_out[pl.ds(16 * k, 16)] = whole[pl.ds(16 * k, 16)] * inv
    else:
        for top, at in ((True, 0), (False, 64), (True, 64), (False, 0)):
            row_links[1, top, at].arrived()
            source, base = (from_down, 2 * N) if top else (from_up, 0)
            update(1, base + at, HALF, source.at[1, :, pl.ds(at, HALF), :])
            halo(base + at, HALF)
        row_links[0, False, 0].arrived()
        update(0, 0, N, from_up.at[0])
        row_links[0, True, 0].arrived()
        update(0, 2 * N, N, from_down.at[0])
        for ch in range(2):
            out[ch, 1] = fresh[0, ch]
        for c in halos:
            c.arrived()
        finish_tiles(out, fresh, hl, hr)
    for c in every:
        c.sent()


def run_batch(batch, last, offs, tiles, others, gin):
    f = jnp.float32
    strip = pltpu.VMEM((PADROWS, N), f)
    sums = jax.ShapeDtypeStruct((2 * MODES + 1, N, N), f)
    reach = HALF if last else N
    if last:
        shapes = (jax.ShapeDtypeStruct((2, TILE, TILE), f), jax.ShapeDtypeStruct((128, 8, N), f))
        extra = [pltpu.VMEM((2 * MODES + 1, N, N), f), pltpu.VMEM((TILES, 8, N), f)]
    else:
        shapes = (jax.ShapeDtypeStruct((2, 3, PADROWS, N), f), sums)
        extra = []
    return pl.pallas_call(
        functools.partial(batch_kernel, batch, last),
        out_shape=shapes,
        in_specs=[SM] + [VM] * (1 + len(others) + len(gin)),
        out_specs=(VM,) * len(shapes),
        scratch_shapes=extra + [
            pltpu.VMEM((len(MOVING), 2, 2, PADROWS, N), f),
            pltpu.VMEM((len(STATIC), 2, N, N), f),
            pltpu.VMEM((3, 2, PADROWS, N), f),
            pltpu.VMEM((2, PADROWS, N), f),
            strip, strip, strip, strip,
            pltpu.VMEM((2, 2, PADROWS, N), f),
            pltpu.VMEM((2, 2, PADROWS, N), f),
            pltpu.VMEM((2, 2, reach, N), f),
            pltpu.VMEM((2, 2, reach, N), f),
        ] + ([] if last else [strip] * 4) + [
            pltpu.SemaphoreType.DMA((26,)),
            pltpu.SemaphoreType.DMA((26,)),
        ] + (reduction_scratch() if last else []),
        compiler_params=pltpu.CompilerParams(
            collective_id=1 + batch, has_side_effects=True, vmem_limit_bytes=36 * 2**20),
        name=f"batch{batch}",
    )(offs, tiles, *others, *gin)


def on_device(object_field, probe, amplitudes, offsets):
    mine = jnp.pad(offsets.reshape(1, 24), ((0, 7), (0, N - 24)))
    amps = amplitudes.reshape(BATCHES, POS, N, N)
    tabs = [jnp.asarray(t) for t in tables()]
    keep = lambda a: pltpu.with_memory_space_constraint(a, pltpu.HBM)
    tiles, offs, *others = run_first(keep(object_field), mine, [keep(a) for a in (*tabs, amps, probe)])
    grads = ()
    for b in range(BATCHES - 1):
        tiles, sums = run_batch(b, False, offs, tiles, others, grads)
        grads = (sums,)
    obj, step = run_batch(BATCHES - 1, True, offs, tiles, others, grads)
    return obj, step.reshape(2, MODES, N, N)


def solution(mesh):
    placed = (
        P(None, "row", "col"),
        P(),
        P("row", "col", None, None, None, None),
        P("row", "col", None, None, None),
    )
    return jax.shard_map(
        on_device,
        mesh=mesh,
        in_specs=placed,
        out_specs=(P(None, "row", "col"), P()),
        check_vma=False,
    )
```

```python
import functools
import math

import jax
import jax.numpy as jnp
import ml_dtypes
import numpy as np
from jax import lax
from jax.experimental import pallas as pl
from jax.experimental.pallas import tpu as pltpu
from jax.sharding import PartitionSpec as P

N = 128
MODES = 4
TILE = 256
POS = 4
BATCHES = 3
HALF = 64
PADROWS = 384
FAR = 100000

AMP_FLOOR = 0.25
OBJECT_REG = 0.5
PROBE_REG = 1.0

MESH = pl.DeviceIdType.MESH
VM = pl.BlockSpec(memory_space=pltpu.VMEM)
SM = pl.BlockSpec(memory_space=pltpu.SMEM)


def tables():
    k = np.arange(N)
    ang = (k[:, None] * k[None, :] % N) * (2.0 * math.pi / N)
    fr, fi = np.cos(ang) / math.sqrt(N), -np.sin(ang) / math.sqrt(N)
    a = np.block([[fr, fi], [-fi, fr]])
    b = np.block([[fr, -fi], [fi, fr]])

    def split(m):
        hi = m.astype(np.float32).astype(ml_dtypes.bfloat16)
        lo = (m - hi.astype(np.float64)).astype(np.float32).astype(ml_dtypes.bfloat16)
        return hi, lo

    ah, al = split(a)
    bh, bl = split(b)
    return ah, al, bh, bl


def lanes(shape):
    return lax.broadcasted_iota(jnp.int32, shape, 1)


def split_hi_lo(x):
    hi = x.astype(jnp.bfloat16)
    lo = (x - hi.astype(jnp.float32)).astype(jnp.bfloat16)
    return hi, lo


def dot(a, b):
    return jnp.dot(a, b, preferred_element_type=jnp.float32)


def right_mul(x, th, tl):
    hi, lo = split_hi_lo(x)
    return dot(jnp.concatenate([hi, lo, hi], axis=1), jnp.concatenate([th, th, tl], axis=0))


def left_mul(th, tl, x):
    hi, lo = split_hi_lo(x)
    return dot(jnp.concatenate([th, th, tl], axis=1), jnp.concatenate([hi, lo, hi], axis=0))


def position():
    row, col = lax.axis_index("row"), lax.axis_index("col")
    rows, cols = lax.axis_size("row"), lax.axis_size("col")
    up = (row > 0, {"row": jnp.maximum(row - 1, 0), "col": col})
    down = (row < rows - 1, {"row": jnp.minimum(row + 1, rows - 1), "col": col})
    left = (col > 0, {"row": row, "col": jnp.maximum(col - 1, 0)})
    right = (col < cols - 1, {"row": row, "col": jnp.minimum(col + 1, cols - 1)})
    return up, down, left, right


def greet(sides, others=()):
    barrier = pltpu.get_barrier_semaphore()
    for there, device in sides:
        @pl.when(there)
        def _(device=device):
            pl.semaphore_signal(barrier, inc=1, device_id=device, device_id_type=MESH)
    for device in others:
        pl.semaphore_signal(barrier, inc=1, device_id=device, device_id_type=MESH)


def greeted(sides, others=()):
    barrier = pltpu.get_barrier_semaphore()
    pl.semaphore_wait(barrier, sum(there.astype(jnp.int32) for there, _ in sides) + len(others))


class Link:
    def __init__(self, src, dst, send, recv, to, source):
        self.there, device = to
        self.source = source[0]
        self.copy = pltpu.make_async_remote_copy(
            src_ref=src, dst_ref=dst, send_sem=send, recv_sem=recv,
            device_id=device, device_id_type=MESH)

    def start(self):
        @pl.when(self.there)
        def _():
            self.copy.start()

    def arrived(self):
        @pl.when(self.source)
        def _():
            self.copy.wait_recv()

    def sent(self):
        @pl.when(self.there)
        def _():
            self.copy.wait_send()


def clear_missing(pairs):
    for there, ref in pairs:
        @pl.when(jnp.logical_not(there))
        def _(ref=ref):
            ref[...] = jnp.zeros(ref.shape, ref.dtype)


def turn(x):
    return pltpu.roll(x, HALF, 1)


def halo_strips(re, im):
    lane = lanes(re.shape)
    ti = turn(im)
    return jnp.where(lane < HALF, ti, re), jnp.where(lane < HALF, re, ti)


def first_kernel(obj_hbm, offs, *rest):
    far_refs, rest = rest[:6], rest[6:]
    out, offs_out, *near_refs = rest[:8]
    obj, me, sl, sr, hl, hr, table, send, recv, local = rest[8:]
    up, down, left, right = position()
    load = pltpu.make_async_copy(obj_hbm, obj, local.at[0])
    load.start()
    loads = [pltpu.make_async_copy(a, b, local.at[i + 1]) for i, (a, b) in enumerate(zip(far_refs, near_refs))]
    for c in loads:
        c.start()
    lane = lanes((TILE, N))
    for cr in range(3):
        for rr in range(3):
            if (cr, rr) != (1, 1):
                table[cr, rr] = jnp.full(table.shape[2:], FAR, jnp.int32)
    own_offs = pltpu.make_async_copy(offs, table.at[1, 1], local.at[7])
    own_offs.start()
    clear_missing([(left[0], hl), (right[0], hr),
                   (up[0], me.at[:, :, pl.ds(0, HALF), :]),
                   (down[0], me.at[:, :, pl.ds(PADROWS - HALF, HALF), :])])
    greet((up, down, left, right))
    own = slice(HALF, HALF + TILE)
    load.wait()
    for ch in range(2):
        a, b = turn(obj[ch, :, 0:128]), turn(obj[ch, :, 128:256])
        me[1, ch, own] = jnp.where(lane < HALF, b, a)
        me[0, ch, own] = jnp.where(lane < HALF, a, b)
    own_offs.wait()
    greeted((up, down, left, right))

    count = iter(range(100))

    def link(src, dst, to, source):
        i = next(count)
        return Link(src, dst, send.at[i], recv.at[i], to, source)

    def rows(which):
        top, bottom = pl.ds(HALF, HALF), pl.ds(TILE, HALF)
        above, below = pl.ds(0, HALF), pl.ds(PADROWS - HALF, HALF)
        return [link(me.at[which, :, top, :], me.at[which, :, below, :], up, down),
                link(me.at[which, :, bottom, :], me.at[which, :, above, :], down, up)]

    def cols(at, size):
        w = slice(at, at + size)
        a, b = halo_strips(me[1, 0, w], me[1, 1, w])
        sl[w] = a
        sr[w] = b
        d = pl.ds(at, size)
        both = [link(sl.at[d], hr.at[d], left, right), link(sr.at[d], hl.at[d], right, left)]
        for c in both:
            c.start()
        return both

    tell = [link(table.at[1, 1], table.at[1, 2], up, down),
            link(table.at[1, 1], table.at[1, 0], down, up)]
    edge = rows(1)
    middle = rows(0)
    for c in tell + edge:
        c.start()
    late = cols(HALF, TILE)
    for c in middle:
        c.start()
    for c in tell:
        c.arrived()
    more = [link(table.at[1], table.at[2], left, right),
            link(table.at[1], table.at[0], right, left)]
    for c in more:
        c.start()
    late += more
    edge[1].arrived()
    late += cols(0, HALF)
    edge[0].arrived()
    late += cols(PADROWS - HALF, HALF)
    for c in middle:
        c.arrived()
    for ch in range(2):
        out[ch, 1] = me[0, ch]
    for c in late:
        c.arrived()
    finish_tiles(out, me, hl, hr)
    offs_out[...] = table[...]
    for c in loads:
        c.wait()
    for c in tell + edge + middle + late:
        c.sent()


def finish_tiles(out, me, hl, hr):
    wide = lanes((PADROWS, N))
    out[0, 0] = jnp.where(wide < HALF, hl[...], me[1, 0])
    out[1, 0] = jnp.where(wide < HALF, turn(hl[...]), me[1, 1])
    out[0, 2] = jnp.where(wide < HALF, me[1, 0], hr[...])
    out[1, 2] = jnp.where(wide < HALF, me[1, 1], turn(hr[...]))


def run_first(obj, offs, others):
    f = jnp.float32
    strip = pltpu.VMEM((PADROWS, N), f)
    hbm = pl.BlockSpec(memory_space=pltpu.HBM)
    return pl.pallas_call(
        first_kernel,
        out_shape=(
            jax.ShapeDtypeStruct((2, 3, PADROWS, N), f),
            jax.ShapeDtypeStruct((3, 3, BATCHES, 2, POS), jnp.int32),
        ) + tuple(jax.ShapeDtypeStruct(a.shape, a.dtype) for a in others),
        in_specs=[hbm] * 8,
        out_specs=(VM,) * 8,
        scratch_shapes=[
            pltpu.VMEM((2, TILE, TILE), f),
            pltpu.VMEM((2, 2, PADROWS, N), f),
            strip, strip, strip, strip,
            pltpu.VMEM((3, 3, BATCHES, 2, POS), jnp.int32),
            pltpu.SemaphoreType.DMA((14,)),
            pltpu.SemaphoreType.DMA((14,)),
            pltpu.SemaphoreType.DMA((8,)),
        ],
        compiler_params=pltpu.CompilerParams(collective_id=0, has_side_effects=True, vmem_limit_bytes=14 * 2**20),
        name="first",
    )(obj, offs, *others)


def spread(dest, value, s):
    lane = lanes((N, N))
    turned = pltpu.roll(value, s, 1)
    dest[0, N:2 * N] = jnp.where(lane >= s, turned, 0.0)
    dest[1, N:2 * N] = jnp.where(lane < s, turned, 0.0)


def window(src, r0, t, i, k):
    j = k - t
    hit = (j == 0) | (j == 1)
    start = jnp.where(hit, jnp.clip(N + N * i - r0, 0, 2 * N), 0)
    return src[jnp.where(hit, j, 0), pl.ds(start, N)]


STATIC = ((0, 0, 0), (1, 2 * N, 2))
MOVING = (2, 3)


def spot(offs, block, batch, p):
    cr, rr = block
    r0 = offs[cr, rr, batch, 0, p] + (rr - 1) * TILE + HALF
    c0 = offs[cr, rr, batch, 1, p] + (cr - 1) * TILE + HALF
    return r0, lax.shift_right_arithmetic(c0, 7), lax.bitwise_and(c0, 127)


def terms(pr, pi, probe, measured, gout, gin, first, ah, al, bh, bl):
    waves = []
    for m in range(MODES):
        qr, qi = probe[0, m], probe[1, m]
        waves.append(jnp.concatenate([qr * pr - qi * pi, qr * pi + qi * pr], axis=1))
    half = right_mul(jnp.concatenate(waves, axis=0), ah[...], al[...])
    rows_of = [half[m * N:(m + 1) * N] for m in range(MODES)]
    stacked = jnp.concatenate(
        [jnp.concatenate([h[:, :N] for h in rows_of], axis=1),
         jnp.concatenate([h[:, N:] for h in rows_of], axis=1)], axis=0)
    far = left_mul(bh[...], bl[...], stacked)
    inten = jnp.zeros((N, N), jnp.float32)
    for m in range(MODES):
        fr, fi = far[:N, m * N:(m + 1) * N], far[N:, m * N:(m + 1) * N]
        inten += fr * fr + fi * fi
    factor = measured * lax.rsqrt(jnp.maximum(inten, AMP_FLOOR * AMP_FLOOR)) - 1.0
    factor = jnp.concatenate([factor] * MODES, axis=1)
    factor = jnp.concatenate([factor] * 2, axis=0)
    back_half = left_mul(ah[...], al[...], far * factor)
    lhs = jnp.concatenate(
        [jnp.concatenate([back_half[:N, m * N:(m + 1) * N], back_half[N:, m * N:(m + 1) * N]], axis=1)
         for m in range(MODES)], axis=0)
    change = right_mul(lhs, bh[...], bl[...])
    tr = jnp.zeros((N, N), jnp.float32)
    ti = jnp.zeros((N, N), jnp.float32)

    def accumulate(k, value):
        if not first:
            gout[k] += value
        elif gin is None:
            gout[k] = value
        else:
            gout[k] = gin[k] + value

    for m in range(MODES):
        qr, qi = probe[0, m], probe[1, m]
        cr, ci = change[m * N:(m + 1) * N, :N], change[m * N:(m + 1) * N, N:]
        tr += qr * cr + qi * ci
        ti += qr * ci - qi * cr
        accumulate(m, pr * cr + pi * ci)
        accumulate(MODES + m, pr * ci - pi * cr)
    accumulate(2 * MODES, pr * pr + pi * pi)
    return tr, ti


def moving_terms(batch, offs, tiles, probe, amp, gout, gin, z, tabs):
    lane = lanes((N, N))
    for n, p in enumerate(MOVING):
        r0, t, s = spot(offs, (1, 1), batch, p)
        rows = pl.ds(r0, N)
        back = lax.bitwise_and(128 - s, 127)
        after = jnp.minimum(t + 1, 2)

        def cut(ch):
            one = pltpu.roll(tiles[ch, t, rows], back, 1)
            two = pltpu.roll(tiles[ch, after, rows], back, 1)
            return jnp.where(lane < 128 - s, one, two)

        tr, ti = terms(cut(0), cut(1), probe, amp[batch, p], gout, gin, n == 0, *tabs)
        spread(z.at[n, 0], tr, s)
        spread(z.at[n, 1], ti, s)


def static_terms(batch, tiles, probe, amp, gout, fixed, tabs):
    for p, at, t in STATIC:
        pr, pi = tiles[0, t, at:at + N], tiles[1, t, at:at + N]
        tr, ti = terms(pr, pi, probe, amp[batch, p], gout, None, False, *tabs)
        fixed[p, 0] = tr
        fixed[p, 1] = ti


def light_maps(batch, offs, probe, zl, light):
    row, rows = lax.axis_index("row"), lax.axis_size("row")
    col, cols = lax.axis_index("col"), lax.axis_size("col")
    lane = lanes((N, N))
    total = jnp.zeros((N, N), jnp.float32)
    for m in range(MODES):
        total += probe[0, m] * probe[0, m] + probe[1, m] * probe[1, m]
    blank = jnp.zeros((N, N), jnp.float32)
    slots = zl.shape[0]
    for n in range(slots):
        for j in range(2):
            zl[n, j, 0:N] = blank
            zl[n, j, 2 * N:] = blank

    def there(yes):
        return yes.astype(jnp.float32)

    up, down, left, right = there(row > 0), there(row < rows - 1), there(col > 0), there(col < cols - 1)
    corner = {(0, 0): 1.0 + up * left, (0, 2): right + up, (2, 0): down + left, (2, 2): 1.0 + down * right}
    sums = {}
    for i in (0, 2):
        sums[i] = total * jnp.where(lane < HALF, corner[i, 2], corner[i, 0])
    light[1, 0:N] = sums[0]
    light[1, N:2 * N] = blank
    light[1, 2 * N:] = sums[2]
    for i in range(3):
        light[0, i * N:i * N + N] = blank

    n = 0
    for cr in range(3):
        for rr in range(3):
            for p in MOVING:
                r0, t, s = spot(offs, (cr, rr), batch, p)
                buf = zl.at[n % slots]
                n += 1
                spread(buf, total, s)
                for i in {0: (0,), 1: (0, 1, 2), 2: (2,)}[rr]:
                    w = slice(i * N, i * N + N)
                    if cr == 0:
                        light[1, w] += jnp.where(lane < HALF, 0.0, window(buf, r0, t, i, 0))
                    elif cr == 2:
                        light[1, w] += jnp.where(lane < HALF, window(buf, r0, t, i, 2), 0.0)
                    else:
                        light[0, w] += window(buf, r0, t, i, 1)
                        light[1, w] += jnp.where(lane < HALF, window(buf, r0, t, i, 2), window(buf, r0, t, i, 0))
    place = lax.broadcasted_iota(jnp.int32, (PADROWS, N), 0)
    low = jnp.where(row == 0, HALF, 0)
    high = jnp.where(row == rows - 1, HALF + TILE, PADROWS)
    inside = (place >= low) & (place < high)
    for j in range(2):
        light[j] = jnp.where(inside, 1.0 / (light[j] + OBJECT_REG), 0.0)


TILES = 144
HALFT = 72
PART = 36
SPLITS = (("y", 4, 9, "x", 4, 3), ("x", 4, 9, "y", 4, 3))


class Mates:
    def __init__(self):
        self.row, self.col = lax.axis_index("row"), lax.axis_index("col")
        self.x, self.y = self.row // 4, self.col // 4
        self.z = self.row % 4 * 2 + self.col // 2 % 2
        self.core = self.col % 2
        self.partner = {"row": self.row, "col": self.col + 1 - 2 * self.core}

    def at(self, axis, d):
        if axis == "y":
            k = lax.rem(self.y + d, 4)
            return k, {"row": self.row, "col": k * 4 + self.col % 4}
        if axis == "x":
            k = lax.rem(self.x + d, 4)
            return k, {"row": k * 4 + self.row % 4, "col": self.col}
        k = lax.rem(self.z + d, 8)
        return k, {"row": self.x * 4 + k // 2, "col": self.y * 4 + k % 2 * 2 + self.core}

    def everyone(self):
        return ([self.partner] + [self.at("y", d)[1] for d in range(1, 4)]
                + [self.at("x", d)[1] for d in range(1, 4)] + [self.at("z", d)[1] for d in range(1, 8)])


def reduce_part(part, mates, g, whole, bufs):
    axis1, n1, p1, axis2, n2, p2 = SPLITS[part]
    r1, s1, r2, s2, r3, z, fin, ag1, ag2, send, recv = bufs
    count = iter(range(100))
    every = []

    def go(src, dst, device):
        i = next(count)
        c = pltpu.make_async_remote_copy(
            src_ref=src, dst_ref=dst, send_sem=send.at[i], recv_sem=recv.at[i],
            device_id=device, device_id_type=MESH)
        c.start()
        every.append(c)
        return c

    def scatter(src, slots, axis, n, p):
        cs = []
        for d in range(1, n):
            k, device = mates.at(axis, d)
            cs.append(go(src.at[pl.ds(k * p, p)], slots.at[d - 1], device))
        return cs

    def collect(src, slots, axis, p, cs):
        acc = src[pl.ds(mates.at(axis, 0)[0] * p, p)]
        for d, c in enumerate(cs):
            c.wait_recv()
            acc = acc + slots[d]
        return acc

    def gather(src, dst, axis, n, p):
        me = pl.ds(mates.at(axis, 0)[0] * p, p)
        cs = [go(src, dst.at[me], mates.at(axis, d)[1]) for d in range(1, n)]
        dst[me] = src[...]
        return cs

    core = mates.core
    if s1.shape[0] > PART:
        s1[pl.ds(PART, s1.shape[0] - PART)] = jnp.zeros((s1.shape[0] - PART, 8, N), jnp.float32)
    s2[pl.ds(p1, s2.shape[0] - p1)] = jnp.zeros((s2.shape[0] - p1, 8, N), jnp.float32)
    c = go(g.at[pl.ds((1 - core) * HALFT + part * PART, PART)], r1, mates.partner)
    yield
    c.wait_recv()
    s1[pl.ds(0, PART)] = g[pl.ds(core * HALFT + part * PART, PART)] + r1[...]
    cs = scatter(s1, r2, axis1, n1, p1)
    yield
    s2[pl.ds(0, p1)] = collect(s1, r2, axis1, p1, cs)
    cs = scatter(s2, r3, axis2, n2, p2)
    yield
    z[0] = collect(s2, r3, axis2, p2, cs)
    cs = [go(z.at[0], z.at[d], mates.at("z", d)[1]) for d in range(1, 8)]
    yield
    for c in cs:
        c.wait_recv()
    acc = z[lax.rem(mates.z, 8)]
    for k in range(1, 8):
        acc = acc + z[lax.rem(mates.z - k + 8, 8)]
    fin[...] = acc
    cs = gather(fin, ag1, axis2, n2, p2)
    yield
    for c in cs:
        c.wait_recv()
    cs = gather(ag1.at[pl.ds(0, p1)], ag2, axis1, n1, p1)
    yield
    for c in cs:
        c.wait_recv()
    mine = pl.ds(core * HALFT + part * PART, PART)
    c = go(ag2.at[pl.ds(0, PART)], whole.at[mine], mates.partner)
    whole[mine] = ag2[pl.ds(0, PART)]
    yield
    c.wait_recv()
    for c in every:
        c.wait_send()
    yield


PART_REFS = 11


def reduction_scratch():
    f = jnp.float32
    shape = lambda *n: pltpu.VMEM(n + (8, N), f)
    refs = [shape(TILES)]
    for _, n1, p1, _, n2, p2 in SPLITS:
        refs += [shape(PART), shape(n1 * p1), shape(n1 - 1, p1), shape(n2 * p2), shape(n2 - 1, p2),
                 shape(8, p2), shape(p2), shape(n2 * p2), shape(n1 * p1),
                 pltpu.SemaphoreType.DMA((21,)), pltpu.SemaphoreType.DMA((21,))]
    return refs


def batch_kernel(batch, last, offs, tiles, *rest):
    tabs, (amp, probe), rest = rest[:4], rest[4:6], rest[6:]
    gin = None
    if batch:
        gin, *rest = rest
    others, parts = (), ()
    if last:
        fresh, whole_out, gout, flat, z, fixed, zl, light, ls, rs, ls_in, rs_in, me, from_up, from_down, send, recv, whole, *more = rest
        mates = Mates()
        others = mates.everyone()
        parts = [reduce_part(k, mates, flat, whole, more[k * PART_REFS:(k + 1) * PART_REFS]) for k in range(2)]
        reach = HALF
    else:
        out, gout, z, fixed, zl, light, ls, rs, ls_in, rs_in, me, fresh, from_up, from_down, sl, sr, hl, hr, send, recv = rest
        reach = N
    up, down, left, right = sides = position()
    clear_missing([(left[0], rs_in), (right[0], ls_in), (up[0], from_up), (down[0], from_down)])
    if not last:
        clear_missing([(left[0], hl), (right[0], hr)])
    greet(sides, others)

    def advance():
        for part in parts:
            next(part)

    blank = jnp.zeros((N, N), jnp.float32)
    for n in range(len(MOVING)):
        for ch in range(2):
            for j in range(2):
                z[n, ch, j, 0:N] = blank
                z[n, ch, j, 2 * N:] = blank
    moving_terms(batch, offs, tiles, probe, amp, gout, gin, z, tabs)
    greeted(sides, others)

    count = iter(range(100))
    every = []

    def link(src, dst, to, source):
        i = next(count)
        c = Link(src, dst, send.at[i], recv.at[i], to, source)
        c.start()
        every.append(c)
        return c

    def gathered(ch, i, k):
        acc = None
        for n, p in enumerate(MOVING):
            r0, t, _ = spot(offs, (1, 1), batch, p)
            w = window(z.at[n, ch], r0, t, i, k)
            acc = w if acc is None else acc + w
        for p, at, tile in STATIC:
            if (at, tile) == (i * N, k):
                acc = acc + fixed[p, ch]
        return acc

    lane = lanes((N, N))
    cols = {}
    row_links = {}

    def side_strips(i):
        w = slice(i * N, i * N + N)
        t0 = [gathered(ch, i, 0) for ch in range(2)]
        t2 = [gathered(ch, i, 2) for ch in range(2)]
        ls[w] = jnp.where(lane < HALF, t0[0], turn(t0[1]))
        rs[w] = jnp.where(lane < HALF, turn(t2[0]), t2[1])
        for ch in range(2):
            me[1, ch, w] = jnp.where(lane < HALF, t2[ch], t0[ch])

    def send_cols(at, size):
        d = pl.ds(at, size)
        cols[at] = [link(ls.at[d], ls_in.at[d], left, right), link(rs.at[d], rs_in.at[d], right, left)]

    def middle(i):
        for ch in range(2):
            me[0, ch, i * N:i * N + N] = gathered(ch, i, 1)

    def send_rows(which, top, at, size):
        base = 0 if top else PADROWS - reach
        src, dst = pl.ds(at, size), pl.ds(at - base, size)
        if top:
            c = link(me.at[which, :, src, :], from_down.at[which, :, dst, :], up, down)
        else:
            c = link(me.at[which, :, src, :], from_up.at[which, :, dst, :], down, up)
        row_links[which, top, at - base] = c

    def fold_cols(at, size):
        for c in cols[at]:
            c.arrived()
        w = slice(at, at + size)
        side = lanes((size, N))
        a, b = ls_in[w], rs_in[w]
        me[1, 0, w] += jnp.where(side < HALF, a, turn(b))
        me[1, 1, w] += jnp.where(side < HALF, turn(a), b)

    middle(0)
    send_rows(0, True, 0, reach)
    middle(2)
    send_rows(0, False, PADROWS - reach, reach)
    side_strips(1)
    send_cols(N, N)
    static_terms(batch, tiles, probe, amp, gout, fixed, tabs)
    if last:
        flat[...] = gout[...].reshape(TILES, 8, N)
    advance()
    order = ((0, True), (320, False), (64, True), (256, False))
    for i in (0, 2):
        side_strips(i)
        if i == 0:
            send_cols(0, HALF)
    send_cols(320, HALF)
    send_cols(64, HALF)
    send_cols(256, HALF)
    advance()
    middle(1)
    light_maps(batch, offs, probe, zl, light)
    for at, top in order:
        fold_cols(at, HALF)
        if not last or at in (0, 320):
            send_rows(1, top, at, HALF)
    advance()
    fold_cols(N, N)
    halos = []

    def update(which, at, size, extra):
        w = slice(at, at + size)
        lv = light[which, w]
        mine = lanes((size, N))
        for ch in range(2):
            t = me[which, ch, w]
            if extra is not None:
                t = t + extra[ch]
            old = tiles[ch, 1, w] if which == 0 else jnp.where(mine < HALF, tiles[ch, 2, w], tiles[ch, 0, w])
            fresh[which, ch, w] = old + t * lv

    def halo(at, size):
        if last:
            return
        w = slice(at, at + size)
        a, b = halo_strips(fresh[1, 0, w], fresh[1, 1, w])
        sl[w] = a
        sr[w] = b
        d = pl.ds(at, size)
        halos.extend([link(sl.at[d], hr.at[d], left, right), link(sr.at[d], hl.at[d], right, left)])

    update(1, N, N, None)
    halo(N, N)
    update(0, N, N, None)
    advance()
    if last:
        row_links[1, False, 0].arrived()
        update(1, HALF, HALF, from_up.at[1])
        row_links[1, True, 0].arrived()
        update(1, 256, HALF, from_down.at[1])
        row_links[0, False, 0].arrived()
        update(0, HALF, HALF, from_up.at[0])
        row_links[0, True, 0].arrived()
        update(0, 256, HALF, from_down.at[0])
        for _ in range(4):
            advance()
        whole_out[...] = whole[...]
    else:
        for top, at in ((True, 0), (False, 64), (True, 64), (False, 0)):
            row_links[1, top, at].arrived()
            source, base = (from_down, 2 * N) if top else (from_up, 0)
            update(1, base + at, HALF, source.at[1, :, pl.ds(at, HALF), :])
            halo(base + at, HALF)
        row_links[0, False, 0].arrived()
        update(0, 0, N, from_up.at[0])
        row_links[0, True, 0].arrived()
        update(0, 2 * N, N, from_down.at[0])
        for ch in range(2):
            out[ch, 1] = fresh[0, ch]
        for c in halos:
            c.arrived()
        finish_tiles(out, fresh, hl, hr)
    for c in every:
        c.sent()


def run_batch(batch, last, offs, tiles, others, gin):
    f = jnp.float32
    strip = pltpu.VMEM((PADROWS, N), f)
    sums = jax.ShapeDtypeStruct((2 * MODES + 1, N, N), f)
    reach = HALF if last else N
    if last:
        shapes = (jax.ShapeDtypeStruct((2, 2, PADROWS, N), f), jax.ShapeDtypeStruct((TILES, 8, N), f))
        extra = [pltpu.VMEM((2 * MODES + 1, N, N), f), pltpu.VMEM((TILES, 8, N), f)]
    else:
        shapes = (jax.ShapeDtypeStruct((2, 3, PADROWS, N), f), sums)
        extra = []
    return pl.pallas_call(
        functools.partial(batch_kernel, batch, last),
        out_shape=shapes,
        in_specs=[SM] + [VM] * (1 + len(others) + len(gin)),
        out_specs=(VM,) * len(shapes),
        scratch_shapes=extra + [
            pltpu.VMEM((len(MOVING), 2, 2, PADROWS, N), f),
            pltpu.VMEM((len(STATIC), 2, N, N), f),
            pltpu.VMEM((3, 2, PADROWS, N), f),
            pltpu.VMEM((2, PADROWS, N), f),
            strip, strip, strip, strip,
            pltpu.VMEM((2, 2, PADROWS, N), f),
        ] + ([] if last else [pltpu.VMEM((2, 2, PADROWS, N), f)]) + [
            pltpu.VMEM((2, 2, reach, N), f),
            pltpu.VMEM((2, 2, reach, N), f),
        ] + ([] if last else [strip] * 4) + [
            pltpu.SemaphoreType.DMA((26,)),
            pltpu.SemaphoreType.DMA((26,)),
        ] + (reduction_scratch() if last else []),
        compiler_params=pltpu.CompilerParams(
            collective_id=1 + batch, has_side_effects=True, vmem_limit_bytes=36 * 2**20),
        name=f"batch{batch}",
    )(offs, tiles, *others, *gin)


def final_kernel(fresh, whole, out, step_out):
    wide = lanes((TILE, N))
    w = slice(HALF, HALF + TILE)
    for ch in range(2):
        m, e = fresh[0, ch, w], fresh[1, ch, w]
        out[ch, :, 0:128] = turn(jnp.where(wide < HALF, m, e))
        out[ch, :, 128:256] = turn(jnp.where(wide < HALF, e, m))
    inv = lax.rsqrt(whole[pl.ds(128, 16)] + PROBE_REG)
    for k in range(8):
        step_out[pl.ds(16 * k, 16)] = whole[pl.ds(16 * k, 16)] * inv


def run_final(fresh, whole):
    return pl.pallas_call(
        final_kernel,
        out_shape=(jax.ShapeDtypeStruct((2, TILE, TILE), jnp.float32), jax.ShapeDtypeStruct((128, 8, N), jnp.float32)),
        in_specs=[VM, VM],
        out_specs=(VM, VM),
        compiler_params=pltpu.CompilerParams(vmem_limit_bytes=8 * 2**20),
        name="final",
    )(fresh, whole)


def on_device(object_field, probe, amplitudes, offsets):
    mine = jnp.swapaxes(offsets, 3, 4).reshape(BATCHES, 2, POS)
    amps = amplitudes.reshape(BATCHES, POS, N, N)
    tabs = [jnp.asarray(t) for t in tables()]
    keep = lambda a: pltpu.with_memory_space_constraint(a, pltpu.HBM)
    tiles, offs, *others = run_first(keep(object_field), keep(mine), [keep(a) for a in (*tabs, amps, probe)])
    grads = ()
    for b in range(BATCHES - 1):
        tiles, sums = run_batch(b, False, offs, tiles, others, grads)
        grads = (sums,)
    obj, step = run_final(*run_batch(BATCHES - 1, True, offs, tiles, others, grads))
    return obj, step.reshape(2, MODES, N, N)


def solution(mesh):
    placed = (
        P(None, "row", "col"),
        P(),
        P("row", "col", None, None, None, None),
        P("row", "col", None, None, None),
    )
    return jax.shard_map(
        on_device,
        mesh=mesh,
        in_specs=placed,
        out_specs=(P(None, "row", "col"), P()),
        check_vma=False,
    )
```

```python
import functools
import math

import jax
import jax.numpy as jnp
import ml_dtypes
import numpy as np
from jax import lax
from jax.experimental import pallas as pl
from jax.experimental.pallas import tpu as pltpu
from jax.sharding import PartitionSpec as P

N = 128
MODES = 4
TILE = 256
POS = 4
BATCHES = 3
HALF = 64
PADROWS = 384
FAR = 100000

AMP_FLOOR = 0.25
OBJECT_REG = 0.5
PROBE_REG = 1.0

MESH = pl.DeviceIdType.MESH
VM = pl.BlockSpec(memory_space=pltpu.VMEM)
SM = pl.BlockSpec(memory_space=pltpu.SMEM)


def tables():
    k = np.arange(N)
    ang = (k[:, None] * k[None, :] % N) * (2.0 * math.pi / N)
    fr, fi = np.cos(ang) / math.sqrt(N), -np.sin(ang) / math.sqrt(N)
    a = np.block([[fr, fi], [-fi, fr]])
    b = np.block([[fr, -fi], [fi, fr]])

    def split(m):
        hi = m.astype(np.float32).astype(ml_dtypes.bfloat16)
        lo = (m - hi.astype(np.float64)).astype(np.float32).astype(ml_dtypes.bfloat16)
        return hi, lo

    ah, al = split(a)
    bh, bl = split(b)
    return ah, al, bh, bl


def lanes(shape):
    return lax.broadcasted_iota(jnp.int32, shape, 1)


def split_hi_lo(x):
    hi = x.astype(jnp.bfloat16)
    lo = (x - hi.astype(jnp.float32)).astype(jnp.bfloat16)
    return hi, lo


def dot(a, b):
    return jnp.dot(a, b, preferred_element_type=jnp.float32)


def right_mul(x, th, tl):
    hi, lo = split_hi_lo(x)
    return dot(jnp.concatenate([hi, lo, hi], axis=1), jnp.concatenate([th, th, tl], axis=0))


def left_mul(th, tl, x):
    hi, lo = split_hi_lo(x)
    return dot(jnp.concatenate([th, th, tl], axis=1), jnp.concatenate([hi, lo, hi], axis=0))


def position():
    row, col = lax.axis_index("row"), lax.axis_index("col")
    rows, cols = lax.axis_size("row"), lax.axis_size("col")
    up = (row > 0, {"row": jnp.maximum(row - 1, 0), "col": col})
    down = (row < rows - 1, {"row": jnp.minimum(row + 1, rows - 1), "col": col})
    left = (col > 0, {"row": row, "col": jnp.maximum(col - 1, 0)})
    right = (col < cols - 1, {"row": row, "col": jnp.minimum(col + 1, cols - 1)})
    return up, down, left, right


def greet(sides, others=()):
    barrier = pltpu.get_barrier_semaphore()
    for there, device in sides:
        @pl.when(there)
        def _(device=device):
            pl.semaphore_signal(barrier, inc=1, device_id=device, device_id_type=MESH)
    for device in others:
        pl.semaphore_signal(barrier, inc=1, device_id=device, device_id_type=MESH)


def greeted(sides, others=()):
    barrier = pltpu.get_barrier_semaphore()
    pl.semaphore_wait(barrier, sum(there.astype(jnp.int32) for there, _ in sides) + len(others))


class Link:
    def __init__(self, src, dst, send, recv, to, source):
        self.there, device = to
        self.source = source[0]
        self.copy = pltpu.make_async_remote_copy(
            src_ref=src, dst_ref=dst, send_sem=send, recv_sem=recv,
            device_id=device, device_id_type=MESH)

    def start(self):
        @pl.when(self.there)
        def _():
            self.copy.start()

    def arrived(self):
        @pl.when(self.source)
        def _():
            self.copy.wait_recv()

    def sent(self):
        @pl.when(self.there)
        def _():
            self.copy.wait_send()


def clear_missing(pairs):
    for there, ref in pairs:
        @pl.when(jnp.logical_not(there))
        def _(ref=ref):
            ref[...] = jnp.zeros(ref.shape, ref.dtype)


def turn(x):
    return pltpu.roll(x, HALF, 1)


def halo_strips(re, im):
    lane = lanes(re.shape)
    ti = turn(im)
    return jnp.where(lane < HALF, ti, re), jnp.where(lane < HALF, re, ti)


def first_kernel(obj_hbm, offs, *rest):
    far_refs, rest = rest[:6], rest[6:]
    out, offs_out, *near_refs = rest[:8]
    obj, me, sl, sr, hl, hr, table, send, recv, local = rest[8:]
    up, down, left, right = position()
    load = pltpu.make_async_copy(obj_hbm, obj, local.at[0])
    load.start()
    loads = [pltpu.make_async_copy(a, b, local.at[i + 1]) for i, (a, b) in enumerate(zip(far_refs, near_refs))]
    for c in loads:
        c.start()
    lane = lanes((TILE, N))
    for cr in range(3):
        for rr in range(3):
            if (cr, rr) != (1, 1):
                table[cr, rr] = jnp.full(table.shape[2:], FAR, jnp.int32)
    own_offs = pltpu.make_async_copy(offs, table.at[1, 1], local.at[7])
    own_offs.start()
    clear_missing([(left[0], hl), (right[0], hr),
                   (up[0], me.at[:, :, pl.ds(0, HALF), :]),
                   (down[0], me.at[:, :, pl.ds(PADROWS - HALF, HALF), :])])
    greet((up, down, left, right))
    own = slice(HALF, HALF + TILE)
    load.wait()
    for ch in range(2):
        a, b = turn(obj[ch, :, 0:128]), turn(obj[ch, :, 128:256])
        me[1, ch, own] = jnp.where(lane < HALF, b, a)
        me[0, ch, own] = jnp.where(lane < HALF, a, b)
    own_offs.wait()
    greeted((up, down, left, right))

    count = iter(range(100))

    def link(src, dst, to, source):
        i = next(count)
        return Link(src, dst, send.at[i], recv.at[i], to, source)

    def rows(which):
        top, bottom = pl.ds(HALF, HALF), pl.ds(TILE, HALF)
        above, below = pl.ds(0, HALF), pl.ds(PADROWS - HALF, HALF)
        return [link(me.at[which, :, top, :], me.at[which, :, below, :], up, down),
                link(me.at[which, :, bottom, :], me.at[which, :, above, :], down, up)]

    def cols(at, size):
        w = slice(at, at + size)
        a, b = halo_strips(me[1, 0, w], me[1, 1, w])
        sl[w] = a
        sr[w] = b
        d = pl.ds(at, size)
        both = [link(sl.at[d], hr.at[d], left, right), link(sr.at[d], hl.at[d], right, left)]
        for c in both:
            c.start()
        return both

    tell = [link(table.at[1, 1], table.at[1, 2], up, down),
            link(table.at[1, 1], table.at[1, 0], down, up)]
    edge = rows(1)
    middle = rows(0)
    for c in tell + edge:
        c.start()
    late = cols(HALF, TILE)
    for c in middle:
        c.start()
    for c in tell:
        c.arrived()
    more = [link(table.at[1], table.at[2], left, right),
            link(table.at[1], table.at[0], right, left)]
    for c in more:
        c.start()
    late += more
    edge[1].arrived()
    late += cols(0, HALF)
    edge[0].arrived()
    late += cols(PADROWS - HALF, HALF)
    for c in middle:
        c.arrived()
    for ch in range(2):
        out[ch, 1] = me[0, ch]
    for c in late:
        c.arrived()
    finish_tiles(out, me, hl, hr)
    offs_out[...] = table[...]
    for c in loads:
        c.wait()
    for c in tell + edge + middle + late:
        c.sent()


def finish_tiles(out, me, hl, hr):
    wide = lanes((PADROWS, N))
    out[0, 0] = jnp.where(wide < HALF, hl[...], me[1, 0])
    out[1, 0] = jnp.where(wide < HALF, turn(hl[...]), me[1, 1])
    out[0, 2] = jnp.where(wide < HALF, me[1, 0], hr[...])
    out[1, 2] = jnp.where(wide < HALF, me[1, 1], turn(hr[...]))


def run_first(obj, offs, others):
    f = jnp.float32
    strip = pltpu.VMEM((PADROWS, N), f)
    hbm = pl.BlockSpec(memory_space=pltpu.HBM)
    return pl.pallas_call(
        first_kernel,
        out_shape=(
            jax.ShapeDtypeStruct((2, 3, PADROWS, N), f),
            jax.ShapeDtypeStruct((3, 3, BATCHES, 2, POS), jnp.int32),
        ) + tuple(jax.ShapeDtypeStruct(a.shape, a.dtype) for a in others),
        in_specs=[hbm] * 8,
        out_specs=(VM,) * 8,
        scratch_shapes=[
            pltpu.VMEM((2, TILE, TILE), f),
            pltpu.VMEM((2, 2, PADROWS, N), f),
            strip, strip, strip, strip,
            pltpu.VMEM((3, 3, BATCHES, 2, POS), jnp.int32),
            pltpu.SemaphoreType.DMA((14,)),
            pltpu.SemaphoreType.DMA((14,)),
            pltpu.SemaphoreType.DMA((8,)),
        ],
        compiler_params=pltpu.CompilerParams(collective_id=0, has_side_effects=True, vmem_limit_bytes=14 * 2**20),
        name="first",
    )(obj, offs, *others)


def spread(dest, value, s):
    lane = lanes((N, N))
    turned = pltpu.roll(value, s, 1)
    dest[0, N:2 * N] = jnp.where(lane >= s, turned, 0.0)
    dest[1, N:2 * N] = jnp.where(lane < s, turned, 0.0)


def window(src, r0, t, i, k):
    j = k - t
    hit = (j == 0) | (j == 1)
    start = jnp.where(hit, jnp.clip(N + N * i - r0, 0, 2 * N), 0)
    return src[jnp.where(hit, j, 0), pl.ds(start, N)]


STATIC = ((0, 0, 0), (1, 2 * N, 2))
MOVING = (2, 3)


def spot(offs, block, batch, p):
    cr, rr = block
    r0 = offs[cr, rr, batch, 0, p] + (rr - 1) * TILE + HALF
    c0 = offs[cr, rr, batch, 1, p] + (cr - 1) * TILE + HALF
    return r0, lax.shift_right_arithmetic(c0, 7), lax.bitwise_and(c0, 127)


def terms(pr, pi, probe, measured, gout, gin, first, ah, al, bh, bl):
    waves = []
    for m in range(MODES):
        qr, qi = probe[0, m], probe[1, m]
        waves.append(jnp.concatenate([qr * pr - qi * pi, qr * pi + qi * pr], axis=1))
    half = right_mul(jnp.concatenate(waves, axis=0), ah[...], al[...])
    rows_of = [half[m * N:(m + 1) * N] for m in range(MODES)]
    stacked = jnp.concatenate(
        [jnp.concatenate([h[:, :N] for h in rows_of], axis=1),
         jnp.concatenate([h[:, N:] for h in rows_of], axis=1)], axis=0)
    far = left_mul(bh[...], bl[...], stacked)
    inten = jnp.zeros((N, N), jnp.float32)
    for m in range(MODES):
        fr, fi = far[:N, m * N:(m + 1) * N], far[N:, m * N:(m + 1) * N]
        inten += fr * fr + fi * fi
    factor = measured * lax.rsqrt(jnp.maximum(inten, AMP_FLOOR * AMP_FLOOR)) - 1.0
    factor = jnp.concatenate([factor] * MODES, axis=1)
    factor = jnp.concatenate([factor] * 2, axis=0)
    back_half = left_mul(ah[...], al[...], far * factor)
    lhs = jnp.concatenate(
        [jnp.concatenate([back_half[:N, m * N:(m + 1) * N], back_half[N:, m * N:(m + 1) * N]], axis=1)
         for m in range(MODES)], axis=0)
    change = right_mul(lhs, bh[...], bl[...])
    tr = jnp.zeros((N, N), jnp.float32)
    ti = jnp.zeros((N, N), jnp.float32)

    def accumulate(k, value):
        if not first:
            gout[k] += value
        elif gin is None:
            gout[k] = value
        else:
            gout[k] = gin[k] + value

    for m in range(MODES):
        qr, qi = probe[0, m], probe[1, m]
        cr, ci = change[m * N:(m + 1) * N, :N], change[m * N:(m + 1) * N, N:]
        tr += qr * cr + qi * ci
        ti += qr * ci - qi * cr
        accumulate(m, pr * cr + pi * ci)
        accumulate(MODES + m, pr * ci - pi * cr)
    accumulate(2 * MODES, pr * pr + pi * pi)
    return tr, ti


def moving_terms(batch, offs, tiles, probe, amp, gout, gin, z, tabs):
    lane = lanes((N, N))
    for n, p in enumerate(MOVING):
        r0, t, s = spot(offs, (1, 1), batch, p)
        rows = pl.ds(r0, N)
        back = lax.bitwise_and(128 - s, 127)
        after = jnp.minimum(t + 1, 2)

        def cut(ch):
            one = pltpu.roll(tiles[ch, t, rows], back, 1)
            two = pltpu.roll(tiles[ch, after, rows], back, 1)
            return jnp.where(lane < 128 - s, one, two)

        tr, ti = terms(cut(0), cut(1), probe, amp[batch, p], gout, gin, n == 0, *tabs)
        spread(z.at[n, 0], tr, s)
        spread(z.at[n, 1], ti, s)


def static_terms(batch, tiles, probe, amp, gout, fixed, tabs):
    for p, at, t in STATIC:
        pr, pi = tiles[0, t, at:at + N], tiles[1, t, at:at + N]
        tr, ti = terms(pr, pi, probe, amp[batch, p], gout, None, False, *tabs)
        fixed[p, 0] = tr
        fixed[p, 1] = ti


def light_maps(batch, offs, probe, zl, light):
    row, rows = lax.axis_index("row"), lax.axis_size("row")
    col, cols = lax.axis_index("col"), lax.axis_size("col")
    lane = lanes((N, N))
    total = jnp.zeros((N, N), jnp.float32)
    for m in range(MODES):
        total += probe[0, m] * probe[0, m] + probe[1, m] * probe[1, m]
    blank = jnp.zeros((N, N), jnp.float32)
    slots = zl.shape[0]
    for n in range(slots):
        for j in range(2):
            zl[n, j, 0:N] = blank
            zl[n, j, 2 * N:] = blank

    def there(yes):
        return yes.astype(jnp.float32)

    up, down, left, right = there(row > 0), there(row < rows - 1), there(col > 0), there(col < cols - 1)
    corner = {(0, 0): 1.0 + up * left, (0, 2): right + up, (2, 0): down + left, (2, 2): 1.0 + down * right}
    sums = {}
    for i in (0, 2):
        sums[i] = total * jnp.where(lane < HALF, corner[i, 2], corner[i, 0])
    light[1, 0:N] = sums[0]
    light[1, N:2 * N] = blank
    light[1, 2 * N:] = sums[2]
    for i in range(3):
        light[0, i * N:i * N + N] = blank

    n = 0
    for cr in range(3):
        for rr in range(3):
            for p in MOVING:
                r0, t, s = spot(offs, (cr, rr), batch, p)
                buf = zl.at[n % slots]
                n += 1
                spread(buf, total, s)
                for i in {0: (0,), 1: (0, 1, 2), 2: (2,)}[rr]:
                    w = slice(i * N, i * N + N)
                    if cr == 0:
                        light[1, w] += jnp.where(lane < HALF, 0.0, window(buf, r0, t, i, 0))
                    elif cr == 2:
                        light[1, w] += jnp.where(lane < HALF, window(buf, r0, t, i, 2), 0.0)
                    else:
                        light[0, w] += window(buf, r0, t, i, 1)
                        light[1, w] += jnp.where(lane < HALF, window(buf, r0, t, i, 2), window(buf, r0, t, i, 0))
    place = lax.broadcasted_iota(jnp.int32, (PADROWS, N), 0)
    low = jnp.where(row == 0, HALF, 0)
    high = jnp.where(row == rows - 1, HALF + TILE, PADROWS)
    inside = (place >= low) & (place < high)
    for j in range(2):
        light[j] = jnp.where(inside, 1.0 / (light[j] + OBJECT_REG), 0.0)


ROWS = 1152
HALFT = 576
PART = 288
SPLITS = (("y", 4, 72, "x", 4, 18), ("x", 4, 72, "y", 4, 18))


class Mates:
    def __init__(self):
        self.row, self.col = lax.axis_index("row"), lax.axis_index("col")
        self.x, self.y = self.row // 4, self.col // 4
        self.z = self.row % 4 * 2 + self.col // 2 % 2
        self.core = self.col % 2
        self.partner = {"row": self.row, "col": self.col + 1 - 2 * self.core}

    def at(self, axis, d):
        if axis == "y":
            k = lax.rem(self.y + d, 4)
            return k, {"row": self.row, "col": k * 4 + self.col % 4}
        if axis == "x":
            k = lax.rem(self.x + d, 4)
            return k, {"row": k * 4 + self.row % 4, "col": self.col}
        k = lax.rem(self.z + d, 8)
        return k, {"row": self.x * 4 + k // 2, "col": self.y * 4 + k % 2 * 2 + self.core}

    def everyone(self):
        return ([self.partner] + [self.at("y", d)[1] for d in range(1, 4)]
                + [self.at("x", d)[1] for d in range(1, 4)] + [self.at("z", d)[1] for d in range(1, 8)])


def reduce_part(part, mates, g, whole, bufs):
    axis1, n1, p1, axis2, n2, p2 = SPLITS[part]
    r1, s1, r2, s2, r3, z, fin, ag1, ag2, send, recv = bufs
    count = iter(range(100))
    every = []

    def go(src, dst, device):
        i = next(count)
        c = pltpu.make_async_remote_copy(
            src_ref=src, dst_ref=dst, send_sem=send.at[i], recv_sem=recv.at[i],
            device_id=device, device_id_type=MESH)
        c.start()
        every.append(c)
        return c

    def scatter(src, slots, axis, n, p):
        cs = []
        for d in range(1, n):
            k, device = mates.at(axis, d)
            cs.append(go(src.at[pl.ds(k * p, p)], slots.at[d - 1], device))
        return cs

    def collect(src, slots, axis, p, cs):
        acc = src[pl.ds(mates.at(axis, 0)[0] * p, p)]
        for d, c in enumerate(cs):
            c.wait_recv()
            acc = acc + slots[d]
        return acc

    def gather(src, dst, axis, n, p):
        me = pl.ds(mates.at(axis, 0)[0] * p, p)
        cs = [go(src, dst.at[me], mates.at(axis, d)[1]) for d in range(1, n)]
        dst[me] = src[...]
        return cs

    core = mates.core
    c = go(g.at[pl.ds((1 - core) * HALFT + part * PART, PART)], r1, mates.partner)
    yield
    c.wait_recv()
    s1[pl.ds(0, PART)] = g[pl.ds(core * HALFT + part * PART, PART)] + r1[...]
    cs = scatter(s1, r2, axis1, n1, p1)
    yield
    s2[pl.ds(0, p1)] = collect(s1, r2, axis1, p1, cs)
    cs = scatter(s2, r3, axis2, n2, p2)
    yield
    z[0] = collect(s2, r3, axis2, p2, cs)
    cs = [go(z.at[0], z.at[d], mates.at("z", d)[1]) for d in range(1, 8)]
    yield
    for c in cs:
        c.wait_recv()
    acc = z[lax.rem(mates.z, 8)]
    for k in range(1, 8):
        acc = acc + z[lax.rem(mates.z - k + 8, 8)]
    fin[...] = acc
    cs = gather(fin, ag1, axis2, n2, p2)
    yield
    for c in cs:
        c.wait_recv()
    cs = gather(ag1.at[pl.ds(0, p1)], ag2, axis1, n1, p1)
    yield
    for c in cs:
        c.wait_recv()
    mine = pl.ds(core * HALFT + part * PART, PART)
    c = go(ag2.at[pl.ds(0, PART)], whole.at[mine], mates.partner)
    whole[mine] = ag2[pl.ds(0, PART)]
    yield
    c.wait_recv()
    for c in every:
        c.wait_send()
    yield


PART_REFS = 11


def reduction_scratch():
    f = jnp.float32
    shape = lambda *n: pltpu.VMEM(n + (N,), f)
    refs = [shape(ROWS)]
    for _, n1, p1, _, n2, p2 in SPLITS:
        refs += [shape(PART), shape(n1 * p1), shape(n1 - 1, p1), shape(n2 * p2), shape(n2 - 1, p2),
                 shape(8, p2), shape(p2), shape(n2 * p2), shape(n1 * p1),
                 pltpu.SemaphoreType.DMA((21,)), pltpu.SemaphoreType.DMA((21,))]
    return refs


def batch_kernel(batch, last, offs, tiles, *rest):
    tabs, (amp, probe), rest = rest[:4], rest[4:6], rest[6:]
    gin = None
    if batch:
        gin, *rest = rest
    others, parts = (), ()
    if last:
        fresh, whole_out, gout, flat, z, fixed, zl, light, ls, rs, ls_in, rs_in, me, from_up, from_down, send, recv, whole, *more = rest
        mates = Mates()
        others = mates.everyone()
        parts = [reduce_part(k, mates, flat, whole, more[k * PART_REFS:(k + 1) * PART_REFS]) for k in range(2)]
        reach = HALF
    else:
        out, gout, z, fixed, zl, light, ls, rs, ls_in, rs_in, me, fresh, from_up, from_down, sl, sr, hl, hr, send, recv = rest
        reach = N
    up, down, left, right = sides = position()
    clear_missing([(left[0], rs_in), (right[0], ls_in), (up[0], from_up), (down[0], from_down)])
    if not last:
        clear_missing([(left[0], hl), (right[0], hr)])
    greet(sides, others)

    def advance():
        for part in parts:
            next(part)

    blank = jnp.zeros((N, N), jnp.float32)
    for n in range(len(MOVING)):
        for ch in range(2):
            for j in range(2):
                z[n, ch, j, 0:N] = blank
                z[n, ch, j, 2 * N:] = blank
    moving_terms(batch, offs, tiles, probe, amp, gout, gin, z, tabs)
    greeted(sides, others)

    count = iter(range(100))
    every = []

    def link(src, dst, to, source):
        i = next(count)
        c = Link(src, dst, send.at[i], recv.at[i], to, source)
        c.start()
        every.append(c)
        return c

    def gathered(ch, i, k):
        acc = None
        for n, p in enumerate(MOVING):
            r0, t, _ = spot(offs, (1, 1), batch, p)
            w = window(z.at[n, ch], r0, t, i, k)
            acc = w if acc is None else acc + w
        for p, at, tile in STATIC:
            if (at, tile) == (i * N, k):
                acc = acc + fixed[p, ch]
        return acc

    lane = lanes((N, N))
    cols = {}
    row_links = {}

    def side_strips(i):
        w = slice(i * N, i * N + N)
        t0 = [gathered(ch, i, 0) for ch in range(2)]
        t2 = [gathered(ch, i, 2) for ch in range(2)]
        ls[w] = jnp.where(lane < HALF, t0[0], turn(t0[1]))
        rs[w] = jnp.where(lane < HALF, turn(t2[0]), t2[1])
        for ch in range(2):
            me[1, ch, w] = jnp.where(lane < HALF, t2[ch], t0[ch])

    def send_cols(at, size):
        d = pl.ds(at, size)
        cols[at] = [link(ls.at[d], ls_in.at[d], left, right), link(rs.at[d], rs_in.at[d], right, left)]

    def middle(i):
        for ch in range(2):
            me[0, ch, i * N:i * N + N] = gathered(ch, i, 1)

    def send_rows(which, top, at, size):
        base = 0 if top else PADROWS - reach
        src, dst = pl.ds(at, size), pl.ds(at - base, size)
        if top:
            c = link(me.at[which, :, src, :], from_down.at[which, :, dst, :], up, down)
        else:
            c = link(me.at[which, :, src, :], from_up.at[which, :, dst, :], down, up)
        row_links[which, top, at - base] = c

    def fold_cols(at, size):
        for c in cols[at]:
            c.arrived()
        w = slice(at, at + size)
        side = lanes((size, N))
        a, b = ls_in[w], rs_in[w]
        me[1, 0, w] += jnp.where(side < HALF, a, turn(b))
        me[1, 1, w] += jnp.where(side < HALF, turn(a), b)

    if last:
        static_terms(batch, tiles, probe, amp, gout, fixed, tabs)
        flat[...] = gout[...].reshape(ROWS, N)
        advance()
    middle(0)
    send_rows(0, True, 0, reach)
    middle(2)
    send_rows(0, False, PADROWS - reach, reach)
    if last:
        advance()
    side_strips(1)
    send_cols(N, N)
    if not last:
        static_terms(batch, tiles, probe, amp, gout, fixed, tabs)
    order = ((0, True), (320, False), (64, True), (256, False))
    for i in (0, 2):
        side_strips(i)
        if i == 0:
            send_cols(0, HALF)
    send_cols(320, HALF)
    send_cols(64, HALF)
    send_cols(256, HALF)
    middle(1)
    light_maps(batch, offs, probe, zl, light)
    for at, top in order:
        fold_cols(at, HALF)
        if not last or at in (0, 320):
            send_rows(1, top, at, HALF)
    advance()
    fold_cols(N, N)
    halos = []

    def update(which, at, size, extra):
        w = slice(at, at + size)
        lv = light[which, w]
        mine = lanes((size, N))
        for ch in range(2):
            t = me[which, ch, w]
            if extra is not None:
                t = t + extra[ch]
            old = tiles[ch, 1, w] if which == 0 else jnp.where(mine < HALF, tiles[ch, 2, w], tiles[ch, 0, w])
            fresh[which, ch, w] = old + t * lv

    def halo(at, size):
        if last:
            return
        w = slice(at, at + size)
        a, b = halo_strips(fresh[1, 0, w], fresh[1, 1, w])
        sl[w] = a
        sr[w] = b
        d = pl.ds(at, size)
        halos.extend([link(sl.at[d], hr.at[d], left, right), link(sr.at[d], hl.at[d], right, left)])

    update(1, N, N, None)
    halo(N, N)
    update(0, N, N, None)
    advance()
    if last:
        row_links[1, False, 0].arrived()
        update(1, HALF, HALF, from_up.at[1])
        row_links[1, True, 0].arrived()
        update(1, 256, HALF, from_down.at[1])
        row_links[0, False, 0].arrived()
        update(0, HALF, HALF, from_up.at[0])
        row_links[0, True, 0].arrived()
        update(0, 256, HALF, from_down.at[0])
        for _ in range(4):
            advance()
        whole_out[...] = whole[...]
    else:
        for top, at in ((True, 0), (False, 64), (True, 64), (False, 0)):
            row_links[1, top, at].arrived()
            source, base = (from_down, 2 * N) if top else (from_up, 0)
            update(1, base + at, HALF, source.at[1, :, pl.ds(at, HALF), :])
            halo(base + at, HALF)
        row_links[0, False, 0].arrived()
        update(0, 0, N, from_up.at[0])
        row_links[0, True, 0].arrived()
        update(0, 2 * N, N, from_down.at[0])
        for ch in range(2):
            out[ch, 1] = fresh[0, ch]
        for c in halos:
            c.arrived()
        finish_tiles(out, fresh, hl, hr)
    for c in every:
        c.sent()


def run_batch(batch, last, offs, tiles, others, gin):
    f = jnp.float32
    strip = pltpu.VMEM((PADROWS, N), f)
    sums = jax.ShapeDtypeStruct((2 * MODES + 1, N, N), f)
    reach = HALF if last else N
    if last:
        shapes = (jax.ShapeDtypeStruct((2, 2, PADROWS, N), f), jax.ShapeDtypeStruct((ROWS, N), f))
        extra = [pltpu.VMEM((2 * MODES + 1, N, N), f), pltpu.VMEM((ROWS, N), f)]
    else:
        shapes = (jax.ShapeDtypeStruct((2, 3, PADROWS, N), f), sums)
        extra = []
    return pl.pallas_call(
        functools.partial(batch_kernel, batch, last),
        out_shape=shapes,
        in_specs=[SM] + [VM] * (1 + len(others) + len(gin)),
        out_specs=(VM,) * len(shapes),
        scratch_shapes=extra + [
            pltpu.VMEM((len(MOVING), 2, 2, PADROWS, N), f),
            pltpu.VMEM((len(STATIC), 2, N, N), f),
            pltpu.VMEM((3, 2, PADROWS, N), f),
            pltpu.VMEM((2, PADROWS, N), f),
            strip, strip, strip, strip,
            pltpu.VMEM((2, 2, PADROWS, N), f),
        ] + ([] if last else [pltpu.VMEM((2, 2, PADROWS, N), f)]) + [
            pltpu.VMEM((2, 2, reach, N), f),
            pltpu.VMEM((2, 2, reach, N), f),
        ] + ([] if last else [strip] * 4) + [
            pltpu.SemaphoreType.DMA((26,)),
            pltpu.SemaphoreType.DMA((26,)),
        ] + (reduction_scratch() if last else []),
        compiler_params=pltpu.CompilerParams(
            collective_id=1 + batch, has_side_effects=True, vmem_limit_bytes=36 * 2**20),
        name=f"batch{batch}",
    )(offs, tiles, *others, *gin)


def final_kernel(fresh, whole, out, step_out):
    wide = lanes((TILE, N))
    w = slice(HALF, HALF + TILE)
    for ch in range(2):
        m, e = fresh[0, ch, w], fresh[1, ch, w]
        out[ch, :, 0:128] = turn(jnp.where(wide < HALF, m, e))
        out[ch, :, 128:256] = turn(jnp.where(wide < HALF, e, m))
    inv = lax.rsqrt(whole[pl.ds(2 * MODES * N, N)] + PROBE_REG)
    for k in range(2 * MODES):
        step_out[pl.ds(N * k, N)] = whole[pl.ds(N * k, N)] * inv


def run_final(fresh, whole):
    return pl.pallas_call(
        final_kernel,
        out_shape=(jax.ShapeDtypeStruct((2, TILE, TILE), jnp.float32), jax.ShapeDtypeStruct((2 * MODES * N, N), jnp.float32)),
        in_specs=[VM, VM],
        out_specs=(VM, VM),
        compiler_params=pltpu.CompilerParams(vmem_limit_bytes=8 * 2**20),
        name="final",
    )(fresh, whole)


def on_device(object_field, probe, amplitudes, offsets):
    mine = jnp.swapaxes(offsets, 3, 4).reshape(BATCHES, 2, POS)
    amps = amplitudes.reshape(BATCHES, POS, N, N)
    tabs = [jnp.asarray(t) for t in tables()]
    keep = lambda a: pltpu.with_memory_space_constraint(a, pltpu.HBM)
    tiles, offs, *others = run_first(keep(object_field), keep(mine), [keep(a) for a in (*tabs, amps, probe)])
    grads = ()
    for b in range(BATCHES - 1):
        tiles, sums = run_batch(b, False, offs, tiles, others, grads)
        grads = (sums,)
    obj, step = run_final(*run_batch(BATCHES - 1, True, offs, tiles, others, grads))
    return obj, step.reshape(2, MODES, N, N)


def solution(mesh):
    placed = (
        P(None, "row", "col"),
        P(),
        P("row", "col", None, None, None, None),
        P("row", "col", None, None, None),
    )
    return jax.shard_map(
        on_device,
        mesh=mesh,
        in_specs=placed,
        out_specs=(P(None, "row", "col"), P()),
        check_vma=False,
    )
```

```python
import functools
import math

import jax
import jax.numpy as jnp
import ml_dtypes
import numpy as np
from jax import lax
from jax.experimental import pallas as pl
from jax.experimental.pallas import tpu as pltpu
from jax.sharding import PartitionSpec as P

N = 128
MODES = 4
TILE = 256
POS = 4
BATCHES = 3
HALF = 64
PADROWS = 384
FAR = 100000

AMP_FLOOR = 0.25
OBJECT_REG = 0.5
PROBE_REG = 1.0

MESH = pl.DeviceIdType.MESH
VM = pl.BlockSpec(memory_space=pltpu.VMEM)
SM = pl.BlockSpec(memory_space=pltpu.SMEM)


def tables():
    k = np.arange(N)
    ang = (k[:, None] * k[None, :] % N) * (2.0 * math.pi / N)
    fr, fi = np.cos(ang) / math.sqrt(N), -np.sin(ang) / math.sqrt(N)
    a = np.block([[fr, fi], [-fi, fr]])
    b = np.block([[fr, -fi], [fi, fr]])

    def split(m):
        hi = m.astype(np.float32).astype(ml_dtypes.bfloat16)
        lo = (m - hi.astype(np.float64)).astype(np.float32).astype(ml_dtypes.bfloat16)
        return hi, lo

    ah, al = split(a)
    bh, bl = split(b)
    return ah, al, bh, bl


def lanes(shape):
    return lax.broadcasted_iota(jnp.int32, shape, 1)


def split_hi_lo(x):
    hi = x.astype(jnp.bfloat16)
    lo = (x - hi.astype(jnp.float32)).astype(jnp.bfloat16)
    return hi, lo


def dot(a, b):
    return jnp.dot(a, b, preferred_element_type=jnp.float32)


def right_mul(x, th, tl):
    hi, lo = split_hi_lo(x)
    return dot(jnp.concatenate([hi, lo, hi], axis=1), jnp.concatenate([th, th, tl], axis=0))


def left_mul(th, tl, x):
    hi, lo = split_hi_lo(x)
    return dot(jnp.concatenate([th, th, tl], axis=1), jnp.concatenate([hi, lo, hi], axis=0))


def position():
    row, col = lax.axis_index("row"), lax.axis_index("col")
    rows, cols = lax.axis_size("row"), lax.axis_size("col")
    up = (row > 0, {"row": jnp.maximum(row - 1, 0), "col": col})
    down = (row < rows - 1, {"row": jnp.minimum(row + 1, rows - 1), "col": col})
    left = (col > 0, {"row": row, "col": jnp.maximum(col - 1, 0)})
    right = (col < cols - 1, {"row": row, "col": jnp.minimum(col + 1, cols - 1)})
    return up, down, left, right


def greet(sides, others=()):
    barrier = pltpu.get_barrier_semaphore()
    for there, device in sides:
        @pl.when(there)
        def _(device=device):
            pl.semaphore_signal(barrier, inc=1, device_id=device, device_id_type=MESH)
    for device in others:
        pl.semaphore_signal(barrier, inc=1, device_id=device, device_id_type=MESH)


def greeted(sides, others=()):
    barrier = pltpu.get_barrier_semaphore()
    pl.semaphore_wait(barrier, sum(there.astype(jnp.int32) for there, _ in sides) + len(others))


class Link:
    def __init__(self, src, dst, send, recv, to, source):
        self.there, device = to
        self.source = source[0]
        self.copy = pltpu.make_async_remote_copy(
            src_ref=src, dst_ref=dst, send_sem=send, recv_sem=recv,
            device_id=device, device_id_type=MESH)

    def start(self):
        @pl.when(self.there)
        def _():
            self.copy.start()

    def arrived(self):
        @pl.when(self.source)
        def _():
            self.copy.wait_recv()

    def sent(self):
        @pl.when(self.there)
        def _():
            self.copy.wait_send()


def clear_missing(pairs):
    for there, ref in pairs:
        @pl.when(jnp.logical_not(there))
        def _(ref=ref):
            ref[...] = jnp.zeros(ref.shape, ref.dtype)


def turn(x):
    return pltpu.roll(x, HALF, 1)


def halo_strips(re, im):
    lane = lanes(re.shape)
    ti = turn(im)
    return jnp.where(lane < HALF, ti, re), jnp.where(lane < HALF, re, ti)


def first_kernel(obj_hbm, offs, *rest):
    far_refs, rest = rest[:6], rest[6:]
    out, offs_out, *near_refs = rest[:8]
    obj, me, sl, sr, hl, hr, table, send, recv, local = rest[8:]
    up, down, left, right = position()
    load = pltpu.make_async_copy(obj_hbm, obj, local.at[0])
    load.start()
    loads = [pltpu.make_async_copy(a, b, local.at[i + 1]) for i, (a, b) in enumerate(zip(far_refs, near_refs))]
    for c in loads:
        c.start()
    lane = lanes((TILE, N))
    for cr in range(3):
        for rr in range(3):
            if (cr, rr) != (1, 1):
                table[cr, rr] = jnp.full(table.shape[2:], FAR, jnp.int32)
    own_offs = pltpu.make_async_copy(offs, table.at[1, 1], local.at[7])
    own_offs.start()
    clear_missing([(left[0], hl), (right[0], hr),
                   (up[0], me.at[:, :, pl.ds(0, HALF), :]),
                   (down[0], me.at[:, :, pl.ds(PADROWS - HALF, HALF), :])])
    greet((up, down, left, right))
    own = slice(HALF, HALF + TILE)
    load.wait()
    for ch in range(2):
        a, b = turn(obj[ch, :, 0:128]), turn(obj[ch, :, 128:256])
        me[1, ch, own] = jnp.where(lane < HALF, b, a)
        me[0, ch, own] = jnp.where(lane < HALF, a, b)
    own_offs.wait()
    greeted((up, down, left, right))

    count = iter(range(100))

    def link(src, dst, to, source):
        i = next(count)
        return Link(src, dst, send.at[i], recv.at[i], to, source)

    def rows(which):
        top, bottom = pl.ds(HALF, HALF), pl.ds(TILE, HALF)
        above, below = pl.ds(0, HALF), pl.ds(PADROWS - HALF, HALF)
        return [link(me.at[which, :, top, :], me.at[which, :, below, :], up, down),
                link(me.at[which, :, bottom, :], me.at[which, :, above, :], down, up)]

    def cols(at, size):
        w = slice(at, at + size)
        a, b = halo_strips(me[1, 0, w], me[1, 1, w])
        sl[w] = a
        sr[w] = b
        d = pl.ds(at, size)
        both = [link(sl.at[d], hr.at[d], left, right), link(sr.at[d], hl.at[d], right, left)]
        for c in both:
            c.start()
        return both

    tell = [link(table.at[1, 1], table.at[1, 2], up, down),
            link(table.at[1, 1], table.at[1, 0], down, up)]
    edge = rows(1)
    middle = rows(0)
    for c in tell + edge:
        c.start()
    late = cols(HALF, TILE)
    for c in middle:
        c.start()
    for c in tell:
        c.arrived()
    more = [link(table.at[1], table.at[2], left, right),
            link(table.at[1], table.at[0], right, left)]
    for c in more:
        c.start()
    late += more
    edge[1].arrived()
    late += cols(0, HALF)
    edge[0].arrived()
    late += cols(PADROWS - HALF, HALF)
    for c in middle:
        c.arrived()
    for ch in range(2):
        out[ch, 1] = me[0, ch]
    for c in late:
        c.arrived()
    finish_tiles(out, me, hl, hr)
    offs_out[...] = table[...]
    for c in loads:
        c.wait()
    for c in tell + edge + middle + late:
        c.sent()


def finish_tiles(out, me, hl, hr):
    wide = lanes((PADROWS, N))
    out[0, 0] = jnp.where(wide < HALF, hl[...], me[1, 0])
    out[1, 0] = jnp.where(wide < HALF, turn(hl[...]), me[1, 1])
    out[0, 2] = jnp.where(wide < HALF, me[1, 0], hr[...])
    out[1, 2] = jnp.where(wide < HALF, me[1, 1], turn(hr[...]))


def run_first(obj, offs, others):
    f = jnp.float32
    strip = pltpu.VMEM((PADROWS, N), f)
    hbm = pl.BlockSpec(memory_space=pltpu.HBM)
    return pl.pallas_call(
        first_kernel,
        out_shape=(
            jax.ShapeDtypeStruct((2, 3, PADROWS, N), f),
            jax.ShapeDtypeStruct((3, 3, BATCHES, 2, POS), jnp.int32),
        ) + tuple(jax.ShapeDtypeStruct(a.shape, a.dtype) for a in others),
        in_specs=[hbm] * 8,
        out_specs=(VM,) * 8,
        scratch_shapes=[
            pltpu.VMEM((2, TILE, TILE), f),
            pltpu.VMEM((2, 2, PADROWS, N), f),
            strip, strip, strip, strip,
            pltpu.VMEM((3, 3, BATCHES, 2, POS), jnp.int32),
            pltpu.SemaphoreType.DMA((14,)),
            pltpu.SemaphoreType.DMA((14,)),
            pltpu.SemaphoreType.DMA((8,)),
        ],
        compiler_params=pltpu.CompilerParams(collective_id=0, has_side_effects=True, vmem_limit_bytes=14 * 2**20),
        name="first",
    )(obj, offs, *others)


def spread(dest, value, s):
    lane = lanes((N, N))
    turned = pltpu.roll(value, s, 1)
    dest[0, N:2 * N] = jnp.where(lane >= s, turned, 0.0)
    dest[1, N:2 * N] = jnp.where(lane < s, turned, 0.0)


def window(src, r0, t, i, k):
    j = k - t
    hit = (j == 0) | (j == 1)
    start = jnp.where(hit, jnp.clip(N + N * i - r0, 0, 2 * N), 0)
    return src[jnp.where(hit, j, 0), pl.ds(start, N)]


STATIC = ((0, 0, 0), (1, 2 * N, 2))
MOVING = (2, 3)


def spot(offs, block, batch, p):
    cr, rr = block
    r0 = offs[cr, rr, batch, 0, p] + (rr - 1) * TILE + HALF
    c0 = offs[cr, rr, batch, 1, p] + (cr - 1) * TILE + HALF
    return r0, lax.shift_right_arithmetic(c0, 7), lax.bitwise_and(c0, 127)


def terms(pr, pi, probe, measured, gout, gin, first, ah, al, bh, bl):
    waves = []
    for m in range(MODES):
        qr, qi = probe[0, m], probe[1, m]
        waves.append(jnp.concatenate([qr * pr - qi * pi, qr * pi + qi * pr], axis=1))
    half = right_mul(jnp.concatenate(waves, axis=0), ah[...], al[...])
    rows_of = [half[m * N:(m + 1) * N] for m in range(MODES)]
    stacked = jnp.concatenate(
        [jnp.concatenate([h[:, :N] for h in rows_of], axis=1),
         jnp.concatenate([h[:, N:] for h in rows_of], axis=1)], axis=0)
    far = left_mul(bh[...], bl[...], stacked)
    inten = jnp.zeros((N, N), jnp.float32)
    for m in range(MODES):
        fr, fi = far[:N, m * N:(m + 1) * N], far[N:, m * N:(m + 1) * N]
        inten += fr * fr + fi * fi
    factor = measured * lax.rsqrt(jnp.maximum(inten, AMP_FLOOR * AMP_FLOOR)) - 1.0
    factor = jnp.concatenate([factor] * MODES, axis=1)
    factor = jnp.concatenate([factor] * 2, axis=0)
    back_half = left_mul(ah[...], al[...], far * factor)
    lhs = jnp.concatenate(
        [jnp.concatenate([back_half[:N, m * N:(m + 1) * N], back_half[N:, m * N:(m + 1) * N]], axis=1)
         for m in range(MODES)], axis=0)
    change = right_mul(lhs, bh[...], bl[...])
    tr = jnp.zeros((N, N), jnp.float32)
    ti = jnp.zeros((N, N), jnp.float32)

    def accumulate(k, value):
        if not first:
            gout[k] += value
        elif gin is None:
            gout[k] = value
        else:
            gout[k] = gin[k] + value

    for m in range(MODES):
        qr, qi = probe[0, m], probe[1, m]
        cr, ci = change[m * N:(m + 1) * N, :N], change[m * N:(m + 1) * N, N:]
        tr += qr * cr + qi * ci
        ti += qr * ci - qi * cr
        accumulate(m, pr * cr + pi * ci)
        accumulate(MODES + m, pr * ci - pi * cr)
    accumulate(2 * MODES, pr * pr + pi * pi)
    return tr, ti


def moving_terms(batch, offs, tiles, probe, amp, gout, gin, z, tabs):
    lane = lanes((N, N))
    for n, p in enumerate(MOVING):
        r0, t, s = spot(offs, (1, 1), batch, p)
        rows = pl.ds(r0, N)
        back = lax.bitwise_and(128 - s, 127)
        after = jnp.minimum(t + 1, 2)

        def cut(ch):
            one = pltpu.roll(tiles[ch, t, rows], back, 1)
            two = pltpu.roll(tiles[ch, after, rows], back, 1)
            return jnp.where(lane < 128 - s, one, two)

        tr, ti = terms(cut(0), cut(1), probe, amp[batch, p], gout, gin, n == 0, *tabs)
        spread(z.at[n, 0], tr, s)
        spread(z.at[n, 1], ti, s)


def static_terms(batch, tiles, probe, amp, gout, fixed, tabs):
    for p, at, t in STATIC:
        pr, pi = tiles[0, t, at:at + N], tiles[1, t, at:at + N]
        tr, ti = terms(pr, pi, probe, amp[batch, p], gout, None, False, *tabs)
        fixed[p, 0] = tr
        fixed[p, 1] = ti


def light_maps(batch, offs, probe, zl, light):
    row, rows = lax.axis_index("row"), lax.axis_size("row")
    col, cols = lax.axis_index("col"), lax.axis_size("col")
    lane = lanes((N, N))
    total = jnp.zeros((N, N), jnp.float32)
    for m in range(MODES):
        total += probe[0, m] * probe[0, m] + probe[1, m] * probe[1, m]
    blank = jnp.zeros((N, N), jnp.float32)
    slots = zl.shape[0]
    for n in range(slots):
        for j in range(2):
            zl[n, j, 0:N] = blank
            zl[n, j, 2 * N:] = blank

    def there(yes):
        return yes.astype(jnp.float32)

    up, down, left, right = there(row > 0), there(row < rows - 1), there(col > 0), there(col < cols - 1)
    corner = {(0, 0): 1.0 + up * left, (0, 2): right + up, (2, 0): down + left, (2, 2): 1.0 + down * right}
    sums = {}
    for i in (0, 2):
        sums[i] = total * jnp.where(lane < HALF, corner[i, 2], corner[i, 0])
    light[1, 0:N] = sums[0]
    light[1, N:2 * N] = blank
    light[1, 2 * N:] = sums[2]
    for i in range(3):
        light[0, i * N:i * N + N] = blank

    n = 0
    for cr in range(3):
        for rr in range(3):
            for p in MOVING:
                r0, t, s = spot(offs, (cr, rr), batch, p)
                buf = zl.at[n % slots]
                n += 1
                spread(buf, total, s)
                for i in {0: (0,), 1: (0, 1, 2), 2: (2,)}[rr]:
                    w = slice(i * N, i * N + N)
                    if cr == 0:
                        light[1, w] += jnp.where(lane < HALF, 0.0, window(buf, r0, t, i, 0))
                    elif cr == 2:
                        light[1, w] += jnp.where(lane < HALF, window(buf, r0, t, i, 2), 0.0)
                    else:
                        light[0, w] += window(buf, r0, t, i, 1)
                        light[1, w] += jnp.where(lane < HALF, window(buf, r0, t, i, 2), window(buf, r0, t, i, 0))
    place = lax.broadcasted_iota(jnp.int32, (PADROWS, N), 0)
    low = jnp.where(row == 0, HALF, 0)
    high = jnp.where(row == rows - 1, HALF + TILE, PADROWS)
    inside = (place >= low) & (place < high)
    for j in range(2):
        light[j] = jnp.where(inside, 1.0 / (light[j] + OBJECT_REG), 0.0)


ROWS = 1152
HALFT = 576
PART = 288
SPLITS = (("y", 4, 72, "x", 4, 18), ("x", 4, 72, "y", 4, 18))


class Mates:
    def __init__(self):
        self.row, self.col = lax.axis_index("row"), lax.axis_index("col")
        self.x, self.y = self.row // 4, self.col // 4
        self.z = self.row % 4 * 2 + self.col // 2 % 2
        self.core = self.col % 2
        self.partner = {"row": self.row, "col": self.col + 1 - 2 * self.core}

    def at(self, axis, d):
        if axis == "y":
            k = lax.rem(self.y + d, 4)
            return k, {"row": self.row, "col": k * 4 + self.col % 4}
        if axis == "x":
            k = lax.rem(self.x + d, 4)
            return k, {"row": k * 4 + self.row % 4, "col": self.col}
        k = lax.rem(self.z + d, 8)
        return k, {"row": self.x * 4 + k // 2, "col": self.y * 4 + k % 2 * 2 + self.core}

    def everyone(self):
        return ([self.partner] + [self.at("y", d)[1] for d in range(1, 4)]
                + [self.at("x", d)[1] for d in range(1, 4)] + [self.at("z", d)[1] for d in range(1, 8)])


def reduce_part(part, mates, g, whole, bufs):
    axis1, n1, p1, axis2, n2, p2 = SPLITS[part]
    r1, s1, r2, s2, r3, z, fin, ag1, ag2, send, recv = bufs
    count = iter(range(100))
    every = []

    def go(src, dst, device):
        i = next(count)
        c = pltpu.make_async_remote_copy(
            src_ref=src, dst_ref=dst, send_sem=send.at[i], recv_sem=recv.at[i],
            device_id=device, device_id_type=MESH)
        c.start()
        every.append(c)
        return c

    def scatter(src, slots, axis, n, p):
        cs = []
        for d in range(1, n):
            k, device = mates.at(axis, d)
            cs.append(go(src.at[pl.ds(k * p, p)], slots.at[d - 1], device))
        return cs

    def collect(src, slots, axis, p, cs):
        acc = src[pl.ds(mates.at(axis, 0)[0] * p, p)]
        for d, c in enumerate(cs):
            c.wait_recv()
            acc = acc + slots[d]
        return acc

    def gather(src, dst, axis, n, p):
        me = pl.ds(mates.at(axis, 0)[0] * p, p)
        cs = [go(src, dst.at[me], mates.at(axis, d)[1]) for d in range(1, n)]
        dst[me] = src[...]
        return cs

    core = mates.core
    c = go(g.at[pl.ds((1 - core) * HALFT + part * PART, PART)], r1, mates.partner)
    yield
    c.wait_recv()
    s1[pl.ds(0, PART)] = g[pl.ds(core * HALFT + part * PART, PART)] + r1[...]
    cs = scatter(s1, r2, axis1, n1, p1)
    yield
    s2[pl.ds(0, p1)] = collect(s1, r2, axis1, p1, cs)
    cs = scatter(s2, r3, axis2, n2, p2)
    yield
    z[0] = collect(s2, r3, axis2, p2, cs)
    cs = [go(z.at[0], z.at[d], mates.at("z", d)[1]) for d in range(1, 8)]
    yield
    for c in cs:
        c.wait_recv()
    acc = z[lax.rem(mates.z, 8)]
    for k in range(1, 8):
        acc = acc + z[lax.rem(mates.z - k + 8, 8)]
    fin[...] = acc
    cs = gather(fin, ag1, axis2, n2, p2)
    yield
    for c in cs:
        c.wait_recv()
    cs = gather(ag1.at[pl.ds(0, p1)], ag2, axis1, n1, p1)
    yield
    for c in cs:
        c.wait_recv()
    mine = pl.ds(core * HALFT + part * PART, PART)
    c = go(ag2.at[pl.ds(0, PART)], whole.at[mine], mates.partner)
    whole[mine] = ag2[pl.ds(0, PART)]
    yield
    c.wait_recv()
    for c in every:
        c.wait_send()
    yield


PART_REFS = 11


def reduction_scratch():
    f = jnp.float32
    shape = lambda *n: pltpu.VMEM(n + (N,), f)
    refs = [shape(ROWS)]
    for _, n1, p1, _, n2, p2 in SPLITS:
        refs += [shape(PART), shape(n1 * p1), shape(n1 - 1, p1), shape(n2 * p2), shape(n2 - 1, p2),
                 shape(8, p2), shape(p2), shape(n2 * p2), shape(n1 * p1),
                 pltpu.SemaphoreType.DMA((21,)), pltpu.SemaphoreType.DMA((21,))]
    return refs


def batch_kernel(batch, last, offs, tiles, *rest):
    tabs, (amp, probe), rest = rest[:4], rest[4:6], rest[6:]
    gin = None
    if batch:
        gin, *rest = rest
    others, parts = (), ()
    if last:
        fresh, whole_out, gout, flat, z, fixed, zl, light, ls, rs, ls_in, rs_in, me, from_up, from_down, send, recv, whole, *more = rest
        mates = Mates()
        others = mates.everyone()
        parts = [reduce_part(k, mates, flat, whole, more[k * PART_REFS:(k + 1) * PART_REFS]) for k in range(2)]
        reach = HALF
    else:
        out, gout, z, fixed, zl, light, ls, rs, ls_in, rs_in, me, fresh, from_up, from_down, sl, sr, hl, hr, send, recv = rest
        reach = N
    up, down, left, right = sides = position()
    clear_missing([(left[0], rs_in), (right[0], ls_in), (up[0], from_up), (down[0], from_down)])
    if not last:
        clear_missing([(left[0], hl), (right[0], hr)])
    greet(sides, others)

    def advance():
        for part in parts:
            next(part)

    blank = jnp.zeros((N, N), jnp.float32)
    for n in range(len(MOVING)):
        for ch in range(2):
            for j in range(2):
                z[n, ch, j, 0:N] = blank
                z[n, ch, j, 2 * N:] = blank
    moving_terms(batch, offs, tiles, probe, amp, gout, gin, z, tabs)
    greeted(sides, others)

    count = iter(range(100))
    every = []

    def link(src, dst, to, source):
        i = next(count)
        c = Link(src, dst, send.at[i], recv.at[i], to, source)
        c.start()
        every.append(c)
        return c

    def gathered(ch, i, k):
        acc = None
        for n, p in enumerate(MOVING):
            r0, t, _ = spot(offs, (1, 1), batch, p)
            w = window(z.at[n, ch], r0, t, i, k)
            acc = w if acc is None else acc + w
        for p, at, tile in STATIC:
            if (at, tile) == (i * N, k):
                acc = acc + fixed[p, ch]
        return acc

    lane = lanes((N, N))
    cols = {}
    row_links = {}

    def side_strips(i):
        w = slice(i * N, i * N + N)
        t0 = [gathered(ch, i, 0) for ch in range(2)]
        t2 = [gathered(ch, i, 2) for ch in range(2)]
        ls[w] = jnp.where(lane < HALF, t0[0], turn(t0[1]))
        rs[w] = jnp.where(lane < HALF, turn(t2[0]), t2[1])
        for ch in range(2):
            me[1, ch, w] = jnp.where(lane < HALF, t2[ch], t0[ch])

    def send_cols(at, size):
        d = pl.ds(at, size)
        cols[at] = [link(ls.at[d], ls_in.at[d], left, right), link(rs.at[d], rs_in.at[d], right, left)]

    def middle(i):
        for ch in range(2):
            me[0, ch, i * N:i * N + N] = gathered(ch, i, 1)

    def send_rows(which, top, at, size):
        base = 0 if top else PADROWS - reach
        src, dst = pl.ds(at, size), pl.ds(at - base, size)
        if top:
            c = link(me.at[which, :, src, :], from_down.at[which, :, dst, :], up, down)
        else:
            c = link(me.at[which, :, src, :], from_up.at[which, :, dst, :], down, up)
        row_links[which, top, at - base] = c

    def fold_cols(at, size):
        for c in cols[at]:
            c.arrived()
        w = slice(at, at + size)
        side = lanes((size, N))
        a, b = ls_in[w], rs_in[w]
        me[1, 0, w] += jnp.where(side < HALF, a, turn(b))
        me[1, 1, w] += jnp.where(side < HALF, turn(a), b)

    middle(0)
    send_rows(0, True, 0, reach)
    middle(2)
    send_rows(0, False, PADROWS - reach, reach)
    side_strips(1)
    send_cols(N, N)
    static_terms(batch, tiles, probe, amp, gout, fixed, tabs)
    if last:
        flat[...] = gout[...].reshape(ROWS, N)
    advance()
    order = ((0, True), (320, False), (64, True), (256, False))
    for i in (0, 2):
        side_strips(i)
        if i == 0:
            send_cols(0, HALF)
    send_cols(320, HALF)
    send_cols(64, HALF)
    send_cols(256, HALF)
    advance()
    middle(1)
    if not last:
        light_maps(batch, offs, probe, zl, light)
    for at, top in order[:2] if last else order:
        fold_cols(at, HALF)
        send_rows(1, top, at, HALF)
    advance()
    if last:
        light_maps(batch, offs, probe, zl, light)
        for at, top in order[2:]:
            fold_cols(at, HALF)
    fold_cols(N, N)
    halos = []

    def update(which, at, size, extra):
        w = slice(at, at + size)
        lv = light[which, w]
        mine = lanes((size, N))
        for ch in range(2):
            t = me[which, ch, w]
            if extra is not None:
                t = t + extra[ch]
            old = tiles[ch, 1, w] if which == 0 else jnp.where(mine < HALF, tiles[ch, 2, w], tiles[ch, 0, w])
            fresh[which, ch, w] = old + t * lv

    def halo(at, size):
        if last:
            return
        w = slice(at, at + size)
        a, b = halo_strips(fresh[1, 0, w], fresh[1, 1, w])
        sl[w] = a
        sr[w] = b
        d = pl.ds(at, size)
        halos.extend([link(sl.at[d], hr.at[d], left, right), link(sr.at[d], hl.at[d], right, left)])

    update(1, N, N, None)
    halo(N, N)
    update(0, N, N, None)
    advance()
    if last:
        row_links[1, False, 0].arrived()
        update(1, HALF, HALF, from_up.at[1])
        row_links[1, True, 0].arrived()
        update(1, 256, HALF, from_down.at[1])
        row_links[0, False, 0].arrived()
        update(0, HALF, HALF, from_up.at[0])
        row_links[0, True, 0].arrived()
        update(0, 256, HALF, from_down.at[0])
        for _ in range(4):
            advance()
        whole_out[...] = whole[...]
    else:
        for top, at in ((True, 0), (False, 64), (True, 64), (False, 0)):
            row_links[1, top, at].arrived()
            source, base = (from_down, 2 * N) if top else (from_up, 0)
            update(1, base + at, HALF, source.at[1, :, pl.ds(at, HALF), :])
            halo(base + at, HALF)
        row_links[0, False, 0].arrived()
        update(0, 0, N, from_up.at[0])
        row_links[0, True, 0].arrived()
        update(0, 2 * N, N, from_down.at[0])
        for ch in range(2):
            out[ch, 1] = fresh[0, ch]
        for c in halos:
            c.arrived()
        finish_tiles(out, fresh, hl, hr)
    for c in every:
        c.sent()


def run_batch(batch, last, offs, tiles, others, gin):
    f = jnp.float32
    strip = pltpu.VMEM((PADROWS, N), f)
    sums = jax.ShapeDtypeStruct((2 * MODES + 1, N, N), f)
    reach = HALF if last else N
    if last:
        shapes = (jax.ShapeDtypeStruct((2, 2, PADROWS, N), f), jax.ShapeDtypeStruct((ROWS, N), f))
        extra = [pltpu.VMEM((2 * MODES + 1, N, N), f), pltpu.VMEM((ROWS, N), f)]
    else:
        shapes = (jax.ShapeDtypeStruct((2, 3, PADROWS, N), f), sums)
        extra = []
    return pl.pallas_call(
        functools.partial(batch_kernel, batch, last),
        out_shape=shapes,
        in_specs=[SM] + [VM] * (1 + len(others) + len(gin)),
        out_specs=(VM,) * len(shapes),
        scratch_shapes=extra + [
            pltpu.VMEM((len(MOVING), 2, 2, PADROWS, N), f),
            pltpu.VMEM((len(STATIC), 2, N, N), f),
            pltpu.VMEM((3, 2, PADROWS, N), f),
            pltpu.VMEM((2, PADROWS, N), f),
            strip, strip, strip, strip,
            pltpu.VMEM((2, 2, PADROWS, N), f),
        ] + ([] if last else [pltpu.VMEM((2, 2, PADROWS, N), f)]) + [
            pltpu.VMEM((2, 2, reach, N), f),
            pltpu.VMEM((2, 2, reach, N), f),
        ] + ([] if last else [strip] * 4) + [
            pltpu.SemaphoreType.DMA((26,)),
            pltpu.SemaphoreType.DMA((26,)),
        ] + (reduction_scratch() if last else []),
        compiler_params=pltpu.CompilerParams(
            collective_id=1 + batch, has_side_effects=True, vmem_limit_bytes=36 * 2**20),
        name=f"batch{batch}",
    )(offs, tiles, *others, *gin)


def final_kernel(fresh, whole, out, step_out):
    wide = lanes((TILE, N))
    w = slice(HALF, HALF + TILE)
    for ch in range(2):
        m, e = fresh[0, ch, w], fresh[1, ch, w]
        out[ch, :, 0:128] = turn(jnp.where(wide < HALF, m, e))
        out[ch, :, 128:256] = turn(jnp.where(wide < HALF, e, m))
    inv = lax.rsqrt(whole[pl.ds(2 * MODES * N, N)] + PROBE_REG)
    for k in range(2 * MODES):
        step_out[pl.ds(N * k, N)] = whole[pl.ds(N * k, N)] * inv


def run_final(fresh, whole):
    return pl.pallas_call(
        final_kernel,
        out_shape=(jax.ShapeDtypeStruct((2, TILE, TILE), jnp.float32), jax.ShapeDtypeStruct((2 * MODES * N, N), jnp.float32)),
        in_specs=[VM, VM],
        out_specs=(VM, VM),
        compiler_params=pltpu.CompilerParams(vmem_limit_bytes=8 * 2**20),
        name="final",
    )(fresh, whole)


def on_device(object_field, probe, amplitudes, offsets):
    mine = jnp.swapaxes(offsets, 3, 4).reshape(BATCHES, 2, POS)
    amps = amplitudes.reshape(BATCHES, POS, N, N)
    tabs = [jnp.asarray(t) for t in tables()]
    keep = lambda a: pltpu.with_memory_space_constraint(a, pltpu.HBM)
    tiles, offs, *others = run_first(keep(object_field), keep(mine), [keep(a) for a in (*tabs, amps, probe)])
    grads = ()
    for b in range(BATCHES - 1):
        tiles, sums = run_batch(b, False, offs, tiles, others, grads)
        grads = (sums,)
    obj, step = run_final(*run_batch(BATCHES - 1, True, offs, tiles, others, grads))
    return obj, step.reshape(2, MODES, N, N)


def solution(mesh):
    placed = (
        P(None, "row", "col"),
        P(),
        P("row", "col", None, None, None, None),
        P("row", "col", None, None, None),
    )
    return jax.shard_map(
        on_device,
        mesh=mesh,
        in_specs=placed,
        out_specs=(P(None, "row", "col"), P()),
        check_vma=False,
    )
```

```python
import functools
import math

import jax
import jax.numpy as jnp
import ml_dtypes
import numpy as np
from jax import lax
from jax.experimental import pallas as pl
from jax.experimental.pallas import tpu as pltpu
from jax.sharding import PartitionSpec as P

N = 128
MODES = 4
TILE = 256
POS = 4
BATCHES = 3
HALF = 64
PADROWS = 384
FAR = 100000

AMP_FLOOR = 0.25
OBJECT_REG = 0.5
PROBE_REG = 1.0

MESH = pl.DeviceIdType.MESH
VM = pl.BlockSpec(memory_space=pltpu.VMEM)
SM = pl.BlockSpec(memory_space=pltpu.SMEM)


def tables():
    k = np.arange(N)
    ang = (k[:, None] * k[None, :] % N) * (2.0 * math.pi / N)
    fr, fi = np.cos(ang) / math.sqrt(N), -np.sin(ang) / math.sqrt(N)
    a = np.block([[fr, fi], [-fi, fr]])
    b = np.block([[fr, -fi], [fi, fr]])

    def split(m):
        hi = m.astype(np.float32).astype(ml_dtypes.bfloat16)
        lo = (m - hi.astype(np.float64)).astype(np.float32).astype(ml_dtypes.bfloat16)
        return hi, lo

    ah, al = split(a)
    bh, bl = split(b)
    return ah, al, bh, bl


def lanes(shape):
    return lax.broadcasted_iota(jnp.int32, shape, 1)


def split_hi_lo(x):
    hi = x.astype(jnp.bfloat16)
    lo = (x - hi.astype(jnp.float32)).astype(jnp.bfloat16)
    return hi, lo


def dot(a, b):
    return jnp.dot(a, b, preferred_element_type=jnp.float32)


def right_mul(x, th, tl):
    hi, lo = split_hi_lo(x)
    return dot(jnp.concatenate([hi, lo, hi], axis=1), jnp.concatenate([th, th, tl], axis=0))


def left_mul(th, tl, x):
    hi, lo = split_hi_lo(x)
    return dot(jnp.concatenate([th, th, tl], axis=1), jnp.concatenate([hi, lo, hi], axis=0))


def position():
    row, col = lax.axis_index("row"), lax.axis_index("col")
    rows, cols = lax.axis_size("row"), lax.axis_size("col")
    up = (row > 0, {"row": jnp.maximum(row - 1, 0), "col": col})
    down = (row < rows - 1, {"row": jnp.minimum(row + 1, rows - 1), "col": col})
    left = (col > 0, {"row": row, "col": jnp.maximum(col - 1, 0)})
    right = (col < cols - 1, {"row": row, "col": jnp.minimum(col + 1, cols - 1)})
    return up, down, left, right


def greet(sides, others=()):
    barrier = pltpu.get_barrier_semaphore()
    for there, device in sides:
        @pl.when(there)
        def _(device=device):
            pl.semaphore_signal(barrier, inc=1, device_id=device, device_id_type=MESH)
    for device in others:
        pl.semaphore_signal(barrier, inc=1, device_id=device, device_id_type=MESH)


def greeted(sides, others=()):
    barrier = pltpu.get_barrier_semaphore()
    pl.semaphore_wait(barrier, sum(there.astype(jnp.int32) for there, _ in sides) + len(others))


class Link:
    def __init__(self, src, dst, send, recv, to, source):
        self.there, device = to
        self.source = source[0]
        self.copy = pltpu.make_async_remote_copy(
            src_ref=src, dst_ref=dst, send_sem=send, recv_sem=recv,
            device_id=device, device_id_type=MESH)

    def start(self):
        @pl.when(self.there)
        def _():
            self.copy.start()

    def arrived(self):
        @pl.when(self.source)
        def _():
            self.copy.wait_recv()

    def sent(self):
        @pl.when(self.there)
        def _():
            self.copy.wait_send()


def clear_missing(pairs):
    for there, ref in pairs:
        @pl.when(jnp.logical_not(there))
        def _(ref=ref):
            ref[...] = jnp.zeros(ref.shape, ref.dtype)


def turn(x):
    return pltpu.roll(x, HALF, 1)


def halo_strips(re, im):
    lane = lanes(re.shape)
    ti = turn(im)
    return jnp.where(lane < HALF, ti, re), jnp.where(lane < HALF, re, ti)


def first_kernel(obj_hbm, offs, *rest):
    far_refs, rest = rest[:6], rest[6:]
    out, offs_out, *near_refs = rest[:8]
    obj, me, sl, sr, hl, hr, table, send, recv, local = rest[8:]
    up, down, left, right = position()
    load = pltpu.make_async_copy(obj_hbm, obj, local.at[0])
    load.start()
    loads = [pltpu.make_async_copy(a, b, local.at[i + 1]) for i, (a, b) in enumerate(zip(far_refs, near_refs))]
    for c in loads:
        c.start()
    lane = lanes((TILE, N))
    for cr in range(3):
        for rr in range(3):
            if (cr, rr) != (1, 1):
                table[cr, rr] = jnp.full(table.shape[2:], FAR, jnp.int32)
    own_offs = pltpu.make_async_copy(offs, table.at[1, 1], local.at[7])
    own_offs.start()
    clear_missing([(left[0], hl), (right[0], hr),
                   (up[0], me.at[:, :, pl.ds(0, HALF), :]),
                   (down[0], me.at[:, :, pl.ds(PADROWS - HALF, HALF), :])])
    greet((up, down, left, right))
    own = slice(HALF, HALF + TILE)
    load.wait()
    for ch in range(2):
        a, b = turn(obj[ch, :, 0:128]), turn(obj[ch, :, 128:256])
        me[1, ch, own] = jnp.where(lane < HALF, b, a)
        me[0, ch, own] = jnp.where(lane < HALF, a, b)
    own_offs.wait()
    greeted((up, down, left, right))

    count = iter(range(100))

    def link(src, dst, to, source):
        i = next(count)
        return Link(src, dst, send.at[i], recv.at[i], to, source)

    def rows(which):
        top, bottom = pl.ds(HALF, HALF), pl.ds(TILE, HALF)
        above, below = pl.ds(0, HALF), pl.ds(PADROWS - HALF, HALF)
        return [link(me.at[which, :, top, :], me.at[which, :, below, :], up, down),
                link(me.at[which, :, bottom, :], me.at[which, :, above, :], down, up)]

    def cols(at, size):
        w = slice(at, at + size)
        a, b = halo_strips(me[1, 0, w], me[1, 1, w])
        sl[w] = a
        sr[w] = b
        d = pl.ds(at, size)
        both = [link(sl.at[d], hr.at[d], left, right), link(sr.at[d], hl.at[d], right, left)]
        for c in both:
            c.start()
        return both

    tell = [link(table.at[1, 1], table.at[1, 2], up, down),
            link(table.at[1, 1], table.at[1, 0], down, up)]
    edge = rows(1)
    middle = rows(0)
    for c in tell + edge:
        c.start()
    late = cols(HALF, TILE)
    for c in middle:
        c.start()
    for c in tell:
        c.arrived()
    more = [link(table.at[1], table.at[2], left, right),
            link(table.at[1], table.at[0], right, left)]
    for c in more:
        c.start()
    late += more
    edge[1].arrived()
    late += cols(0, HALF)
    edge[0].arrived()
    late += cols(PADROWS - HALF, HALF)
    for c in middle:
        c.arrived()
    for ch in range(2):
        out[ch, 1] = me[0, ch]
    for c in late:
        c.arrived()
    finish_tiles(out, me, hl, hr)
    offs_out[...] = table[...]
    for c in loads:
        c.wait()
    for c in tell + edge + middle + late:
        c.sent()


def finish_tiles(out, me, hl, hr):
    wide = lanes((PADROWS, N))
    out[0, 0] = jnp.where(wide < HALF, hl[...], me[1, 0])
    out[1, 0] = jnp.where(wide < HALF, turn(hl[...]), me[1, 1])
    out[0, 2] = jnp.where(wide < HALF, me[1, 0], hr[...])
    out[1, 2] = jnp.where(wide < HALF, me[1, 1], turn(hr[...]))


def run_first(obj, offs, others):
    f = jnp.float32
    strip = pltpu.VMEM((PADROWS, N), f)
    hbm = pl.BlockSpec(memory_space=pltpu.HBM)
    return pl.pallas_call(
        first_kernel,
        out_shape=(
            jax.ShapeDtypeStruct((2, 3, PADROWS, N), f),
            jax.ShapeDtypeStruct((3, 3, BATCHES, 2, POS), jnp.int32),
        ) + tuple(jax.ShapeDtypeStruct(a.shape, a.dtype) for a in others),
        in_specs=[hbm] * 8,
        out_specs=(VM,) * 8,
        scratch_shapes=[
            pltpu.VMEM((2, TILE, TILE), f),
            pltpu.VMEM((2, 2, PADROWS, N), f),
            strip, strip, strip, strip,
            pltpu.VMEM((3, 3, BATCHES, 2, POS), jnp.int32),
            pltpu.SemaphoreType.DMA((14,)),
            pltpu.SemaphoreType.DMA((14,)),
            pltpu.SemaphoreType.DMA((8,)),
        ],
        compiler_params=pltpu.CompilerParams(collective_id=0, has_side_effects=True, vmem_limit_bytes=14 * 2**20),
        name="first",
    )(obj, offs, *others)


def spread(dest, value, s):
    lane = lanes((N, N))
    turned = pltpu.roll(value, s, 1)
    dest[0, N:2 * N] = jnp.where(lane >= s, turned, 0.0)
    dest[1, N:2 * N] = jnp.where(lane < s, turned, 0.0)


def window(src, r0, t, i, k):
    j = k - t
    hit = (j == 0) | (j == 1)
    start = jnp.where(hit, jnp.clip(N + N * i - r0, 0, 2 * N), 0)
    return src[jnp.where(hit, j, 0), pl.ds(start, N)]


STATIC = ((0, 0, 0), (1, 2 * N, 2))
MOVING = (2, 3)


def spot(offs, block, batch, p):
    cr, rr = block
    r0 = offs[cr, rr, batch, 0, p] + (rr - 1) * TILE + HALF
    c0 = offs[cr, rr, batch, 1, p] + (cr - 1) * TILE + HALF
    return r0, lax.shift_right_arithmetic(c0, 7), lax.bitwise_and(c0, 127)


def terms(pr, pi, probe, measured, gout, gin, first, ah, al, bh, bl):
    waves = []
    for m in range(MODES):
        qr, qi = probe[0, m], probe[1, m]
        waves.append(jnp.concatenate([qr * pr - qi * pi, qr * pi + qi * pr], axis=1))
    half = right_mul(jnp.concatenate(waves, axis=0), ah[...], al[...])
    rows_of = [half[m * N:(m + 1) * N] for m in range(MODES)]
    stacked = jnp.concatenate(
        [jnp.concatenate([h[:, :N] for h in rows_of], axis=1),
         jnp.concatenate([h[:, N:] for h in rows_of], axis=1)], axis=0)
    far = left_mul(bh[...], bl[...], stacked)
    inten = jnp.zeros((N, N), jnp.float32)
    for m in range(MODES):
        fr, fi = far[:N, m * N:(m + 1) * N], far[N:, m * N:(m + 1) * N]
        inten += fr * fr + fi * fi
    factor = measured * lax.rsqrt(jnp.maximum(inten, AMP_FLOOR * AMP_FLOOR)) - 1.0
    factor = jnp.concatenate([factor] * MODES, axis=1)
    factor = jnp.concatenate([factor] * 2, axis=0)
    back_half = left_mul(ah[...], al[...], far * factor)
    lhs = jnp.concatenate(
        [jnp.concatenate([back_half[:N, m * N:(m + 1) * N], back_half[N:, m * N:(m + 1) * N]], axis=1)
         for m in range(MODES)], axis=0)
    change = right_mul(lhs, bh[...], bl[...])
    tr = jnp.zeros((N, N), jnp.float32)
    ti = jnp.zeros((N, N), jnp.float32)

    def accumulate(k, value):
        if not first:
            gout[k] += value
        elif gin is None:
            gout[k] = value
        else:
            gout[k] = gin[k] + value

    for m in range(MODES):
        qr, qi = probe[0, m], probe[1, m]
        cr, ci = change[m * N:(m + 1) * N, :N], change[m * N:(m + 1) * N, N:]
        tr += qr * cr + qi * ci
        ti += qr * ci - qi * cr
        accumulate(m, pr * cr + pi * ci)
        accumulate(MODES + m, pr * ci - pi * cr)
    accumulate(2 * MODES, pr * pr + pi * pi)
    return tr, ti


def moving_terms(batch, offs, tiles, probe, amp, gout, gin, z, tabs):
    lane = lanes((N, N))
    for n, p in enumerate(MOVING):
        r0, t, s = spot(offs, (1, 1), batch, p)
        rows = pl.ds(r0, N)
        back = lax.bitwise_and(128 - s, 127)
        after = jnp.minimum(t + 1, 2)

        def cut(ch):
            one = pltpu.roll(tiles[ch, t, rows], back, 1)
            two = pltpu.roll(tiles[ch, after, rows], back, 1)
            return jnp.where(lane < 128 - s, one, two)

        tr, ti = terms(cut(0), cut(1), probe, amp[batch, p], gout, gin, n == 0, *tabs)
        spread(z.at[n, 0], tr, s)
        spread(z.at[n, 1], ti, s)


def static_terms(batch, tiles, probe, amp, gout, fixed, tabs):
    for p, at, t in STATIC:
        pr, pi = tiles[0, t, at:at + N], tiles[1, t, at:at + N]
        tr, ti = terms(pr, pi, probe, amp[batch, p], gout, None, False, *tabs)
        fixed[p, 0] = tr
        fixed[p, 1] = ti


def light_maps(batch, offs, probe, zl, light):
    row, rows = lax.axis_index("row"), lax.axis_size("row")
    col, cols = lax.axis_index("col"), lax.axis_size("col")
    lane = lanes((N, N))
    total = jnp.zeros((N, N), jnp.float32)
    for m in range(MODES):
        total += probe[0, m] * probe[0, m] + probe[1, m] * probe[1, m]
    blank = jnp.zeros((N, N), jnp.float32)
    slots = zl.shape[0]
    for n in range(slots):
        for j in range(2):
            zl[n, j, 0:N] = blank
            zl[n, j, 2 * N:] = blank

    def there(yes):
        return yes.astype(jnp.float32)

    up, down, left, right = there(row > 0), there(row < rows - 1), there(col > 0), there(col < cols - 1)
    corner = {(0, 0): 1.0 + up * left, (0, 2): right + up, (2, 0): down + left, (2, 2): 1.0 + down * right}
    sums = {}
    for i in (0, 2):
        sums[i] = total * jnp.where(lane < HALF, corner[i, 2], corner[i, 0])
    light[1, 0:N] = sums[0]
    light[1, N:2 * N] = blank
    light[1, 2 * N:] = sums[2]
    for i in range(3):
        light[0, i * N:i * N + N] = blank

    n = 0
    for cr in range(3):
        for rr in range(3):
            for p in MOVING:
                r0, t, s = spot(offs, (cr, rr), batch, p)
                buf = zl.at[n % slots]
                n += 1
                spread(buf, total, s)
                for i in {0: (0,), 1: (0, 1, 2), 2: (2,)}[rr]:
                    w = slice(i * N, i * N + N)
                    if cr == 0:
                        light[1, w] += jnp.where(lane < HALF, 0.0, window(buf, r0, t, i, 0))
                    elif cr == 2:
                        light[1, w] += jnp.where(lane < HALF, window(buf, r0, t, i, 2), 0.0)
                    else:
                        light[0, w] += window(buf, r0, t, i, 1)
                        light[1, w] += jnp.where(lane < HALF, window(buf, r0, t, i, 2), window(buf, r0, t, i, 0))
    place = lax.broadcasted_iota(jnp.int32, (PADROWS, N), 0)
    low = jnp.where(row == 0, HALF, 0)
    high = jnp.where(row == rows - 1, HALF + TILE, PADROWS)
    inside = (place >= low) & (place < high)
    for j in range(2):
        light[j] = jnp.where(inside, 1.0 / (light[j] + OBJECT_REG), 0.0)


ROWS = 1152
HALFT = 576
PART = 288
SPLITS = (("y", 4, 72, "x", 4, 18), ("x", 4, 72, "y", 4, 18))


class Mates:
    def __init__(self):
        self.row, self.col = lax.axis_index("row"), lax.axis_index("col")
        self.x, self.y = self.row // 4, self.col // 4
        self.z = self.row % 4 * 2 + self.col // 2 % 2
        self.core = self.col % 2
        self.partner = {"row": self.row, "col": self.col + 1 - 2 * self.core}

    def at(self, axis, d):
        if axis == "y":
            k = lax.rem(self.y + d, 4)
            return k, {"row": self.row, "col": k * 4 + self.col % 4}
        if axis == "x":
            k = lax.rem(self.x + d, 4)
            return k, {"row": k * 4 + self.row % 4, "col": self.col}
        k = lax.rem(self.z + d, 8)
        return k, {"row": self.x * 4 + k // 2, "col": self.y * 4 + k % 2 * 2 + self.core}

    def everyone(self):
        return ([self.partner] + [self.at("y", d)[1] for d in range(1, 4)]
                + [self.at("x", d)[1] for d in range(1, 4)] + [self.at("z", d)[1] for d in range(1, 8)])


def reduce_part(part, mates, g, whole, bufs):
    axis1, n1, p1, axis2, n2, p2 = SPLITS[part]
    r1, s1, r2, s2, r3, z, fin, ag1, ag2, send, recv = bufs
    count = iter(range(100))
    every = []

    def go(src, dst, device):
        i = next(count)
        c = pltpu.make_async_remote_copy(
            src_ref=src, dst_ref=dst, send_sem=send.at[i], recv_sem=recv.at[i],
            device_id=device, device_id_type=MESH)
        c.start()
        every.append(c)
        return c

    def scatter(src, slots, axis, n, p):
        cs = []
        for d in range(1, n):
            k, device = mates.at(axis, d)
            cs.append(go(src.at[pl.ds(k * p, p)], slots.at[d - 1], device))
        return cs

    def collect(src, slots, axis, p, cs):
        acc = src[pl.ds(mates.at(axis, 0)[0] * p, p)]
        for d, c in enumerate(cs):
            c.wait_recv()
            acc = acc + slots[d]
        return acc

    def gather(src, dst, axis, n, p):
        me = pl.ds(mates.at(axis, 0)[0] * p, p)
        cs = [go(src, dst.at[me], mates.at(axis, d)[1]) for d in range(1, n)]
        dst[me] = src[...]
        return cs

    core = mates.core
    c = go(g.at[pl.ds((1 - core) * HALFT + part * PART, PART)], r1, mates.partner)
    yield
    c.wait_recv()
    s1[pl.ds(0, PART)] = g[pl.ds(core * HALFT + part * PART, PART)] + r1[...]
    cs = scatter(s1, r2, axis1, n1, p1)
    yield
    s2[pl.ds(0, p1)] = collect(s1, r2, axis1, p1, cs)
    cs = scatter(s2, r3, axis2, n2, p2)
    yield
    z[0] = collect(s2, r3, axis2, p2, cs)
    cs = [go(z.at[0], z.at[d], mates.at("z", d)[1]) for d in range(1, 8)]
    yield
    for c in cs:
        c.wait_recv()
    acc = z[lax.rem(mates.z, 8)]
    for k in range(1, 8):
        acc = acc + z[lax.rem(mates.z - k + 8, 8)]
    fin[...] = acc
    cs = gather(fin, ag1, axis2, n2, p2)
    yield
    for c in cs:
        c.wait_recv()
    cs = gather(ag1.at[pl.ds(0, p1)], ag2, axis1, n1, p1)
    yield
    for c in cs:
        c.wait_recv()
    mine = pl.ds(core * HALFT + part * PART, PART)
    c = go(ag2.at[pl.ds(0, PART)], whole.at[mine], mates.partner)
    whole[mine] = ag2[pl.ds(0, PART)]
    yield
    c.wait_recv()
    for c in every:
        c.wait_send()
    yield


PART_REFS = 11


def reduction_scratch():
    f = jnp.float32
    shape = lambda *n: pltpu.VMEM(n + (N,), f)
    refs = [shape(ROWS)]
    for _, n1, p1, _, n2, p2 in SPLITS:
        refs += [shape(PART), shape(n1 * p1), shape(n1 - 1, p1), shape(n2 * p2), shape(n2 - 1, p2),
                 shape(8, p2), shape(p2), shape(n2 * p2), shape(n1 * p1),
                 pltpu.SemaphoreType.DMA((21,)), pltpu.SemaphoreType.DMA((21,))]
    return refs


def batch_kernel(batch, last, offs, tiles, *rest):
    tabs, (amp, probe), rest = rest[:4], rest[4:6], rest[6:]
    gin = None
    if batch:
        gin, *rest = rest
    others, parts = (), ()
    if last:
        fresh, whole_out, gout, flat, z, fixed, zl, light, ls, rs, ls_in, rs_in, me, from_up, from_down, send, recv, whole, *more = rest
        mates = Mates()
        others = mates.everyone()
        parts = [reduce_part(k, mates, flat, whole, more[k * PART_REFS:(k + 1) * PART_REFS]) for k in range(2)]
        reach = HALF
    else:
        out, gout, z, fixed, zl, light, ls, rs, ls_in, rs_in, me, fresh, from_up, from_down, sl, sr, hl, hr, send, recv = rest
        reach = N
    up, down, left, right = sides = position()
    clear_missing([(left[0], rs_in), (right[0], ls_in), (up[0], from_up), (down[0], from_down)])
    if not last:
        clear_missing([(left[0], hl), (right[0], hr)])
    greet(sides, others)

    def advance():
        for part in parts:
            next(part)

    blank = jnp.zeros((N, N), jnp.float32)
    for n in range(len(MOVING)):
        for ch in range(2):
            for j in range(2):
                z[n, ch, j, 0:N] = blank
                z[n, ch, j, 2 * N:] = blank
    moving_terms(batch, offs, tiles, probe, amp, gout, gin, z, tabs)
    greeted(sides, others)

    count = iter(range(100))
    every = []

    def link(src, dst, to, source):
        i = next(count)
        c = Link(src, dst, send.at[i], recv.at[i], to, source)
        c.start()
        every.append(c)
        return c

    def gathered(ch, i, k):
        acc = None
        for n, p in enumerate(MOVING):
            r0, t, _ = spot(offs, (1, 1), batch, p)
            w = window(z.at[n, ch], r0, t, i, k)
            acc = w if acc is None else acc + w
        for p, at, tile in STATIC:
            if (at, tile) == (i * N, k):
                acc = acc + fixed[p, ch]
        return acc

    lane = lanes((N, N))
    cols = {}
    row_links = {}

    def side_strips(i):
        w = slice(i * N, i * N + N)
        t0 = [gathered(ch, i, 0) for ch in range(2)]
        t2 = [gathered(ch, i, 2) for ch in range(2)]
        ls[w] = jnp.where(lane < HALF, t0[0], turn(t0[1]))
        rs[w] = jnp.where(lane < HALF, turn(t2[0]), t2[1])
        for ch in range(2):
            me[1, ch, w] = jnp.where(lane < HALF, t2[ch], t0[ch])

    def send_cols(at, size):
        d = pl.ds(at, size)
        cols[at] = [link(ls.at[d], ls_in.at[d], left, right), link(rs.at[d], rs_in.at[d], right, left)]

    def middle(i):
        for ch in range(2):
            me[0, ch, i * N:i * N + N] = gathered(ch, i, 1)

    def send_rows(which, top, at, size):
        base = 0 if top else PADROWS - reach
        src, dst = pl.ds(at, size), pl.ds(at - base, size)
        if top:
            c = link(me.at[which, :, src, :], from_down.at[which, :, dst, :], up, down)
        else:
            c = link(me.at[which, :, src, :], from_up.at[which, :, dst, :], down, up)
        row_links[which, top, at - base] = c

    def fold_cols(at, size):
        for c in cols[at]:
            c.arrived()
        w = slice(at, at + size)
        side = lanes((size, N))
        a, b = ls_in[w], rs_in[w]
        me[1, 0, w] += jnp.where(side < HALF, a, turn(b))
        me[1, 1, w] += jnp.where(side < HALF, turn(a), b)

    middle(0)
    send_rows(0, True, 0, reach)
    middle(2)
    send_rows(0, False, PADROWS - reach, reach)
    side_strips(1)
    send_cols(N, N)
    static_terms(batch, tiles, probe, amp, gout, fixed, tabs)
    if last:
        flat[...] = gout[...].reshape(ROWS, N)
    advance()
    order = ((0, True), (320, False), (64, True), (256, False))
    for i in (0, 2):
        side_strips(i)
        if i == 0:
            send_cols(0, HALF)
    send_cols(320, HALF)
    send_cols(64, HALF)
    send_cols(256, HALF)
    advance()
    middle(1)
    for at, top in order[:2] if last else order:
        fold_cols(at, HALF)
        send_rows(1, top, at, HALF)
    advance()
    light_maps(batch, offs, probe, zl, light)
    if last:
        for at, top in order[2:]:
            fold_cols(at, HALF)
    fold_cols(N, N)
    halos = []

    def update(which, at, size, extra):
        w = slice(at, at + size)
        lv = light[which, w]
        mine = lanes((size, N))
        for ch in range(2):
            t = me[which, ch, w]
            if extra is not None:
                t = t + extra[ch]
            old = tiles[ch, 1, w] if which == 0 else jnp.where(mine < HALF, tiles[ch, 2, w], tiles[ch, 0, w])
            fresh[which, ch, w] = old + t * lv

    def halo(at, size):
        if last:
            return
        w = slice(at, at + size)
        a, b = halo_strips(fresh[1, 0, w], fresh[1, 1, w])
        sl[w] = a
        sr[w] = b
        d = pl.ds(at, size)
        halos.extend([link(sl.at[d], hr.at[d], left, right), link(sr.at[d], hl.at[d], right, left)])

    update(1, N, N, None)
    halo(N, N)
    update(0, N, N, None)
    advance()
    if last:
        row_links[1, False, 0].arrived()
        update(1, HALF, HALF, from_up.at[1])
        row_links[1, True, 0].arrived()
        update(1, 256, HALF, from_down.at[1])
        row_links[0, False, 0].arrived()
        update(0, HALF, HALF, from_up.at[0])
        row_links[0, True, 0].arrived()
        update(0, 256, HALF, from_down.at[0])
        for _ in range(4):
            advance()
        whole_out[...] = whole[...]
    else:
        for top, at in ((True, 0), (False, 64), (True, 64), (False, 0)):
            row_links[1, top, at].arrived()
            source, base = (from_down, 2 * N) if top else (from_up, 0)
            update(1, base + at, HALF, source.at[1, :, pl.ds(at, HALF), :])
            halo(base + at, HALF)
        row_links[0, False, 0].arrived()
        update(0, 0, N, from_up.at[0])
        row_links[0, True, 0].arrived()
        update(0, 2 * N, N, from_down.at[0])
        for ch in range(2):
            out[ch, 1] = fresh[0, ch]
        for c in halos:
            c.arrived()
        finish_tiles(out, fresh, hl, hr)
    for c in every:
        c.sent()


def run_batch(batch, last, offs, tiles, others, gin):
    f = jnp.float32
    strip = pltpu.VMEM((PADROWS, N), f)
    sums = jax.ShapeDtypeStruct((2 * MODES + 1, N, N), f)
    reach = HALF if last else N
    if last:
        shapes = (jax.ShapeDtypeStruct((2, 2, PADROWS, N), f), jax.ShapeDtypeStruct((ROWS, N), f))
        extra = [pltpu.VMEM((2 * MODES + 1, N, N), f), pltpu.VMEM((ROWS, N), f)]
    else:
        shapes = (jax.ShapeDtypeStruct((2, 3, PADROWS, N), f), sums)
        extra = []
    return pl.pallas_call(
        functools.partial(batch_kernel, batch, last),
        out_shape=shapes,
        in_specs=[SM] + [VM] * (1 + len(others) + len(gin)),
        out_specs=(VM,) * len(shapes),
        scratch_shapes=extra + [
            pltpu.VMEM((len(MOVING), 2, 2, PADROWS, N), f),
            pltpu.VMEM((len(STATIC), 2, N, N), f),
            pltpu.VMEM((3, 2, PADROWS, N), f),
            pltpu.VMEM((2, PADROWS, N), f),
            strip, strip, strip, strip,
            pltpu.VMEM((2, 2, PADROWS, N), f),
        ] + ([] if last else [pltpu.VMEM((2, 2, PADROWS, N), f)]) + [
            pltpu.VMEM((2, 2, reach, N), f),
            pltpu.VMEM((2, 2, reach, N), f),
        ] + ([] if last else [strip] * 4) + [
            pltpu.SemaphoreType.DMA((26,)),
            pltpu.SemaphoreType.DMA((26,)),
        ] + (reduction_scratch() if last else []),
        compiler_params=pltpu.CompilerParams(
            collective_id=1 + batch, has_side_effects=True, vmem_limit_bytes=36 * 2**20),
        name=f"batch{batch}",
    )(offs, tiles, *others, *gin)


def final_kernel(fresh, whole, out, step_out):
    wide = lanes((TILE, N))
    w = slice(HALF, HALF + TILE)
    for ch in range(2):
        m, e = fresh[0, ch, w], fresh[1, ch, w]
        out[ch, :, 0:128] = turn(jnp.where(wide < HALF, m, e))
        out[ch, :, 128:256] = turn(jnp.where(wide < HALF, e, m))
    inv = lax.rsqrt(whole[pl.ds(2 * MODES * N, N)] + PROBE_REG)
    for k in range(2 * MODES):
        step_out[pl.ds(N * k, N)] = whole[pl.ds(N * k, N)] * inv


def run_final(fresh, whole):
    return pl.pallas_call(
        final_kernel,
        out_shape=(jax.ShapeDtypeStruct((2, TILE, TILE), jnp.float32), jax.ShapeDtypeStruct((2 * MODES * N, N), jnp.float32)),
        in_specs=[VM, VM],
        out_specs=(VM, VM),
        compiler_params=pltpu.CompilerParams(vmem_limit_bytes=8 * 2**20),
        name="final",
    )(fresh, whole)


def on_device(object_field, probe, amplitudes, offsets):
    mine = jnp.swapaxes(offsets, 3, 4).reshape(BATCHES, 2, POS)
    amps = amplitudes.reshape(BATCHES, POS, N, N)
    tabs = [jnp.asarray(t) for t in tables()]
    keep = lambda a: pltpu.with_memory_space_constraint(a, pltpu.HBM)
    tiles, offs, *others = run_first(keep(object_field), keep(mine), [keep(a) for a in (*tabs, amps, probe)])
    grads = ()
    for b in range(BATCHES - 1):
        tiles, sums = run_batch(b, False, offs, tiles, others, grads)
        grads = (sums,)
    obj, step = run_final(*run_batch(BATCHES - 1, True, offs, tiles, others, grads))
    return obj, step.reshape(2, MODES, N, N)


def solution(mesh):
    placed = (
        P(None, "row", "col"),
        P(),
        P("row", "col", None, None, None, None),
        P("row", "col", None, None, None),
    )
    return jax.shard_map(
        on_device,
        mesh=mesh,
        in_specs=placed,
        out_specs=(P(None, "row", "col"), P()),
        check_vma=False,
    )
```
